32 devices in a mesh: dp: 8 (over z, x), mp: 4 (over y, core).
Axes of the slice: x: 2, y: 2, z: 4, core: 2. Of those that a mesh axis runs over, the one named last changes fastest.
Arguments:
- tokens: bfloat16 [12288, 1024], P(('dp', 'mp')), may hold values from -12 to 12
- encoder_out: bfloat16 [4096, 1024], P(('dp', 'mp')), may hold values from -6 to 6
- segments: int32 [8, 1536], P('dp', 'mp'), may hold values from 0 to 7, never falling along the last dimension, each value on 1 to 768 neighbouring positions
- encoder_segments: int32 [8, 512], P('dp', 'mp'), may hold values from 0 to 7, never falling along the last dimension, each value on 1 to 256 neighbouring positions
- buckets: int32 [1536], replicated, may hold values from 0 to 31, as said below
- rel_table: float32 [32, 16], replicated, may hold values from -3 to 3
- gain_attend: float32 [1024], replicated, may hold values from 0.5 to 1.5
- gain_cross: float32 [1024], replicated, may hold values from 0.5 to 1.5
- gain_feed: float32 [1024], replicated, may hold values from 0.5 to 1.5
- self_query: float32 [1024, 1024], P('dp', 'mp'), may hold values from -0.09375 to 0.09375
- self_key: float32 [1024, 1024], P('dp', 'mp'), may hold values from -0.09375 to 0.09375
- self_value: float32 [1024, 1024], P('dp', 'mp'), may hold values from -0.1875 to 0.1875
- self_output: float32 [1024, 1024], P('mp', 'dp'), may hold values from -0.75 to 0.75
- cross_query: float32 [1024, 1024], P('dp', 'mp'), may hold values from -0.09375 to 0.09375
- cross_key: float32 [1024, 1024], P('dp', 'mp'), may hold values from -0.09375 to 0.09375
- cross_value: float32 [1024, 1024], P('dp', 'mp'), may hold values from -0.1875 to 0.1875
- cross_output: float32 [1024, 1024], P('mp', 'dp'), may hold values from -0.75 to 0.75
- w_gate: float32 [1024, 2816], P('dp', 'mp'), may hold values from -0.1875 to 0.1875
- w_up: float32 [1024, 2816], P('dp', 'mp'), may hold values from -0.1875 to 0.1875
- w_down: float32 [2816, 1024], P('mp', 'dp'), may hold values from -0.109375 to 0.109375
- out_grad: bfloat16 [12288, 1024], P(('dp', 'mp')), may hold values from -12 to 12
Outputs:
- layer_out: bfloat16 [12288, 1024], P(('dp', 'mp'))
- tokens_grad: float32 [12288, 1024], P(('dp', 'mp'))
- encoder_grad: float32 [4096, 1024], P(('dp', 'mp'))
- rel_table_grad: float32 [32, 16], replicated
- gain_attend_grad: float32 [1024], replicated
- gain_cross_grad: float32 [1024], replicated
- gain_feed_grad: float32 [1024], replicated
- self_query_grad: float32 [1024, 1024], P('dp', 'mp')
- self_key_grad: float32 [1024, 1024], P('dp', 'mp')
- self_value_grad: float32 [1024, 1024], P('dp', 'mp')
- self_output_grad: float32 [1024, 1024], P('mp', 'dp')
- cross_query_grad: float32 [1024, 1024], P('dp', 'mp')
- cross_key_grad: float32 [1024, 1024], P('dp', 'mp')
- cross_value_grad: float32 [1024, 1024], P('dp', 'mp')
- cross_output_grad: float32 [1024, 1024], P('mp', 'dp')
- w_gate_grad: float32 [1024, 2816], P('dp', 'mp')
- w_up_grad: float32 [1024, 2816], P('dp', 'mp')
- w_down_grad: float32 [2816, 1024], P('mp', 'dp')
The draws below stay inside these ranges and needn't reach their ends.
Inputs may be any that keep to these rules, and one draw needn't show every extreme that they name: `segments`: in each sequence the numbers never fall and each of the 8 numbers occurs; the longest document has 768 tokens. `encoder_segments`: in each sequence the numbers never fall and each of the 8 numbers occurs; the longest document has 256 encoder outputs. `buckets`: never falls with the distance; distance 0 has bucket 0 and distance 1536 - 1 has bucket 32 - 1.
All inputs are finite; a program needn't handle non-finite values.
Results may differ from the reference program's by a relative error of at most 0.029.
The reference program's roundings to bfloat16 on the way count: a program that leaves them out, or rounds other values in their place, can miss the bound.
Values may be sent and summed in bfloat16 or wider, within the bound.
No kernel may reach another device: no remote copies, remote signals or barrier semaphores. Data moves between devices by JAX's collectives and lax.ppermute only.
A program may use at most 192 MiB of HBM per device.

```python
import math
import jax
import jax.numpy as jnp
import numpy as np
from jax import lax

D = 1024
H = 16
DK = 64
FF = 2816
NB = 32
ENC = 512
DOCS = 8
LEN = 1536
SEQS = 8
TOKENS = 12288
ENC_ROWS = 4096


def draw_buckets(key, part):
    cuts = jax.random.permutation(key, LEN - 1)[:NB - 1].astype(jnp.int32) + 1
    distance = jnp.arange(LEN, dtype=jnp.int32)
    return jnp.sum((cuts[None, :] <= distance[:, None]).astype(jnp.int32), axis=1).astype(jnp.int32)


def strengthened(result, own_key, source, target, shards_of, factor):
    def block_of(dim):
        return (jnp.arange(result.shape[dim]) // (result.shape[dim] // shards_of)).reshape((-1,) + (1,) * (result.ndim - 1 - dim))

    near = jax.random.permutation(own_key, shards_of)[block_of(target)]
    far = (block_of(target) + shards_of // 2) % shards_of
    return jnp.where((block_of(source) == near) | (block_of(source) == far), factor * result, result)


def level_of(key, dims, pieces, least, high):
    loudness = 1.0
    for axis_at, parts in pieces:
        steps = jax.random.uniform(jax.random.fold_in(jax.random.fold_in(key, 6), axis_at), (parts,), jnp.float32, least / len(pieces), high / len(pieces))
        loudness = loudness * jnp.repeat(jnp.exp(steps), dims[axis_at] // parts).reshape((-1,) + (1,) * (len(dims) - 1 - axis_at))
    return loudness


def profile(count, total, limit, lean):
    portions = [(1 << 20) // math.isqrt(rank ** lean) + 1 for rank in range(2, count + 1)]
    rest, counts = total - limit - (count - 1), [1] * (count - 1)
    while rest > 0:
        candidates = [i for i in range(count - 1) if counts[i] < limit]
        pool, budget = sum([portions[i] for i in candidates]), rest
        for i in candidates:
            addition = min(limit - counts[i], max(1, budget * portions[i] // pool), rest)
            counts[i] = counts[i] + addition
            rest = rest - addition
    return np.array([limit] + counts)


def uneven(own_key, number_of, total, most, slope):
    if number_of == 2:
        one = jax.random.randint(own_key, (), max(1, total - most), min(most, total - 1) + 1)
        return jnp.stack([one, total - one])
    lengths = jnp.asarray(profile(number_of, total, most, slope), jnp.int32)
    twos = (number_of - 1) // 2
    source_of, receiver = lengths[1:1 + 2 * twos:2], lengths[2:2 + 2 * twos:2]
    slack = jnp.minimum(source_of - 1, most - receiver)
    passed = jax.random.randint(jax.random.fold_in(own_key, 1), (twos,), 0, 1 << 20) % (slack + 1)
    lengths = lengths.at[1:1 + 2 * twos:2].set(source_of - passed).at[2:2 + 2 * twos:2].set(receiver + passed)
    return lengths[jax.random.permutation(jax.random.fold_in(own_key, 2), number_of)]


def scatter_about(stream_key, dims, scale, bound, cuts=(), held_as=jnp.bfloat16):
    array = jax.random.normal(stream_key, dims, jnp.float32) * scale
    if len(cuts) > 0:
        array = level_of(stream_key, dims, cuts, -0.22, 0.18) * array
    return jnp.clip(array, min=-bound, max=bound).astype(held_as)


def bell_draw_with(own_key, dims, scale, reach, cuts, heavy, kind=jnp.bfloat16):
    values = scale * jax.random.normal(own_key, dims, jnp.float32)
    if cuts:
        values = values * level_of(own_key, dims, cuts, -0.22, 0.18)
    return jnp.clip(strengthened(values, jax.random.fold_in(own_key, 3), *heavy), -reach, reach).astype(kind)


def setup_inputs(seed: int = 0) -> dict:
    streams_of = jax.random.split(jax.random.key(seed), 22)
    return {
        "tokens": bell_draw_with(streams_of[0], (TOKENS, D), 1.0, 12.0, ((0, 32),), (0, 1, 32, 2.75)),
        "encoder_out": scatter_about(streams_of[1], (ENC_ROWS, D), 1.0, 6.0, ((0, 32),)),
        "segments": jax.vmap(lambda own: jnp.searchsorted(jnp.cumsum(uneven(own, DOCS, LEN, LEN // 2, 2)), jnp.arange(LEN), side="right"))(jax.random.split(streams_of[2], SEQS)).reshape((SEQS, LEN)).astype(jnp.int32),
        "encoder_segments": jax.vmap(lambda own: jnp.searchsorted(jnp.cumsum(uneven(own, DOCS, ENC, ENC // 2, 2)), jnp.arange(ENC), side="right"))(jax.random.split(streams_of[3], SEQS)).reshape((SEQS, ENC)).astype(jnp.int32),
        "buckets": draw_buckets(jax.random.fold_in(streams_of[21], 71), 0),
        "rel_table": scatter_about(streams_of[5], (NB, H), 0.5, 3.0, (), jnp.float32),
        "gain_attend": jnp.clip(1.0 + 0.1 * jax.random.normal(streams_of[6], (D,), jnp.float32), 0.5, 1.5),
        "gain_cross": jnp.clip(1.0 + 0.1 * jax.random.normal(streams_of[7], (D,), jnp.float32), 0.5, 1.5),
        "gain_feed": jnp.clip(1.0 + 0.1 * jax.random.normal(streams_of[8], (D,), jnp.float32), 0.5, 1.5),
        "self_query": scatter_about(streams_of[9], (D, H * DK), (4 * D) ** -0.5, 0.09375, ((0, 8), (1, 4)), jnp.float32),
        "self_key": scatter_about(streams_of[10], (D, H * DK), (4 * D) ** -0.5, 0.09375, ((0, 8), (1, 4)), jnp.float32),
        "self_value": scatter_about(streams_of[11], (D, H * DK), D ** -0.5, 0.1875, ((0, 8), (1, 4)), jnp.float32),
        "self_output": scatter_about(streams_of[12], (H * DK, D), (H * DK // 16) ** -0.5, 0.75, ((0, 4), (1, 8)), jnp.float32),
        "cross_query": scatter_about(streams_of[13], (D, H * DK), (4 * D) ** -0.5, 0.09375, ((0, 8), (1, 4)), jnp.float32),
        "cross_key": scatter_about(streams_of[14], (D, H * DK), (4 * D) ** -0.5, 0.09375, ((0, 8), (1, 4)), jnp.float32),
        "cross_value": scatter_about(streams_of[15], (D, H * DK), D ** -0.5, 0.1875, ((0, 8), (1, 4)), jnp.float32),
        "cross_output": scatter_about(streams_of[16], (H * DK, D), (H * DK // 16) ** -0.5, 0.75, ((0, 4), (1, 8)), jnp.float32),
        "w_gate": scatter_about(streams_of[17], (D, FF), D ** -0.5, 0.1875, ((0, 8), (1, 4)), jnp.float32),
        "w_up": scatter_about(streams_of[18], (D, FF), D ** -0.5, 0.1875, ((0, 8), (1, 4)), jnp.float32),
        "w_down": scatter_about(streams_of[19], (FF, D), FF ** -0.5, 0.109375, ((0, 4), (1, 8)), jnp.float32),
        "out_grad": bell_draw_with(streams_of[20], (TOKENS, D), 1.0, 12.0, ((0, 32),), (0, 1, 32, 2.75)),
    }


@jax.custom_vjp
def low(v):
    return lax.optimization_barrier(v.astype(jnp.bfloat16)).astype(jnp.float32)

@jax.custom_vjp
def low_back(v):
    return v

def low_keep(v):
    return (low(v), None)

def low_pass(kept, grad):
    return (grad,)

def back_keep(v):
    return (v, None)

def back_low(kept, grad):
    return (low(grad),)
low.defvjp(low_keep, low_pass)
low_back.defvjp(back_keep, back_low)
norm_eps = 1e-06
gelu_factor = 0.7978845608028654
highest = lax.Precision.HIGHEST

def both_round(value):
    return low(low_back(value))

def product(left, right):
    return jnp.dot(left, right, precision=highest, preferred_element_type=jnp.float32)

def rms_norm(rows, gain):
    return rows * lax.rsqrt(lax.optimization_barrier(jnp.mean(rows * rows, axis=-1, keepdims=True)) + norm_eps) * gain

def gelu_tanh(value):
    return 0.5 * value * (1.0 + jnp.tanh(gelu_factor * (value + 0.044715 * value * value * value)))

def attend(queries, keys, values, table, mask_of, bias_of):
    rows = queries.shape[0]
    block = min(512, rows)
    query_heads = queries.reshape(rows, H, DK)
    key_heads = keys.reshape(keys.shape[0], H, DK)
    value_heads = values.reshape(values.shape[0], H, DK)

    def one_block(index, query_heads, key_heads, value_heads, table):
        start = (index * block).astype(jnp.int32)
        query_block = lax.dynamic_slice_in_dim(query_heads, start, block, 0)
        scores = jnp.einsum('qhd,khd->hqk', query_block, key_heads, precision=highest)
        scores = low_back(scores + bias_of(start, block, table))
        scores = jnp.where(mask_of(start, block)[None, :, :], scores, -1e+30)
        shares = low(jax.nn.softmax(scores, axis=-1))
        return jnp.einsum('hqk,khd->qhd', shares, value_heads, precision=highest)
    saved = jax.checkpoint(one_block)
    blocks = lax.map(lambda index: saved(index, query_heads, key_heads, value_heads, table), jnp.arange(rows // block, dtype=jnp.int32))
    return blocks.reshape(rows, H * DK)

def layer(token_rows, encoder_rows, params, segment_row, encoder_ids, buckets):
    table, gain_attend, gain_cross, gain_feed, self_query, self_key, self_value, self_output, cross_query, cross_key, cross_value, cross_output, w_gate, w_up, w_down = params
    query_one = low(self_query)
    key_one = low(self_key)
    value_one = low(self_value)
    output_one = low(self_output)
    query_two = low(cross_query)
    key_two = low(cross_key)
    value_two = low(cross_value)
    output_two = low(cross_output)
    gate_full = low(w_gate)
    up_full = low(w_up)
    down_full = low(w_down)
    position = jnp.arange(LEN, dtype=jnp.int32)

    def self_mask(start, block):
        row_ids = start + jnp.arange(block, dtype=jnp.int32)
        row_segments = lax.dynamic_slice_in_dim(segment_row, start, block)
        return (row_segments[:, None] == segment_row[None, :]) & (position[None, :] <= row_ids[:, None])

    def cross_mask(start, block):
        row_segments = lax.dynamic_slice_in_dim(segment_row, start, block)
        return row_segments[:, None] == encoder_ids[None, :]

    def self_bias(start, block, table):
        distance = (start + jnp.arange(block, dtype=jnp.int32))[:, None] - position[None, :]
        distance = jnp.clip(distance, 0, LEN - 1).astype(jnp.int32)
        bucket = buckets[distance]
        return jnp.transpose(table[bucket], (2, 0, 1))

    def no_bias(start, block, table):
        return jnp.zeros((), jnp.float32)
    normed = low(rms_norm(token_rows, gain_attend))
    queries = both_round(product(normed, query_one))
    keys = both_round(product(normed, key_one))
    values = both_round(product(normed, value_one))
    context = both_round(attend(queries, keys, values, table, self_mask, self_bias))
    stream_one = token_rows + low_back(product(context, output_one))
    normed = low(rms_norm(stream_one, gain_cross))
    queries = both_round(product(normed, query_two))
    keys = both_round(product(encoder_rows, key_two))
    values = both_round(product(encoder_rows, value_two))
    context = both_round(attend(queries, keys, values, table, cross_mask, no_bias))
    stream_two = stream_one + low_back(product(context, output_two))
    normed = low(rms_norm(stream_two, gain_feed))
    gate = low_back(product(normed, gate_full))
    up = low_back(product(normed, up_full))
    hidden = low(gelu_tanh(gate) * up)
    return stream_two + low_back(product(hidden, down_full))

def reference(tokens, encoder_out, segments, encoder_segments, buckets, rel_table, gain_attend, gain_cross, gain_feed, self_query, self_key, self_value, self_output, cross_query, cross_key, cross_value, cross_output, w_gate, w_up, w_down, out_grad):
    params = tuple((param.astype(jnp.float32) for param in (rel_table, gain_attend, gain_cross, gain_feed, self_query, self_key, self_value, self_output, cross_query, cross_key, cross_value, cross_output, w_gate, w_up, w_down)))
    seq_tokens = tokens.astype(jnp.float32).reshape(SEQS, LEN, D)
    seq_encoder = encoder_out.astype(jnp.float32).reshape(SEQS, ENC, D)
    seq_grads = out_grad.astype(jnp.float32).reshape(SEQS, LEN, D)

    def one_sequence(totals, inputs):
        token_rows, encoder_rows, segment_row, encoder_ids, cotangent = inputs

        def forward(token_rows, encoder_rows, params):
            return layer(token_rows, encoder_rows, params, segment_row, encoder_ids, buckets)
        output, pullback = jax.vjp(forward, token_rows, encoder_rows, params)
        token_grad, encoder_grad, param_grads = pullback(cotangent)
        totals = jax.tree.map(lambda left, right: left + right, totals, param_grads)
        return (totals, (output.astype(jnp.bfloat16), token_grad, encoder_grad))
    zeros = jax.tree.map(jnp.zeros_like, params)
    totals, (outputs, token_grads, encoder_grads) = lax.scan(one_sequence, zeros, (seq_tokens, seq_encoder, segments, encoder_segments, seq_grads))
    table_grad, attend_gain_grad, cross_gain_grad, feed_gain_grad, query_one_grad, key_one_grad, value_one_grad, output_one_grad, query_two_grad, key_two_grad, value_two_grad, output_two_grad, gate_grad, up_grad, down_grad = totals
    return (outputs.reshape(TOKENS, D), token_grads.reshape(TOKENS, D), encoder_grads.reshape(ENC_ROWS, D), table_grad, attend_gain_grad, cross_gain_grad, feed_gain_grad, query_one_grad, key_one_grad, value_one_grad, output_one_grad, query_two_grad, key_two_grad, value_two_grad, output_two_grad, gate_grad, up_grad, down_grad)
```

```python
import functools
import jax
import jax.numpy as jnp
from jax import lax
from jax.experimental import pallas as pl
from jax.experimental.pallas import tpu as pltpu
from jax.sharding import PartitionSpec as P

DK = 64
PAIR = 2 * DK
NEG = -1e30

norm_eps = 1e-06
gelu_factor = 0.7978845608028654


def product(left, right):
    return jnp.dot(left, right, preferred_element_type=jnp.float32)


def rows_product(left, right):
    return lax.dot_general(left, right, (((0,), (0,)), ((), ())), preferred_element_type=jnp.float32)


def columns_product(left, right):
    return lax.dot_general(left, right, (((1,), (1,)), ((), ())), preferred_element_type=jnp.float32)


def norm_scale(rows):
    return lax.rsqrt(jnp.mean(rows * rows, axis=-1, keepdims=True) + norm_eps)


def gelu_parts(value):
    cubic = 0.044715 * value * value * value
    tangent = jnp.tanh(gelu_factor * (value + cubic))
    result = 0.5 * value * (1.0 + tangent)
    slope = 0.5 * (1.0 + tangent) + 0.5 * value * (1.0 - tangent * tangent) * gelu_factor * (
        1.0 + 3.0 * 0.044715 * value * value
    )
    return (result, slope)


def norm_back(grads, rows, scale, gain):
    scaled = grads * gain
    row_grad = scale * scaled - rows * (scale * scale * scale) * jnp.mean(scaled * rows, axis=-1, keepdims=True)
    gain_grad = jnp.sum(grads * rows * scale, axis=0)
    return (row_grad, gain_grad)


def low(value):
    return value.astype(jnp.bfloat16)


def nt_product(left, right):
    return lax.dot_general(left, right, (((1,), (1,)), ((), ())), preferred_element_type=jnp.float32)


def nn_product(left, right):
    return jnp.dot(left, right, preferred_element_type=jnp.float32)


def own_lanes(rows, head):
    lane = lax.broadcasted_iota(jnp.int32, rows.shape, 1)
    mine = (lane < DK) if head % 2 == 0 else (lane >= DK)
    return jnp.where(mine, rows, jnp.zeros_like(rows))


def bias_kernel(series_ref, tiles_ref, *, block):
    heads = series_ref.shape[0]
    for offset in range(tiles_ref.shape[0]):
        for head in range(heads):
            low = series_ref[pl.ds(head, 1), pl.ds(offset * block, block)]
            high = series_ref[pl.ds(head, 1), pl.ds((offset + 1) * block, block)]
            base = jnp.broadcast_to(jnp.concatenate([high, low], axis=1), (block, 2 * block))
            rolled = pltpu.roll(base, 0, 1, stride=1, stride_axis=0)
            tiles_ref[offset, head] = rolled[:, :block]


def bias_tiles(series, offsets, block):
    heads = series.shape[0]
    return pl.pallas_call(
        functools.partial(bias_kernel, block=block),
        out_shape=jax.ShapeDtypeStruct((offsets, heads, block, block), jnp.float32),
        name="bias_tiles",
    )(series)


def forward_kernel(*refs, heads, block, biased, at_query, at_key, at_value):
    if biased:
        low_ref, high_ref, q_ref, first_ref, last_ref, bias_ref, ctx_ref, ot_ref, lse_ref, acc_ref, vt_ref = refs
        kv_ref = q_ref
    else:
        low_ref, high_ref, q_ref, kv_ref, first_ref, last_ref, ctx_ref, ot_ref, lse_ref, acc_ref, vt_ref = refs
    rows = q_ref.shape[0]
    width = heads * DK
    key_iota = lax.broadcasted_iota(jnp.int32, (block, block), 0)
    for tile in range(kv_ref.shape[0] // block):
        vt_ref[:, pl.ds(tile * block, block)] = jnp.transpose(
            kv_ref[pl.ds(tile * block, block), pl.ds(at_value, width)]
        )

    def one_block(index, _):
        start = pl.multiple_of(index * block, block)
        first = first_ref[:, pl.ds(start, block)]
        last = last_ref[:, pl.ds(start, block)]
        queries = [
            own_lanes(q_ref[pl.ds(start, block), pl.ds(at_query + (head // 2) * PAIR, PAIR)], head)
            for head in range(heads)
        ]
        acc_ref[...] = jnp.zeros_like(acc_ref)

        def one_tile(tile, carry):
            at = pl.multiple_of(tile * block, block)
            valid = (key_iota >= first - at) & (key_iota < last - at)
            results = []
            for head in range(heads):
                top, total = carry[head]
                keys = kv_ref[pl.ds(at, block), pl.ds(at_key + (head // 2) * PAIR, PAIR)]
                scores = nt_product(keys, queries[head])
                if biased:
                    scores = scores + bias_ref[index - tile, head]
                scores = jnp.where(valid, scores, NEG)
                new_top = jnp.maximum(top, jnp.max(scores, axis=0, keepdims=True))
                raised = jnp.exp(scores - new_top)
                shrink = jnp.exp(top - new_top)
                total = shrink * total + jnp.sum(raised, axis=0, keepdims=True)
                mine = pl.ds(head * DK, DK)
                acc_ref[mine, :] = acc_ref[mine, :] * shrink + nn_product(
                    vt_ref[mine, pl.ds(at, block)], raised.astype(jnp.bfloat16)
                )
                results.append((new_top, total))
            return tuple(results)

        empty = tuple(
            (jnp.full((1, block), NEG, jnp.float32), jnp.zeros((1, block), jnp.float32)) for _ in range(heads)
        )
        stats = lax.fori_loop(low_ref[index], high_ref[index], one_tile, empty)
        for head in range(heads):
            top, total = stats[head]
            mine = pl.ds(head * DK, DK)
            acc_ref[mine, :] = acc_ref[mine, :] / total
            lse_ref[pl.ds(head, 1), pl.ds(start, block)] = top + jnp.log(total)
        ot_ref[:, pl.ds(start, block)] = acc_ref[...]
        ctx_ref[pl.ds(start, block), :] = jnp.transpose(acc_ref[...]).astype(jnp.bfloat16)
        return 0

    lax.fori_loop(0, rows // block, one_block, 0)


SMEM_SPEC = pl.BlockSpec(memory_space=pltpu.SMEM)
VMEM_SPEC = pl.BlockSpec(memory_space=pltpu.VMEM)


def attend_forward(ranges, queries, keys_values, bias, heads, block):
    low_block, high_block, first, last = ranges
    rows = queries.shape[0]
    width = heads * DK
    biased = bias is not None
    if biased:
        operands = [low_block, high_block, queries, first, last, bias]
        at_key = width
        key_rows = rows
    else:
        operands = [low_block, high_block, queries, keys_values, first, last]
        at_key = 0
        key_rows = keys_values.shape[0]
    return pl.pallas_call(
        functools.partial(
            forward_kernel,
            heads=heads,
            block=block,
            biased=biased,
            at_query=0,
            at_key=at_key,
            at_value=at_key + width,
        ),
        out_shape=(
            jax.ShapeDtypeStruct((rows, width), jnp.bfloat16),
            jax.ShapeDtypeStruct((width, rows), jnp.float32),
            jax.ShapeDtypeStruct((heads, rows), jnp.float32),
        ),
        in_specs=[SMEM_SPEC, SMEM_SPEC] + [VMEM_SPEC] * (len(operands) - 2),
        out_specs=(VMEM_SPEC, VMEM_SPEC, VMEM_SPEC),
        scratch_shapes=[pltpu.VMEM((width, block), jnp.float32), pltpu.VMEM((width, key_rows), jnp.bfloat16)],
        compiler_params=pltpu.CompilerParams(vmem_limit_bytes=40 << 20),
        cost_estimate=pl.CostEstimate(flops=2 << 30, bytes_accessed=8 << 20, transcendentals=4 << 20),
        name="attend_forward",
    )(*operands)


def backward_kernel(*refs, heads, block, biased, at_key, at_value):
    if biased:
        low_ref, high_ref, q_ref, g_ref, ot_ref, lse_ref, first_ref, last_ref, bias_ref = refs[:9]
        dq_ref, series_ref, dqt_ref, kt_ref, dka_ref, dva_ref, diag_ref = refs[9:]
        kv_ref, dkv_ref = q_ref, dq_ref
    else:
        low_ref, high_ref, q_ref, kv_ref, g_ref, ot_ref, lse_ref, first_ref, last_ref = refs[:9]
        dq_ref, dkv_ref, dqt_ref, kt_ref, dka_ref, dva_ref = refs[9:]
    rows = q_ref.shape[0]
    width = heads * DK
    key_iota = lax.broadcasted_iota(jnp.int32, (block, block), 0)
    for tile in range(kv_ref.shape[0] // block):
        kt_ref[:, pl.ds(tile * block, block)] = jnp.transpose(
            kv_ref[pl.ds(tile * block, block), pl.ds(at_key, width)]
        )
    dka_ref[...] = jnp.zeros_like(dka_ref)
    dva_ref[...] = jnp.zeros_like(dva_ref)
    if biased:
        diag_ref[...] = jnp.zeros_like(diag_ref)

    def one_block(index, _):
        start = pl.multiple_of(index * block, block)
        first = first_ref[:, pl.ds(start, block)]
        last = last_ref[:, pl.ds(start, block)]
        pairs = [pl.ds(pair * PAIR, PAIR) for pair in range(heads // 2)]
        queries = [own_lanes(q_ref[pl.ds(start, block), pairs[head // 2]], head) for head in range(heads)]
        grads = [own_lanes(g_ref[pl.ds(start, block), pairs[head // 2]], head) for head in range(heads)]
        shared = jnp.transpose(g_ref[pl.ds(start, block), :].astype(jnp.float32)) * ot_ref[:, pl.ds(start, block)]
        deltas = [jnp.sum(shared[head * DK : (head + 1) * DK], axis=0, keepdims=True) for head in range(heads)]
        totals = [lse_ref[pl.ds(head, 1), pl.ds(start, block)] for head in range(heads)]
        dqt_ref[...] = jnp.zeros_like(dqt_ref)

        def one_tile(tile, carry):
            at = pl.multiple_of(tile * block, block)
            valid = (key_iota >= first - at) & (key_iota < last - at)
            for pair in range(heads // 2):
                lanes = pl.ds(pair * PAIR, PAIR)
                keys = kv_ref[pl.ds(at, block), pl.ds(at_key + pair * PAIR, PAIR)]
                values = kv_ref[pl.ds(at, block), pl.ds(at_value + pair * PAIR, PAIR)]
                dk = dka_ref[pl.ds(at, block), lanes]
                dv = dva_ref[pl.ds(at, block), lanes]
                for head in (2 * pair, 2 * pair + 1):
                    scores = nt_product(keys, queries[head])
                    if biased:
                        scores = scores + bias_ref[index - tile, head]
                    shares = jnp.exp(jnp.where(valid, scores - totals[head], NEG))
                    share_grad = nt_product(values, grads[head])
                    score_grad = (shares * (share_grad - deltas[head])).astype(jnp.bfloat16)
                    dv = dv + nn_product(shares.astype(jnp.bfloat16), grads[head])
                    dk = dk + nn_product(score_grad, queries[head])
                    mine = pl.ds(head * DK, DK)
                    dqt_ref[mine, :] += nn_product(kt_ref[mine, pl.ds(at, block)], score_grad)
                    if biased:
                        diag_ref[index - tile, head] += score_grad.astype(jnp.float32)
                dka_ref[pl.ds(at, block), lanes] = dk
                dva_ref[pl.ds(at, block), lanes] = dv
            return carry

        lax.fori_loop(low_ref[index], high_ref[index], one_tile, 0)
        dq_ref[pl.ds(start, block), pl.ds(0, width)] = jnp.transpose(dqt_ref[...]).astype(jnp.bfloat16)
        return 0

    lax.fori_loop(0, rows // block, one_block, 0)
    dkv_ref[:, pl.ds(at_key, width)] = dka_ref[...].astype(jnp.bfloat16)
    dkv_ref[:, pl.ds(at_value, width)] = dva_ref[...].astype(jnp.bfloat16)
    if biased:
        for offset in range(diag_ref.shape[0]):
            for head in range(heads):
                slab = jnp.zeros((8, 2 * block), jnp.float32)
                for group in range(block // 8):
                    piece = diag_ref[offset, head, pl.ds(8 * group, 8), :]
                    wide = jnp.concatenate([piece, jnp.zeros_like(piece)], axis=1)
                    slab = slab + (pltpu.roll(wide, 2 * block - 8 * group, 1) if group else wide)
                line = slab[0:1]
                for row in range(1, 8):
                    line = line + pltpu.roll(slab[row : row + 1], 2 * block - row, 1)
                series_ref[offset, pl.ds(head, 1), :] = line


def attend_backward(ranges, queries, keys_values, grads, context_t, totals, bias, heads, block):
    low_block, high_block, first, last = ranges
    rows = queries.shape[0]
    width = heads * DK
    biased = bias is not None
    if biased:
        operands = [low_block, high_block, queries, grads, context_t, totals, first, last, bias]
        key_rows = rows
        at_key = width
        shapes = [
            jax.ShapeDtypeStruct((rows, 3 * width), jnp.bfloat16),
            jax.ShapeDtypeStruct((bias.shape[0], heads, 2 * block), jnp.float32),
        ]
    else:
        operands = [low_block, high_block, queries, keys_values, grads, context_t, totals, first, last]
        key_rows = keys_values.shape[0]
        at_key = 0
        shapes = [
            jax.ShapeDtypeStruct((rows, width), jnp.bfloat16),
            jax.ShapeDtypeStruct((key_rows, 2 * width), jnp.bfloat16),
        ]
    scratch = [
        pltpu.VMEM((width, block), jnp.float32),
        pltpu.VMEM((width, key_rows), jnp.bfloat16),
        pltpu.VMEM((key_rows, width), jnp.float32),
        pltpu.VMEM((key_rows, width), jnp.float32),
    ]
    if biased:
        scratch.append(pltpu.VMEM(bias.shape, jnp.float32))
    return pl.pallas_call(
        functools.partial(
            backward_kernel,
            heads=heads,
            block=block,
            biased=biased,
            at_key=at_key,
            at_value=at_key + width,
        ),
        out_shape=tuple(shapes),
        in_specs=[SMEM_SPEC, SMEM_SPEC] + [VMEM_SPEC] * (len(operands) - 2),
        out_specs=tuple(VMEM_SPEC for _ in shapes),
        scratch_shapes=scratch,
        compiler_params=pltpu.CompilerParams(vmem_limit_bytes=48 << 20),
        cost_estimate=pl.CostEstimate(flops=6 << 30, bytes_accessed=12 << 20, transcendentals=4 << 20),
        name="attend_backward",
    )(*operands)


PEERS = 4


def to_core(rows):
    return lax.ppermute(rows, "mp", [(i, i ^ 1) for i in range(PEERS)])


def across(rows):
    return lax.ppermute(rows, "mp", [(i, i ^ 2) for i in range(PEERS)])


def gather_halves(rows):
    far_own = across(rows)
    near = jnp.concatenate([rows, to_core(rows)], axis=0)
    far = jnp.concatenate([far_own, to_core(far_own)], axis=0)
    return near, far


def swap_order(rows, me):
    size = rows.shape[0] // PEERS
    return jnp.concatenate(
        [lax.dynamic_slice_in_dim(rows, (me ^ peer) * size, size, 0) for peer in range(PEERS)], axis=0
    )


def send_far(far):
    size = far.shape[0] // 2
    arrived = to_core(low(far[size:]))
    return across(low(far[:size] + arrived.astype(jnp.float32)))


def sum_near(near, far_sum):
    size = near.shape[0] // 2
    arrived = to_core(low(near[size:]))
    return near[:size] + arrived.astype(jnp.float32) + far_sum.astype(jnp.float32)


def gather_weights(parts):
    return lax.all_gather(low(jnp.concatenate(parts, axis=1)), "dp", axis=0, tiled=True)


def reduce_weights(parts):
    whole = jnp.concatenate([low(part) for part in parts], axis=1)
    return lax.psum_scatter(whole, "dp", scatter_dimension=0, tiled=True).astype(jnp.float32)


def sum_everywhere(value, sizes):
    for axis in ("mp", "dp"):
        step = 1
        while step < sizes[axis]:
            value = value + lax.ppermute(value, axis, [(i, i ^ step) for i in range(sizes[axis])])
            step *= 2
    return value


def columns_of(array, widths):
    pieces = []
    at = 0
    for width in widths:
        pieces.append(array[:, at : at + width])
        at += width
    return pieces


def key_ranges(ids, key_ids, documents):
    numbers = jnp.arange(documents, dtype=jnp.int32)
    below = jnp.sum((key_ids[None, :] < numbers[:, None]).astype(jnp.int32), axis=1)
    upto = jnp.sum((key_ids[None, :] <= numbers[:, None]).astype(jnp.int32), axis=1)
    mine = (ids[None, :] == numbers[:, None]).astype(jnp.int32)
    return (jnp.sum(mine * below[:, None], axis=0), jnp.sum(mine * upto[:, None], axis=0))


def block_ranges(first, last, block):
    return (first[::block] // block, (last[block - 1 :: block] + block - 1) // block)


DOCUMENTS = 8
LONGEST = 768


def per_device(
    tokens,
    encoder_out,
    segments,
    encoder_segments,
    buckets,
    rel_table,
    gain_attend,
    gain_cross,
    gain_feed,
    self_query,
    self_key,
    self_value,
    self_output,
    cross_query,
    cross_key,
    cross_value,
    cross_output,
    w_gate,
    w_up,
    w_down,
    out_grad,
    *,
    sizes,
):
    wide = self_query.shape[1]
    hidden_wide = w_gate.shape[1]
    heads = wide // DK
    block = 256
    me = lax.axis_index("mp")
    self_all = gather_weights([self_query, self_key, self_value, self_output.T])
    cross_all = gather_weights([cross_query, cross_key, cross_value, cross_output.T])
    feed_all = gather_weights([w_gate, w_up, w_down.T])
    qkv_one, output_one = columns_of(self_all, [3 * wide, wide])
    query_two, key_value_two, output_two = columns_of(cross_all, [wide, 2 * wide, wide])
    gate_full, up_full, down_full = columns_of(feed_all, [hidden_wide] * 3)

    buckets_count = rel_table.shape[0]
    own_tokens = segments.shape[1]
    ids = lax.all_gather(jnp.concatenate([segments, encoder_segments], axis=1), "mp", axis=0, tiled=True)
    decoder_ids = ids[:, :own_tokens].reshape(-1)
    encoder_ids = ids[:, own_tokens:].reshape(-1)
    length = decoder_ids.shape[0]
    self_first, unused = key_ranges(decoder_ids, decoder_ids, DOCUMENTS)
    self_last = jnp.arange(length, dtype=jnp.int32) + 1
    cross_first, cross_last = key_ranges(decoder_ids, encoder_ids, DOCUMENTS)
    self_low, self_high = block_ranges(self_first, self_last, block)
    cross_low, cross_high = block_ranges(cross_first, cross_last, block)
    self_ranges = (self_low, self_high, self_first[None], self_last[None])
    cross_ranges = (cross_low, cross_high, cross_first[None], cross_last[None])

    offsets = min((LONGEST + block - 2) // block + 1, length // block)
    reach = offsets * block
    table_local = lax.dynamic_slice_in_dim(rel_table, me * heads, heads, 1)
    onehot = (buckets[None, :reach] == jnp.arange(buckets_count, dtype=jnp.int32)[:, None]).astype(jnp.float32)
    series = lax.dot_general(table_local, onehot, (((0,), (0,)), ((), ())), precision=lax.Precision.HIGHEST)
    bias = bias_tiles(jnp.pad(series, ((0, 0), (block, 0))), offsets, block)

    stream_zero = tokens.astype(jnp.float32)
    scale_zero = norm_scale(stream_zero)
    normed_one = low(stream_zero * scale_zero * gain_attend)
    normed_one = swap_order(jnp.concatenate(gather_halves(normed_one), axis=0), me)
    encoder_all = swap_order(jnp.concatenate(gather_halves(encoder_out), axis=0), me)
    top_near, top_far = gather_halves(out_grad)
    half = 2 * tokens.shape[0]

    qkv = low(product(normed_one, qkv_one))
    context_one, context_one_t, totals_one = attend_forward(self_ranges, qkv, None, bias, heads, block)
    context_one = swap_order(context_one, me)
    far_sum = send_far(columns_product(context_one[half:], output_one))
    stream_one = stream_zero + sum_near(columns_product(context_one[:half], output_one), far_sum)

    scale_one = norm_scale(stream_one)
    normed_two_near, normed_two_far = gather_halves(low(stream_one * scale_one * gain_cross))
    keys_values_two = low(product(encoder_all, key_value_two))
    queries_two = swap_order(
        jnp.concatenate([low(product(normed_two_near, query_two)), low(product(normed_two_far, query_two))], axis=0), me
    )
    context_two, context_two_t, totals_two = attend_forward(
        cross_ranges, queries_two, keys_values_two, None, heads, block
    )
    context_two = swap_order(context_two, me)
    far_sum = send_far(columns_product(context_two[half:], output_two))
    stream_two = stream_one + sum_near(columns_product(context_two[:half], output_two), far_sum)

    scale_two = norm_scale(stream_two)
    normed_three_near, normed_three_far = gather_halves(low(stream_two * scale_two * gain_feed))

    def feed(normed, top):
        gate = product(normed, gate_full)
        up = product(normed, up_full)
        gelu_value, gelu_slope = gelu_parts(gate)
        hidden = low(gelu_value * up)
        hidden_grad = product(top, down_full)
        gate_grad = low(hidden_grad * up * gelu_slope)
        up_grad = low(hidden_grad * gelu_value)
        return hidden, gate_grad, up_grad

    def feed_back(gate_grad, up_grad):
        return columns_product(gate_grad, gate_full) + columns_product(up_grad, up_full)

    hidden_near, gate_grad_near, up_grad_near = feed(normed_three_near, top_near)
    hidden_far, gate_grad_far, up_grad_far = feed(normed_three_far, top_far)
    far_sum = send_far(feed_back(gate_grad_far, up_grad_far))
    normed_grad = sum_near(feed_back(gate_grad_near, up_grad_near), far_sum)
    down_grad = rows_product(top_near, hidden_near) + rows_product(top_far, hidden_far)
    gate_weight_grad = rows_product(normed_three_near, gate_grad_near) + rows_product(normed_three_far, gate_grad_far)
    up_weight_grad = rows_product(normed_three_near, up_grad_near) + rows_product(normed_three_far, up_grad_far)
    feed_sums = reduce_weights([gate_weight_grad, up_weight_grad, down_grad])
    far_sum = send_far(columns_product(hidden_far, down_full))
    layer_out = low(stream_two + sum_near(columns_product(hidden_near, down_full), far_sum))

    top_grad = out_grad.astype(jnp.float32)
    part_grad, feed_gain_grad = norm_back(normed_grad, stream_two, scale_two, gain_feed)
    stream_grad = top_grad + part_grad

    grad_near, grad_far = gather_halves(low(stream_grad))
    context_grad = swap_order(
        jnp.concatenate([low(product(grad_near, output_two)), low(product(grad_far, output_two))], axis=0), me
    )
    query_grad, key_value_grad = attend_backward(
        cross_ranges, queries_two, keys_values_two, context_grad, context_two_t, totals_two, None, heads, block
    )
    query_grad = swap_order(query_grad, me)
    query_grad_near, query_grad_far = query_grad[:half], query_grad[half:]
    far_sum = send_far(columns_product(query_grad_far, query_two))
    normed_grad = sum_near(columns_product(query_grad_near, query_two), far_sum)
    encoder_part = swap_order(columns_product(key_value_grad, key_value_two), me)
    encoder_half = encoder_part.shape[0] // 2
    encoder_grad = sum_near(encoder_part[:encoder_half], send_far(encoder_part[encoder_half:]))
    output_two_grad = rows_product(grad_near, context_two[:half]) + rows_product(grad_far, context_two[half:])
    query_two_grad = rows_product(normed_two_near, query_grad_near) + rows_product(normed_two_far, query_grad_far)
    key_value_two_grad = rows_product(encoder_all, key_value_grad)
    cross_sums = reduce_weights([query_two_grad, key_value_two_grad, output_two_grad])
    part_grad, cross_gain_grad = norm_back(normed_grad, stream_one, scale_one, gain_cross)
    stream_grad = stream_grad + part_grad

    grad_near, grad_far = gather_halves(low(stream_grad))
    context_grad = swap_order(
        jnp.concatenate([low(product(grad_near, output_one)), low(product(grad_far, output_one))], axis=0), me
    )
    qkv_grad, diagonals = attend_backward(
        self_ranges, qkv, None, context_grad, context_one_t, totals_one, bias, heads, block
    )
    qkv_grad_swapped = swap_order(qkv_grad, me)
    far_sum = send_far(columns_product(qkv_grad_swapped[half:], qkv_one))
    normed_grad = sum_near(columns_product(qkv_grad_swapped[:half], qkv_one), far_sum)
    output_one_grad = rows_product(grad_near, context_one[:half]) + rows_product(grad_far, context_one[half:])
    qkv_one_grad = rows_product(normed_one, qkv_grad)
    self_sums = reduce_weights([qkv_one_grad, output_one_grad])
    part_grad, attend_gain_grad = norm_back(normed_grad, stream_zero, scale_zero, gain_attend)
    tokens_grad = stream_grad + part_grad

    ahead = jnp.moveaxis(diagonals[:, :, :block], 0, 1).reshape(heads, reach)
    behind = jnp.moveaxis(diagonals[1:, :, block:], 0, 1).reshape(heads, reach - block)
    series_grad = ahead + jnp.pad(behind, ((0, 0), (0, block)))
    table_grad = lax.dot_general(onehot, series_grad, (((1,), (1,)), ((), ())), precision=lax.Precision.HIGHEST)
    table_full = lax.dynamic_update_slice(jnp.zeros(rel_table.shape, jnp.float32), table_grad, (0, me * heads))
    features = gain_attend.shape[0]
    small = jnp.concatenate([attend_gain_grad, cross_gain_grad, feed_gain_grad, table_full.reshape(-1)])
    small = sum_everywhere(small.reshape(-1, 128), sizes).reshape(-1)
    attend_gain_sum, cross_gain_sum, feed_gain_sum = (
        small[:features],
        small[features : 2 * features],
        small[2 * features : 3 * features],
    )
    table_sum = small[3 * features :].reshape(rel_table.shape)
    query_one_sum, key_one_sum, value_one_sum, output_one_sum = columns_of(self_sums, [wide] * 4)
    query_two_sum, key_two_sum, value_two_sum, output_two_sum = columns_of(cross_sums, [wide] * 4)
    gate_sum, up_sum, down_sum = columns_of(feed_sums, [hidden_wide] * 3)
    return (
        layer_out,
        tokens_grad,
        encoder_grad,
        table_sum,
        attend_gain_sum,
        cross_gain_sum,
        feed_gain_sum,
        query_one_sum,
        key_one_sum,
        value_one_sum,
        output_one_sum.T,
        query_two_sum,
        key_two_sum,
        value_two_sum,
        output_two_sum.T,
        gate_sum,
        up_sum,
        down_sum.T,
    )


def solution(mesh):
    in_specs = (
        P(("dp", "mp"), None),
        P(("dp", "mp"), None),
        P("dp", "mp"),
        P("dp", "mp"),
        P(),
        P(),
        P(),
        P(),
        P(),
        P("dp", "mp"),
        P("dp", "mp"),
        P("dp", "mp"),
        P("mp", "dp"),
        P("dp", "mp"),
        P("dp", "mp"),
        P("dp", "mp"),
        P("mp", "dp"),
        P("dp", "mp"),
        P("dp", "mp"),
        P("mp", "dp"),
        P(("dp", "mp"), None),
    )
    out_specs = (
        P(("dp", "mp"), None),
        P(("dp", "mp"), None),
        P(("dp", "mp"), None),
        P(),
        P(),
        P(),
        P(),
        P("dp", "mp"),
        P("dp", "mp"),
        P("dp", "mp"),
        P("mp", "dp"),
        P("dp", "mp"),
        P("dp", "mp"),
        P("dp", "mp"),
        P("mp", "dp"),
        P("dp", "mp"),
        P("dp", "mp"),
        P("mp", "dp"),
    )
    return jax.shard_map(
        functools.partial(per_device, sizes=dict(mesh.shape)), mesh=mesh, in_specs=in_specs, out_specs=out_specs, check_vma=False
    )
```

```python
import functools
import jax
import jax.numpy as jnp
from jax import lax
from jax.experimental import pallas as pl
from jax.experimental.pallas import tpu as pltpu
from jax.sharding import PartitionSpec as P

DK = 64
PAIR = 2 * DK
NEG = -1e30
PEERS = 4

norm_eps = 1e-06
gelu_factor = 0.7978845608028654


def product(left, right):
    return jnp.dot(left, right, preferred_element_type=jnp.float32)


def rows_product(left, right):
    return lax.dot_general(left, right, (((0,), (0,)), ((), ())), preferred_element_type=jnp.float32)


def columns_product(left, right):
    return lax.dot_general(left, right, (((1,), (1,)), ((), ())), preferred_element_type=jnp.float32)


def norm_scale(rows):
    return lax.rsqrt(jnp.mean(rows * rows, axis=-1, keepdims=True) + norm_eps)


def gelu_parts(value):
    cubic = 0.044715 * value * value * value
    tangent = jnp.tanh(gelu_factor * (value + cubic))
    result = 0.5 * value * (1.0 + tangent)
    slope = 0.5 * (1.0 + tangent) + 0.5 * value * (1.0 - tangent * tangent) * gelu_factor * (
        1.0 + 3.0 * 0.044715 * value * value
    )
    return (result, slope)


def norm_back(grads, rows, scale, gain):
    scaled = grads * gain
    row_grad = scale * scaled - rows * (scale * scale * scale) * jnp.mean(scaled * rows, axis=-1, keepdims=True)
    gain_grad = jnp.sum(grads * rows * scale, axis=0)
    return (row_grad, gain_grad)


def low(value):
    return value.astype(jnp.bfloat16)


def nt_product(left, right):
    return lax.dot_general(left, right, (((1,), (1,)), ((), ())), preferred_element_type=jnp.float32)


def nn_product(left, right):
    return jnp.dot(left, right, preferred_element_type=jnp.float32)


def own_lanes(rows, head):
    lane = lax.broadcasted_iota(jnp.int32, rows.shape, 1)
    mine = (lane < DK) if head % 2 == 0 else (lane >= DK)
    return jnp.where(mine, rows, jnp.zeros_like(rows))


def bias_kernel(series_ref, tiles_ref, *, block):
    heads = series_ref.shape[0]
    for offset in range(tiles_ref.shape[0]):
        for head in range(heads):
            low = series_ref[pl.ds(head, 1), pl.ds(offset * block, block)]
            high = series_ref[pl.ds(head, 1), pl.ds((offset + 1) * block, block)]
            base = jnp.broadcast_to(jnp.concatenate([high, low], axis=1), (block, 2 * block))
            rolled = pltpu.roll(base, 0, 1, stride=1, stride_axis=0)
            tiles_ref[offset, head] = rolled[:, :block]


def bias_tiles(series, offsets, block):
    heads = series.shape[0]
    return pl.pallas_call(
        functools.partial(bias_kernel, block=block),
        out_shape=jax.ShapeDtypeStruct((offsets, heads, block, block), jnp.float32),
        name="bias_tiles",
    )(series)


def load_order(me, pieces, target_ref):
    size = target_ref.shape[0] // PEERS
    for order in range(PEERS):
        at = pl.multiple_of((me ^ order) * size, size)
        target_ref[pl.ds(at, size), :] = pieces[order // 2][pl.ds((order % 2) * size, size), :]


def store_order(me, source_ref, pieces):
    size = source_ref.shape[0] // PEERS
    for order in range(PEERS):
        at = pl.multiple_of((me ^ order) * size, size)
        pieces[order // 2][pl.ds((order % 2) * size, size), :] = source_ref[pl.ds(at, size), :].astype(jnp.bfloat16)


def forward_kernel(*refs, heads, block, tall, biased, at_key, at_value):
    low_ref, high_ref, me_ref, near_ref, far_ref, first_ref, last_ref = refs[:7]
    if biased:
        bias_ref, ctx_near_ref, ctx_far_ref, ot_ref, lse_ref, acc_ref, vt_ref, q_ref, ctx_ref = refs[7:]
        kv_ref = q_ref
    else:
        kv_ref, ctx_near_ref, ctx_far_ref, ot_ref, lse_ref, acc_ref, vt_ref, q_ref, ctx_ref = refs[7:]
    load_order(me_ref[0], (near_ref, far_ref), q_ref)
    rows = q_ref.shape[0]
    width = heads * DK
    key_iota = lax.broadcasted_iota(jnp.int32, (tall, block), 0)
    for tile in range(kv_ref.shape[0] // tall):
        vt_ref[:, pl.ds(tile * tall, tall)] = jnp.transpose(kv_ref[pl.ds(tile * tall, tall), pl.ds(at_value, width)])

    def one_block(index, _):
        start = pl.multiple_of(index * block, block)
        first = first_ref[:, pl.ds(start, block)]
        last = last_ref[:, pl.ds(start, block)]
        queries = [
            own_lanes(q_ref[pl.ds(start, block), pl.ds((head // 2) * PAIR, PAIR)], head) for head in range(heads)
        ]
        acc_ref[...] = jnp.zeros_like(acc_ref)

        def one_tile(tile, carry):
            at = pl.multiple_of(tile * tall, tall)
            valid = (key_iota >= first - at) & (key_iota < last - at)
            results = []
            for head in range(heads):
                top, total = carry[head]
                keys = kv_ref[pl.ds(at, tall), pl.ds(at_key + (head // 2) * PAIR, PAIR)]
                scores = nt_product(keys, queries[head])
                if biased:
                    scores = scores + bias_ref[index - tile, head]
                scores = jnp.where(valid, scores, NEG)
                new_top = jnp.maximum(top, jnp.max(scores, axis=0, keepdims=True))
                raised = jnp.exp(scores - new_top)
                shrink = jnp.exp(top - new_top)
                total = shrink * total + jnp.sum(raised, axis=0, keepdims=True)
                mine = pl.ds(head * DK, DK)
                acc_ref[mine, :] = acc_ref[mine, :] * shrink + nn_product(
                    vt_ref[mine, pl.ds(at, tall)], raised.astype(jnp.bfloat16)
                )
                results.append((new_top, total))
            return tuple(results)

        empty = tuple(
            (jnp.full((1, block), NEG, jnp.float32), jnp.zeros((1, block), jnp.float32)) for _ in range(heads)
        )
        stats = lax.fori_loop(low_ref[index], high_ref[index], one_tile, empty)
        for head in range(heads):
            top, total = stats[head]
            mine = pl.ds(head * DK, DK)
            acc_ref[mine, :] = acc_ref[mine, :] / total
            lse_ref[pl.ds(head, 1), pl.ds(start, block)] = top + jnp.log(total)
        ot_ref[:, pl.ds(start, block)] = acc_ref[...]
        ctx_ref[pl.ds(start, block), :] = jnp.transpose(acc_ref[...])
        return 0

    lax.fori_loop(0, rows // block, one_block, 0)
    store_order(me_ref[0], ctx_ref, (ctx_near_ref, ctx_far_ref))


LIGHT = pl.CostEstimate(flops=1 << 20, bytes_accessed=1 << 10, transcendentals=0)
SMEM_SPEC = pl.BlockSpec(memory_space=pltpu.SMEM)
VMEM_SPEC = pl.BlockSpec(memory_space=pltpu.VMEM)


def attend_forward(ranges, me, queries, keys_values, bias, heads, block, tall):
    low_block, high_block, first, last = ranges
    near, far = queries
    half = near.shape[0]
    rows = 2 * half
    width = heads * DK
    biased = bias is not None
    at_key = width if biased else 0
    key_rows = rows if biased else keys_values.shape[0]
    operands = [low_block, high_block, me[None], near, far, first, last, bias if biased else keys_values]
    return pl.pallas_call(
        functools.partial(
            forward_kernel,
            heads=heads,
            block=block,
            tall=tall,
            biased=biased,
            at_key=at_key,
            at_value=at_key + width,
        ),
        out_shape=(
            jax.ShapeDtypeStruct((half, width), jnp.bfloat16),
            jax.ShapeDtypeStruct((half, width), jnp.bfloat16),
            jax.ShapeDtypeStruct((width, rows), jnp.float32),
            jax.ShapeDtypeStruct((heads, rows), jnp.float32),
        ),
        in_specs=[SMEM_SPEC] * 3 + [VMEM_SPEC] * (len(operands) - 3),
        out_specs=(VMEM_SPEC,) * 4,
        scratch_shapes=[
            pltpu.VMEM((width, block), jnp.float32),
            pltpu.VMEM((width, key_rows), jnp.bfloat16),
            pltpu.VMEM((rows, near.shape[1]), jnp.bfloat16),
            pltpu.VMEM((rows, width), jnp.float32),
        ],
        compiler_params=pltpu.CompilerParams(vmem_limit_bytes=40 << 20),
        cost_estimate=LIGHT,
        name="attend_forward",
    )(*operands)


def backward_kernel(*refs, heads, block, tall, biased, at_key, at_value):
    (
        low_ref, high_ref, me_ref, near_ref, far_ref, g_near_ref, g_far_ref, ot_ref, lse_ref, first_ref, last_ref, extra_ref
    ) = refs[:12]
    if biased:
        dq_near_ref, dq_far_ref, series_ref, dqt_ref, kt_ref, dka_ref, dva_ref, q_ref, g_ref, dq_ref, diag_ref = refs[12:]
        bias_ref = extra_ref
        kv_ref, dkv_ref = q_ref, dq_ref
    else:
        dq_near_ref, dq_far_ref, dkv_ref, dqt_ref, kt_ref, dka_ref, dva_ref, q_ref, g_ref, dq_ref = refs[12:]
        kv_ref = extra_ref
    load_order(me_ref[0], (near_ref, far_ref), q_ref)
    load_order(me_ref[0], (g_near_ref, g_far_ref), g_ref)
    rows = q_ref.shape[0]
    width = heads * DK
    key_iota = lax.broadcasted_iota(jnp.int32, (tall, block), 0)
    for tile in range(kv_ref.shape[0] // tall):
        kt_ref[:, pl.ds(tile * tall, tall)] = jnp.transpose(kv_ref[pl.ds(tile * tall, tall), pl.ds(at_key, width)])
    dka_ref[...] = jnp.zeros_like(dka_ref)
    dva_ref[...] = jnp.zeros_like(dva_ref)
    if biased:
        diag_ref[...] = jnp.zeros_like(diag_ref)

    def one_block(index, _):
        start = pl.multiple_of(index * block, block)
        first = first_ref[:, pl.ds(start, block)]
        last = last_ref[:, pl.ds(start, block)]
        pairs = [pl.ds(pair * PAIR, PAIR) for pair in range(heads // 2)]
        queries = [own_lanes(q_ref[pl.ds(start, block), pairs[head // 2]], head) for head in range(heads)]
        grads = [own_lanes(g_ref[pl.ds(start, block), pairs[head // 2]], head) for head in range(heads)]
        shared = jnp.transpose(g_ref[pl.ds(start, block), :].astype(jnp.float32)) * ot_ref[:, pl.ds(start, block)]
        deltas = [jnp.sum(shared[head * DK : (head + 1) * DK], axis=0, keepdims=True) for head in range(heads)]
        totals = [lse_ref[pl.ds(head, 1), pl.ds(start, block)] for head in range(heads)]
        dqt_ref[...] = jnp.zeros_like(dqt_ref)

        def one_tile(tile, carry):
            at = pl.multiple_of(tile * tall, tall)
            valid = (key_iota >= first - at) & (key_iota < last - at)
            for pair in range(heads // 2):
                lanes = pl.ds(pair * PAIR, PAIR)
                keys = kv_ref[pl.ds(at, tall), pl.ds(at_key + pair * PAIR, PAIR)]
                values = kv_ref[pl.ds(at, tall), pl.ds(at_value + pair * PAIR, PAIR)]
                dk = dka_ref[pl.ds(at, tall), lanes]
                dv = dva_ref[pl.ds(at, tall), lanes]
                for head in (2 * pair, 2 * pair + 1):
                    scores = nt_product(keys, queries[head])
                    if biased:
                        scores = scores + bias_ref[index - tile, head]
                    shares = jnp.exp(jnp.where(valid, scores - totals[head], NEG))
                    share_grad = nt_product(values, grads[head])
                    score_grad = (shares * (share_grad - deltas[head])).astype(jnp.bfloat16)
                    dv = dv + nn_product(shares.astype(jnp.bfloat16), grads[head])
                    dk = dk + nn_product(score_grad, queries[head])
                    mine = pl.ds(head * DK, DK)
                    dqt_ref[mine, :] += nn_product(kt_ref[mine, pl.ds(at, tall)], score_grad)
                    if biased:
                        diag_ref[index - tile, head] += score_grad.astype(jnp.float32)
                dka_ref[pl.ds(at, tall), lanes] = dk
                dva_ref[pl.ds(at, tall), lanes] = dv
            return carry

        lax.fori_loop(low_ref[index], high_ref[index], one_tile, 0)
        dq_ref[pl.ds(start, block), pl.ds(0, width)] = jnp.transpose(dqt_ref[...]).astype(jnp.bfloat16)
        return 0

    lax.fori_loop(0, rows // block, one_block, 0)
    dkv_ref[:, pl.ds(at_key, width)] = dka_ref[...].astype(jnp.bfloat16)
    dkv_ref[:, pl.ds(at_value, width)] = dva_ref[...].astype(jnp.bfloat16)
    store_order(me_ref[0], dq_ref, (dq_near_ref, dq_far_ref))
    if biased:
        for offset in range(diag_ref.shape[0]):
            for head in range(heads):
                slab = jnp.zeros((8, 2 * block), jnp.float32)
                for group in range(block // 8):
                    piece = diag_ref[offset, head, pl.ds(8 * group, 8), :]
                    wide = jnp.concatenate([piece, jnp.zeros_like(piece)], axis=1)
                    slab = slab + (pltpu.roll(wide, 2 * block - 8 * group, 1) if group else wide)
                line = slab[0:1]
                for row in range(1, 8):
                    line = line + pltpu.roll(slab[row : row + 1], 2 * block - row, 1)
                series_ref[offset, pl.ds(head, 1), :] = line


def attend_backward(ranges, me, queries, keys_values, grads, context_t, totals, bias, heads, block, tall):
    low_block, high_block, first, last = ranges
    half, depth = queries[0].shape
    rows = 2 * half
    width = heads * DK
    biased = bias is not None
    at_key = width if biased else 0
    key_rows = rows if biased else keys_values.shape[0]
    operands = [low_block, high_block, me[None], *queries, *grads, context_t, totals, first, last]
    operands.append(bias if biased else keys_values)
    shapes = [jax.ShapeDtypeStruct((half, depth), jnp.bfloat16)] * 2
    scratch = [
        pltpu.VMEM((width, block), jnp.float32),
        pltpu.VMEM((width, key_rows), jnp.bfloat16),
        pltpu.VMEM((key_rows, width), jnp.float32),
        pltpu.VMEM((key_rows, width), jnp.float32),
        pltpu.VMEM((rows, depth), jnp.bfloat16),
        pltpu.VMEM((rows, width), jnp.bfloat16),
        pltpu.VMEM((rows, depth), jnp.bfloat16),
    ]
    if biased:
        shapes.append(jax.ShapeDtypeStruct((bias.shape[0], heads, 2 * block), jnp.float32))
        scratch.append(pltpu.VMEM(bias.shape, jnp.float32))
    else:
        shapes.append(jax.ShapeDtypeStruct((key_rows, 2 * width), jnp.bfloat16))
    return pl.pallas_call(
        functools.partial(
            backward_kernel,
            heads=heads,
            block=block,
            tall=tall,
            biased=biased,
            at_key=at_key,
            at_value=at_key + width,
        ),
        out_shape=tuple(shapes),
        in_specs=[SMEM_SPEC] * 3 + [VMEM_SPEC] * (len(operands) - 3),
        out_specs=(VMEM_SPEC,) * len(shapes),
        scratch_shapes=scratch,
        compiler_params=pltpu.CompilerParams(vmem_limit_bytes=50 << 20),
        cost_estimate=LIGHT,
        name="attend_backward",
    )(*operands)


def place_kernel(me_ref, *refs, first):
    out_ref = refs[-1]
    pieces = refs[:-1]
    size = out_ref.shape[0] // len(pieces)
    for order, piece in enumerate(pieces):
        at = pl.multiple_of((me_ref[0] ^ order) * size, size)
        out_ref[pl.ds(at, size), :] = piece[pl.ds(first, size), :]


def place(pieces, me, first=0, size=None):
    size = size or pieces[0].shape[0]
    width = pieces[0].shape[1]
    count = len(pieces)
    return pl.pallas_call(
        functools.partial(place_kernel, first=first),
        out_shape=jax.ShapeDtypeStruct((count * size, width), pieces[0].dtype),
        in_specs=[SMEM_SPEC] + [VMEM_SPEC] * count,
        out_specs=VMEM_SPEC,
        compiler_params=pltpu.CompilerParams(vmem_limit_bytes=24 << 20),
        cost_estimate=LIGHT,
        name="place",
    )(me[None], *pieces)


def swap_kernel(me_ref, rows_ref, out_ref, *, count):
    size = rows_ref.shape[0] // count
    for order in range(count):
        at = pl.multiple_of((me_ref[0] ^ order) * size, size)
        out_ref[pl.ds(order * size, size), :] = rows_ref[pl.ds(at, size), :]


def swap_order(rows, me, count=4):
    return pl.pallas_call(
        functools.partial(swap_kernel, count=count),
        out_shape=jax.ShapeDtypeStruct(rows.shape, rows.dtype),
        in_specs=[SMEM_SPEC, VMEM_SPEC],
        out_specs=VMEM_SPEC,
        compiler_params=pltpu.CompilerParams(vmem_limit_bytes=24 << 20),
        cost_estimate=LIGHT,
        name="swap_order",
    )(me[None], rows)


def weights_kernel(me_ref, *refs, groups, chunk, sending):
    out_ref = refs[-1]
    rows = out_ref.shape[-2]
    features = refs[0].shape[1]

    def one_chunk(index, _):
        lanes = pl.ds(pl.multiple_of(index * chunk, chunk), chunk)
        at = 0
        column = 0
        for terms in groups:
            total = None
            for _ in range(terms):
                left_ref, right_ref = refs[at], refs[at + 1]
                at += 2
                term = lax.dot_general(
                    left_ref[:, lanes],
                    right_ref[...],
                    (((0,), (0,)), ((), ())),
                    preferred_element_type=jnp.float32,
                )
                total = term if total is None else total + term
            width = total.shape[1]
            total = total.astype(jnp.bfloat16)
            for part in range(chunk // rows):
                block = index * (chunk // rows) + part
                if sending:
                    block = block ^ me_ref[0]
                    place_at = (block & 1, block >> 1)
                else:
                    place_at = (block >> 1, block & 1)
                out_ref[place_at[0], place_at[1], :, pl.ds(column, width)] = total[part * rows : (part + 1) * rows]
            column += width
        return 0

    lax.fori_loop(0, features // chunk, one_chunk, 0)


def weight_grads(groups, me, parts, sending):
    operands = [array for group in groups for pair in group for array in pair]
    features = operands[0].shape[1]
    width = sum(group[0][1].shape[1] for group in groups)
    rows = features // parts
    shape = (2, parts // 2, rows, width) if sending else (parts // 2, 2, rows, width)
    return pl.pallas_call(
        functools.partial(
            weights_kernel, groups=tuple(len(group) for group in groups), chunk=max(256, rows), sending=sending
        ),
        out_shape=jax.ShapeDtypeStruct(shape, jnp.bfloat16),
        in_specs=[SMEM_SPEC] + [VMEM_SPEC] * len(operands),
        out_specs=VMEM_SPEC,
        compiler_params=pltpu.CompilerParams(vmem_limit_bytes=48 << 20),
        cost_estimate=LIGHT,
        name="weight_grads",
    )(me[None], *operands)


def exchange(rows, axis, size, bits):
    return lax.ppermute(rows, axis, [(i, i ^ bits) for i in range(size)])


def to_core(rows):
    return exchange(rows, "mp", PEERS, 1)


def across(rows):
    return exchange(rows, "mp", PEERS, 2)


def after(value, *others):
    return lax.optimization_barrier((value, *others))[0]


def gather_four(rows):
    far = across(rows)
    return rows, to_core(rows), far, to_core(far)


def gather_halves(rows):
    one, two, three, four = gather_four(rows)
    return jnp.concatenate([one, two], axis=0), jnp.concatenate([three, four], axis=0)


def send_far(far):
    size = far.shape[0] // 2
    arrived = to_core(low(far[size:]))
    return across(low(far[:size] + arrived.astype(jnp.float32)))


def sum_core(near):
    size = near.shape[0] // 2
    arrived = to_core(low(near[size:]))
    return near[:size] + arrived.astype(jnp.float32)


def gather_weights(weights):
    return lax.all_gather(low(jnp.concatenate(weights, axis=1)), "dp", axis=0, tiled=True)


def reduce_weights(grads):
    return lax.psum_scatter(grads, "dp", scatter_dimension=0, tiled=True).astype(jnp.float32)


def reduce_directly(grads, size):
    arrived = lax.all_to_all(grads, "dp", split_axis=0, concat_axis=0, tiled=True)
    return jnp.sum(arrived.reshape(size, -1, grads.shape[1]).astype(jnp.float32), axis=0)


def sum_everywhere(value, sizes):
    for axis in ("mp", "dp"):
        step = 1
        while step < sizes[axis]:
            value = value + exchange(value, axis, sizes[axis], step)
            step *= 2
    return value


def columns_of(array, widths):
    pieces = []
    at = 0
    for width in widths:
        pieces.append(array[:, at : at + width])
        at += width
    return pieces


def key_ranges(ids, key_ids, documents):
    numbers = jnp.arange(documents, dtype=jnp.int32)
    below = jnp.sum((key_ids[None, :] < numbers[:, None]).astype(jnp.int32), axis=1)
    upto = jnp.sum((key_ids[None, :] <= numbers[:, None]).astype(jnp.int32), axis=1)
    mine = (ids[None, :] == numbers[:, None]).astype(jnp.int32)
    return (jnp.sum(mine * below[:, None], axis=0), jnp.sum(mine * upto[:, None], axis=0))


def block_ranges(first, last, block, tall):
    return (first[::block] // tall, (last[block - 1 :: block] + tall - 1) // tall)


DOCUMENTS = 8
LONGEST = 768


def per_device(
    tokens,
    encoder_out,
    segments,
    encoder_segments,
    buckets,
    rel_table,
    gain_attend,
    gain_cross,
    gain_feed,
    self_query,
    self_key,
    self_value,
    self_output,
    cross_query,
    cross_key,
    cross_value,
    cross_output,
    w_gate,
    w_up,
    w_down,
    out_grad,
    *,
    sizes,
):
    parts = sizes["dp"]
    wide = self_query.shape[1]
    hidden_wide = w_gate.shape[1]
    heads = wide // DK
    block = 256
    own_rows = tokens.shape[0]
    half = 2 * own_rows
    me = lax.axis_index("mp")
    dp_index = lax.axis_index("dp")

    self_all = gather_weights([self_query, self_key, self_value, self_output.T])
    cross_all = gather_weights([cross_query, cross_key, cross_value, cross_output.T])
    feed_all = gather_weights([w_gate, w_up, w_down.T])
    qkv_one, output_one = columns_of(self_all, [3 * wide, wide])
    query_two, key_value_two, output_two = columns_of(cross_all, [wide, 2 * wide, wide])
    gate_full, up_full, down_full = columns_of(feed_all, [hidden_wide] * 3)

    buckets_count = rel_table.shape[0]
    stream_zero = tokens.astype(jnp.float32)
    scale_zero = norm_scale(stream_zero)
    normed_zero = low(stream_zero * scale_zero * gain_attend)
    features = tokens.shape[1]
    encoder_rows = encoder_out.shape[0]
    ids = jnp.concatenate([segments, encoder_segments], axis=1)
    ids = jnp.pad(ids, ((0, 15), (0, features - ids.shape[1]))).astype(jnp.bfloat16)
    row_pieces = gather_four(jnp.concatenate([normed_zero, encoder_out, ids], axis=0))
    normed_one_near, normed_one_far = [
        jnp.concatenate([piece[:own_rows] for piece in pieces], axis=0) for pieces in (row_pieces[:2], row_pieces[2:])
    ]
    encoder_all = place(row_pieces, me, own_rows, encoder_rows)
    top_near, top_far = gather_halves(after(out_grad, *row_pieces))

    id_rows = jnp.concatenate([piece[own_rows + encoder_rows :][:1] for piece in row_pieces], axis=0).astype(jnp.int32)
    near_ids = id_rows[:, :own_rows].reshape(-1)
    ids = jnp.concatenate([lax.dynamic_slice_in_dim(id_rows, me ^ peer, 1, 0) for peer in range(PEERS)], axis=0)
    decoder_ids = ids[:, :own_rows].reshape(-1)
    encoder_ids = ids[:, own_rows : own_rows + encoder_rows].reshape(-1)
    length = decoder_ids.shape[0]
    self_first, unused = key_ranges(decoder_ids, decoder_ids, DOCUMENTS)
    self_last = jnp.arange(length, dtype=jnp.int32) + 1
    self_low, self_high = block_ranges(self_first, self_last, block, block)
    self_ranges = (self_low, self_high, self_first[None], self_last[None])
    cross_first, cross_last = key_ranges(near_ids, encoder_ids, DOCUMENTS)
    cross_low, cross_high = block_ranges(cross_first, cross_last, own_rows, block)
    cross_ranges = (cross_low, cross_high, cross_first[None], cross_last[None])

    offsets = min((LONGEST + block - 2) // block + 1, length // block)
    reach = offsets * block
    table_local = lax.dynamic_slice_in_dim(rel_table, me * heads, heads, 1)
    onehot = (buckets[None, :reach] == jnp.arange(buckets_count, dtype=jnp.int32)[:, None]).astype(jnp.float32)
    series = lax.dot_general(table_local, onehot, (((0,), (0,)), ((), ())), precision=lax.Precision.HIGHEST)
    bias = bias_tiles(jnp.pad(series, ((0, 0), (block, 0))), offsets, block)

    qkv_near = low(product(normed_one_near, qkv_one))
    qkv_far = after(low(product(normed_one_far, qkv_one)), top_near, top_far)
    qkv = (qkv_near, qkv_far)
    context_one_near, context_one_far, context_one_t, totals_one = attend_forward(
        self_ranges, me, qkv, None, bias, heads, block, block
    )
    far_sum = send_far(columns_product(context_one_far, output_one))
    stream_one = sum_core(columns_product(context_one_near, output_one)) + stream_zero
    keys_values_two = low(product(encoder_all, key_value_two))
    stream_one = stream_one + far_sum.astype(jnp.float32)

    scale_one = norm_scale(stream_one)
    normed_two = low(stream_one * scale_one * gain_cross)
    normed_two_near = jnp.concatenate([normed_two, to_core(normed_two)], axis=0)
    query_two_near = low(product(normed_two_near, query_two))
    normed_two_far = after(across(normed_two), query_two_near, keys_values_two)
    normed_two_far = jnp.concatenate([normed_two_far, to_core(normed_two_far)], axis=0)
    query_two_far = low(product(normed_two_far, query_two))
    queries_two = (query_two_near, query_two_far)
    still = jnp.zeros_like(me)
    context_two_near, context_two_far, context_two_t, totals_two = attend_forward(
        cross_ranges, still, queries_two, keys_values_two, None, heads, own_rows, block
    )
    far_sum = send_far(columns_product(context_two_far, output_two))
    stream_two = sum_core(columns_product(context_two_near, output_two)) + stream_one
    stream_two = stream_two + far_sum.astype(jnp.float32)

    scale_two = norm_scale(stream_two)
    normed_three = low(stream_two * scale_two * gain_feed)
    normed_three_near = jnp.concatenate([normed_three, to_core(normed_three)], axis=0)

    def feed(normed, top):
        gate = product(normed, gate_full)
        up = product(normed, up_full)
        gelu_value, gelu_slope = gelu_parts(gate)
        hidden = low(gelu_value * up)
        hidden_grad = product(top, down_full)
        gate_grad = low(hidden_grad * up * gelu_slope)
        up_grad = low(hidden_grad * gelu_value)
        return hidden, gate_grad, up_grad

    def feed_back(gate_grad, up_grad):
        return columns_product(gate_grad, gate_full) + columns_product(up_grad, up_full)

    hidden_near, gate_grad_near, up_grad_near = feed(normed_three_near, top_near)
    normed_three_far = after(across(normed_three), hidden_near, gate_grad_near, up_grad_near)
    normed_three_far = jnp.concatenate([normed_three_far, to_core(normed_three_far)], axis=0)
    hidden_far, gate_grad_far, up_grad_far = feed(normed_three_far, top_far)
    far_sum = send_far(feed_back(gate_grad_far, up_grad_far))
    normed_grad = sum_core(feed_back(gate_grad_near, up_grad_near))
    feed_grads = weight_grads(
        [
            [(normed_three_near, gate_grad_near), (normed_three_far, gate_grad_far)],
            [(normed_three_near, up_grad_near), (normed_three_far, up_grad_far)],
            [(top_near, hidden_near), (top_far, hidden_far)],
        ],
        dp_index,
        parts,
        False,
    ).reshape(feed_all.shape)
    far_sum = after(far_sum, feed_grads, normed_grad)
    normed_grad = normed_grad + far_sum.astype(jnp.float32)
    feed_sums = reduce_weights(feed_grads)

    top_grad = out_grad.astype(jnp.float32)
    part_grad, feed_gain_grad = norm_back(normed_grad, stream_two, scale_two, gain_feed)
    stream_grad = top_grad + part_grad

    grad_two = low(stream_grad)
    grad_two_near = jnp.concatenate([grad_two, to_core(grad_two)], axis=0)
    context_grad_near = low(product(grad_two_near, output_two))
    layer_near = sum_core(columns_product(hidden_near, down_full))
    layer_far = columns_product(after(hidden_far, normed_grad), down_full)
    grad_two_far = after(across(grad_two), context_grad_near, layer_near, layer_far)
    grad_two_far = jnp.concatenate([grad_two_far, to_core(grad_two_far)], axis=0)
    context_grad = (context_grad_near, low(product(grad_two_far, output_two)))
    query_grad_near, query_grad_far, key_value_grad = attend_backward(
        cross_ranges,
        still,
        queries_two,
        keys_values_two,
        context_grad,
        context_two_t,
        totals_two,
        None,
        heads,
        own_rows,
        block,
    )
    far_sum = send_far(columns_product(query_grad_far, query_two))
    normed_grad = sum_core(columns_product(query_grad_near, query_two))
    cross_grads = weight_grads(
        [
            [(normed_two_near, query_grad_near), (normed_two_far, query_grad_far)],
            [(encoder_all, key_value_grad)],
            [(grad_two_near, context_two_near), (grad_two_far, context_two_far)],
        ],
        dp_index,
        parts,
        False,
    ).reshape(cross_all.shape)
    encoder_part = columns_product(swap_order(key_value_grad, me), key_value_two)
    far_sum = after(far_sum, cross_grads, normed_grad, encoder_part)
    cross_sums = reduce_weights(cross_grads)
    normed_grad = normed_grad + far_sum.astype(jnp.float32)
    part_grad, cross_gain_grad = norm_back(normed_grad, stream_one, scale_one, gain_cross)
    stream_grad = stream_grad + part_grad

    grad_one = low(stream_grad)
    grad_near = jnp.concatenate([grad_one, to_core(grad_one)], axis=0)
    context_grad_near = low(product(grad_near, output_one))
    grad_far = after(across(grad_one), context_grad_near)
    grad_far = jnp.concatenate([grad_far, to_core(grad_far)], axis=0)
    context_grad = (context_grad_near, low(product(grad_far, output_one)))
    layer_far = send_far(after(layer_far, grad_far))
    encoder_half = encoder_part.shape[0] // 2
    encoder_far = send_far(after(encoder_part[encoder_half:], grad_far))
    qkv_grad_near, qkv_grad_far, diagonals = attend_backward(
        self_ranges, me, qkv, None, context_grad, context_one_t, totals_one, bias, heads, block, block
    )
    qkv_grad_far, unused, unused, unused = lax.optimization_barrier((qkv_grad_far, layer_far, encoder_far, feed_sums))
    layer_out = low(stream_two + layer_near + layer_far.astype(jnp.float32))
    encoder_grad = sum_core(encoder_part[:encoder_half]) + encoder_far.astype(jnp.float32)
    far_sum = send_far(columns_product(qkv_grad_far, qkv_one))
    self_grads = weight_grads(
        [
            [(normed_one_near, qkv_grad_near), (normed_one_far, qkv_grad_far)],
            [(grad_near, context_one_near), (grad_far, context_one_far)],
        ],
        dp_index,
        parts,
        False,
    ).reshape(self_all.shape)
    self_sums = reduce_directly(self_grads, parts)
    normed_grad = sum_core(columns_product(qkv_grad_near, qkv_one))
    normed_grad = normed_grad + after(far_sum, self_grads, normed_grad).astype(jnp.float32)
    part_grad, attend_gain_grad = norm_back(normed_grad, stream_zero, scale_zero, gain_attend)
    tokens_grad = stream_grad + part_grad

    ahead = jnp.moveaxis(diagonals[:, :, :block], 0, 1).reshape(heads, reach)
    behind = jnp.moveaxis(diagonals[1:, :, block:], 0, 1).reshape(heads, reach - block)
    series_grad = ahead + jnp.pad(behind, ((0, 0), (0, block)))
    table_grad = lax.dot_general(onehot, series_grad, (((1,), (1,)), ((), ())), precision=lax.Precision.HIGHEST)
    table_full = lax.dynamic_update_slice(jnp.zeros(rel_table.shape, jnp.float32), table_grad, (0, me * heads))
    small = jnp.concatenate([attend_gain_grad, cross_gain_grad, feed_gain_grad, table_full.reshape(-1)])
    small = sum_everywhere(small.reshape(-1, 128), sizes).reshape(-1)
    attend_gain_sum, cross_gain_sum, feed_gain_sum = (
        small[:features],
        small[features : 2 * features],
        small[2 * features : 3 * features],
    )
    table_sum = small[3 * features :].reshape(rel_table.shape)
    query_one_sum, key_one_sum, value_one_sum, output_one_sum = columns_of(self_sums, [wide] * 4)
    query_two_sum, key_two_sum, value_two_sum, output_two_sum = columns_of(cross_sums, [wide] * 4)
    gate_sum, up_sum, down_sum = columns_of(feed_sums, [hidden_wide] * 3)
    return (
        layer_out,
        tokens_grad,
        encoder_grad,
        table_sum,
        attend_gain_sum,
        cross_gain_sum,
        feed_gain_sum,
        query_one_sum,
        key_one_sum,
        value_one_sum,
        output_one_sum.T,
        query_two_sum,
        key_two_sum,
        value_two_sum,
        output_two_sum.T,
        gate_sum,
        up_sum,
        down_sum.T,
    )


def solution(mesh):
    in_specs = (
        P(("dp", "mp"), None),
        P(("dp", "mp"), None),
        P("dp", "mp"),
        P("dp", "mp"),
        P(),
        P(),
        P(),
        P(),
        P(),
        P("dp", "mp"),
        P("dp", "mp"),
        P("dp", "mp"),
        P("mp", "dp"),
        P("dp", "mp"),
        P("dp", "mp"),
        P("dp", "mp"),
        P("mp", "dp"),
        P("dp", "mp"),
        P("dp", "mp"),
        P("mp", "dp"),
        P(("dp", "mp"), None),
    )
    out_specs = (
        P(("dp", "mp"), None),
        P(("dp", "mp"), None),
        P(("dp", "mp"), None),
        P(),
        P(),
        P(),
        P(),
        P("dp", "mp"),
        P("dp", "mp"),
        P("dp", "mp"),
        P("mp", "dp"),
        P("dp", "mp"),
        P("dp", "mp"),
        P("dp", "mp"),
        P("mp", "dp"),
        P("dp", "mp"),
        P("dp", "mp"),
        P("mp", "dp"),
    )
    return jax.shard_map(
        functools.partial(per_device, sizes=dict(mesh.shape)), mesh=mesh, in_specs=in_specs, out_specs=out_specs, check_vma=False
    )
```

```python
import functools
import jax
import jax.numpy as jnp
from jax import lax
from jax.experimental import pallas as pl
from jax.experimental.pallas import tpu as pltpu
from jax.sharding import PartitionSpec as P

DK = 64
PAIR = 2 * DK
NEG = -1e30
PEERS = 4

norm_eps = 1e-06
gelu_factor = 0.7978845608028654


def product(left, right):
    return jnp.dot(left, right, preferred_element_type=jnp.float32)


def rows_product(left, right):
    return lax.dot_general(left, right, (((0,), (0,)), ((), ())), preferred_element_type=jnp.float32)


def columns_product(left, right):
    return lax.dot_general(left, right, (((1,), (1,)), ((), ())), preferred_element_type=jnp.float32)


def norm_scale(rows):
    return lax.rsqrt(jnp.mean(rows * rows, axis=-1, keepdims=True) + norm_eps)


def gelu_parts(value):
    cubic = 0.044715 * value * value * value
    tangent = jnp.tanh(gelu_factor * (value + cubic))
    result = 0.5 * value * (1.0 + tangent)
    slope = 0.5 * (1.0 + tangent) + 0.5 * value * (1.0 - tangent * tangent) * gelu_factor * (
        1.0 + 3.0 * 0.044715 * value * value
    )
    return (result, slope)


def norm_back(grads, rows, scale, gain):
    scaled = grads * gain
    row_grad = scale * scaled - rows * (scale * scale * scale) * jnp.mean(scaled * rows, axis=-1, keepdims=True)
    gain_grad = jnp.sum(grads * rows * scale, axis=0)
    return (row_grad, gain_grad)


def low(value):
    return value.astype(jnp.bfloat16)


def nt_product(left, right):
    return lax.dot_general(left, right, (((1,), (1,)), ((), ())), preferred_element_type=jnp.float32)


def nn_product(left, right):
    return jnp.dot(left, right, preferred_element_type=jnp.float32)


def own_lanes(rows, head):
    lane = lax.broadcasted_iota(jnp.int32, rows.shape, 1)
    mine = (lane < DK) if head % 2 == 0 else (lane >= DK)
    return jnp.where(mine, rows, jnp.zeros_like(rows))


def bias_kernel(series_ref, tiles_ref, *, block):
    heads = series_ref.shape[0]
    for offset in range(tiles_ref.shape[0]):
        for head in range(heads):
            low = series_ref[pl.ds(head, 1), pl.ds(offset * block, block)]
            high = series_ref[pl.ds(head, 1), pl.ds((offset + 1) * block, block)]
            base = jnp.broadcast_to(jnp.concatenate([high, low], axis=1), (block, 2 * block))
            rolled = pltpu.roll(base, 0, 1, stride=1, stride_axis=0)
            tiles_ref[offset, head] = rolled[:, :block]


def bias_tiles(series, offsets, block):
    heads = series.shape[0]
    return pl.pallas_call(
        functools.partial(bias_kernel, block=block),
        out_shape=jax.ShapeDtypeStruct((offsets, heads, block, block), jnp.float32),
        compiler_params=pltpu.CompilerParams(vmem_limit_bytes=16 << 20),
        cost_estimate=lasting(4),
        name="bias_tiles",
    )(series)


def load_order(me, pieces, target_ref):
    size = pieces[0].shape[0]
    for order, piece in enumerate(pieces):
        at = pl.multiple_of((me ^ order) * size, size)
        target_ref[pl.ds(at, size), :] = piece[...]


def store_order(me, source_ref, pieces):
    size = pieces[0].shape[0]
    for order, piece in enumerate(pieces):
        at = pl.multiple_of((me ^ order) * size, size)
        piece[...] = source_ref[pl.ds(at, size), :].astype(jnp.bfloat16)


def forward_kernel(*refs, heads, block, tall, biased, at_key, at_value, pieces):
    low_ref, high_ref, me_ref, first_ref, last_ref, extra_ref = refs[:6]
    piece_refs = refs[6 : 6 + pieces]
    ctx_refs = refs[6 + pieces : 6 + 2 * pieces]
    ot_ref, lse_ref, acc_ref, vt_ref, q_ref, ctx_ref = refs[6 + 2 * pieces :]
    if biased:
        bias_ref, kv_ref = extra_ref, q_ref
    else:
        kv_ref = extra_ref
    load_order(me_ref[0], piece_refs, q_ref)
    rows = q_ref.shape[0]
    width = heads * DK
    key_iota = lax.broadcasted_iota(jnp.int32, (tall, block), 0)
    for tile in range(kv_ref.shape[0] // tall):
        vt_ref[:, pl.ds(tile * tall, tall)] = jnp.transpose(kv_ref[pl.ds(tile * tall, tall), pl.ds(at_value, width)])

    def one_block(index, _):
        start = pl.multiple_of(index * block, block)
        first = first_ref[:, pl.ds(start, block)]
        last = last_ref[:, pl.ds(start, block)]
        queries = [
            own_lanes(q_ref[pl.ds(start, block), pl.ds((head // 2) * PAIR, PAIR)], head) for head in range(heads)
        ]
        acc_ref[...] = jnp.zeros_like(acc_ref)

        def one_tile(tile, carry):
            at = pl.multiple_of(tile * tall, tall)
            valid = (key_iota >= first - at) & (key_iota < last - at)
            results = []
            for head in range(heads):
                top, total = carry[head]
                keys = kv_ref[pl.ds(at, tall), pl.ds(at_key + (head // 2) * PAIR, PAIR)]
                scores = nt_product(keys, queries[head])
                if biased:
                    scores = scores + bias_ref[index - tile, head]
                scores = jnp.where(valid, scores, NEG)
                new_top = jnp.maximum(top, jnp.max(scores, axis=0, keepdims=True))
                raised = jnp.exp(scores - new_top)
                shrink = jnp.exp(top - new_top)
                total = shrink * total + jnp.sum(raised, axis=0, keepdims=True)
                mine = pl.ds(head * DK, DK)
                acc_ref[mine, :] = acc_ref[mine, :] * shrink + nn_product(
                    vt_ref[mine, pl.ds(at, tall)], raised.astype(jnp.bfloat16)
                )
                results.append((new_top, total))
            return tuple(results)

        empty = tuple(
            (jnp.full((1, block), NEG, jnp.float32), jnp.zeros((1, block), jnp.float32)) for _ in range(heads)
        )
        stats = lax.fori_loop(low_ref[index], high_ref[index], one_tile, empty)
        for head in range(heads):
            top, total = stats[head]
            mine = pl.ds(head * DK, DK)
            acc_ref[mine, :] = acc_ref[mine, :] / total
            lse_ref[pl.ds(head, 1), pl.ds(start, block)] = top + jnp.log(total)
        ot_ref[:, pl.ds(start, block)] = acc_ref[...]
        ctx_ref[pl.ds(start, block), :] = jnp.transpose(acc_ref[...])
        return 0

    lax.fori_loop(0, rows // block, one_block, 0)
    store_order(me_ref[0], ctx_ref, ctx_refs)


def lasting(micros):
    return pl.CostEstimate(flops=int(micros * 1.1e9), bytes_accessed=1 << 10, transcendentals=0)


SMEM_SPEC = pl.BlockSpec(memory_space=pltpu.SMEM)
VMEM_SPEC = pl.BlockSpec(memory_space=pltpu.VMEM)


def attend_forward(ranges, me, queries, keys_values, bias, heads, block, tall):
    low_block, high_block, first, last = ranges
    pieces = len(queries)
    size, depth = queries[0].shape
    rows = pieces * size
    width = heads * DK
    biased = bias is not None
    at_key = width if biased else 0
    key_rows = rows if biased else keys_values.shape[0]
    operands = [low_block, high_block, me[None], first, last, bias if biased else keys_values, *queries]
    return pl.pallas_call(
        functools.partial(
            forward_kernel,
            heads=heads,
            block=block,
            tall=tall,
            biased=biased,
            at_key=at_key,
            at_value=at_key + width,
            pieces=pieces,
        ),
        out_shape=(
            *([jax.ShapeDtypeStruct((size, width), jnp.bfloat16)] * pieces),
            jax.ShapeDtypeStruct((width, rows), jnp.float32),
            jax.ShapeDtypeStruct((heads, rows), jnp.float32),
        ),
        in_specs=[SMEM_SPEC] * 3 + [VMEM_SPEC] * (len(operands) - 3),
        out_specs=(VMEM_SPEC,) * (pieces + 2),
        scratch_shapes=[
            pltpu.VMEM((width, block), jnp.float32),
            pltpu.VMEM((width, key_rows), jnp.bfloat16),
            pltpu.VMEM((rows, depth), jnp.bfloat16),
            pltpu.VMEM((rows, width), jnp.float32),
        ],
        compiler_params=pltpu.CompilerParams(vmem_limit_bytes=24 << 20),
        cost_estimate=lasting(1),
        name="attend_forward",
    )(*operands)


def backward_kernel(*refs, heads, block, tall, biased, at_key, at_value, pieces):
    low_ref, high_ref, me_ref, ot_ref, lse_ref, first_ref, last_ref, extra_ref = refs[:8]
    piece_refs = refs[8 : 8 + pieces]
    g_refs = refs[8 + pieces : 8 + 2 * pieces]
    out_refs = refs[8 + 2 * pieces : 8 + 3 * pieces]
    refs = refs[8 + 3 * pieces :]
    if biased:
        series_ref, dqt_ref, kt_ref, dka_ref, dva_ref, q_ref, g_ref, dq_ref, diag_ref = refs
        bias_ref = extra_ref
        kv_ref, dkv_ref = q_ref, dq_ref
    else:
        dkv_ref, dqt_ref, kt_ref, dka_ref, dva_ref, q_ref, g_ref, dq_ref = refs
        kv_ref = extra_ref
    load_order(me_ref[0], piece_refs, q_ref)
    load_order(me_ref[0], g_refs, g_ref)
    rows = q_ref.shape[0]
    width = heads * DK
    key_iota = lax.broadcasted_iota(jnp.int32, (tall, block), 0)
    for tile in range(kv_ref.shape[0] // tall):
        kt_ref[:, pl.ds(tile * tall, tall)] = jnp.transpose(kv_ref[pl.ds(tile * tall, tall), pl.ds(at_key, width)])
    dka_ref[...] = jnp.zeros_like(dka_ref)
    dva_ref[...] = jnp.zeros_like(dva_ref)
    if biased:
        diag_ref[...] = jnp.zeros_like(diag_ref)

    def one_block(index, _):
        start = pl.multiple_of(index * block, block)
        first = first_ref[:, pl.ds(start, block)]
        last = last_ref[:, pl.ds(start, block)]
        pairs = [pl.ds(pair * PAIR, PAIR) for pair in range(heads // 2)]
        queries = [own_lanes(q_ref[pl.ds(start, block), pairs[head // 2]], head) for head in range(heads)]
        grads = [own_lanes(g_ref[pl.ds(start, block), pairs[head // 2]], head) for head in range(heads)]
        shared = jnp.transpose(g_ref[pl.ds(start, block), :].astype(jnp.float32)) * ot_ref[:, pl.ds(start, block)]
        deltas = [jnp.sum(shared[head * DK : (head + 1) * DK], axis=0, keepdims=True) for head in range(heads)]
        totals = [lse_ref[pl.ds(head, 1), pl.ds(start, block)] for head in range(heads)]
        dqt_ref[...] = jnp.zeros_like(dqt_ref)

        def one_tile(tile, carry):
            at = pl.multiple_of(tile * tall, tall)
            valid = (key_iota >= first - at) & (key_iota < last - at)
            for pair in range(heads // 2):
                lanes = pl.ds(pair * PAIR, PAIR)
                keys = kv_ref[pl.ds(at, tall), pl.ds(at_key + pair * PAIR, PAIR)]
                values = kv_ref[pl.ds(at, tall), pl.ds(at_value + pair * PAIR, PAIR)]
                dk = dka_ref[pl.ds(at, tall), lanes]
                dv = dva_ref[pl.ds(at, tall), lanes]
                for head in (2 * pair, 2 * pair + 1):
                    scores = nt_product(keys, queries[head])
                    if biased:
                        scores = scores + bias_ref[index - tile, head]
                    shares = jnp.exp(jnp.where(valid, scores - totals[head], NEG))
                    share_grad = nt_product(values, grads[head])
                    score_grad = (shares * (share_grad - deltas[head])).astype(jnp.bfloat16)
                    dv = dv + nn_product(shares.astype(jnp.bfloat16), grads[head])
                    dk = dk + nn_product(score_grad, queries[head])
                    mine = pl.ds(head * DK, DK)
                    dqt_ref[mine, :] += nn_product(kt_ref[mine, pl.ds(at, tall)], score_grad)
                    if biased:
                        diag_ref[index - tile, head] += score_grad.astype(jnp.float32)
                dka_ref[pl.ds(at, tall), lanes] = dk
                dva_ref[pl.ds(at, tall), lanes] = dv
            return carry

        lax.fori_loop(low_ref[index], high_ref[index], one_tile, 0)
        dq_ref[pl.ds(start, block), pl.ds(0, width)] = jnp.transpose(dqt_ref[...]).astype(jnp.bfloat16)
        return 0

    lax.fori_loop(0, rows // block, one_block, 0)
    dkv_ref[:, pl.ds(at_key, width)] = dka_ref[...].astype(jnp.bfloat16)
    dkv_ref[:, pl.ds(at_value, width)] = dva_ref[...].astype(jnp.bfloat16)
    store_order(me_ref[0], dq_ref, out_refs)
    if biased:
        def one_diagonal(index, _):
            offset, head = index >> (heads.bit_length() - 1), index & (heads - 1)
            slab = jnp.zeros((8, 2 * block), jnp.float32)
            for group in range(block // 8):
                piece = diag_ref[offset, head, pl.ds(8 * group, 8), :]
                wide = jnp.concatenate([piece, jnp.zeros_like(piece)], axis=1)
                slab = slab + (pltpu.roll(wide, 2 * block - 8 * group, 1) if group else wide)
            line = slab[0:1]
            for row in range(1, 8):
                line = line + pltpu.roll(slab[row : row + 1], 2 * block - row, 1)
            series_ref[offset, pl.ds(head, 1), :] = line
            return 0

        lax.fori_loop(0, diag_ref.shape[0] * heads, one_diagonal, 0)


def attend_backward(ranges, me, queries, keys_values, grads, context_t, totals, bias, heads, block, tall):
    low_block, high_block, first, last = ranges
    pieces = len(queries)
    size, depth = queries[0].shape
    rows = pieces * size
    width = heads * DK
    biased = bias is not None
    at_key = width if biased else 0
    key_rows = rows if biased else keys_values.shape[0]
    operands = [low_block, high_block, me[None], context_t, totals, first, last, bias if biased else keys_values]
    operands += [*queries, *grads]
    shapes = [jax.ShapeDtypeStruct((size, depth), jnp.bfloat16)] * pieces
    scratch = [
        pltpu.VMEM((width, block), jnp.float32),
        pltpu.VMEM((width, key_rows), jnp.bfloat16),
        pltpu.VMEM((key_rows, width), jnp.float32),
        pltpu.VMEM((key_rows, width), jnp.float32),
        pltpu.VMEM((rows, depth), jnp.bfloat16),
        pltpu.VMEM((rows, width), jnp.bfloat16),
        pltpu.VMEM((rows, depth), jnp.bfloat16),
    ]
    if biased:
        shapes.append(jax.ShapeDtypeStruct((bias.shape[0], heads, 2 * block), jnp.float32))
        scratch.append(pltpu.VMEM(bias.shape, jnp.float32))
    else:
        shapes.append(jax.ShapeDtypeStruct((key_rows, 2 * width), jnp.bfloat16))
    return pl.pallas_call(
        functools.partial(
            backward_kernel,
            heads=heads,
            block=block,
            tall=tall,
            biased=biased,
            at_key=at_key,
            at_value=at_key + width,
            pieces=pieces,
        ),
        out_shape=tuple(shapes),
        in_specs=[SMEM_SPEC] * 3 + [VMEM_SPEC] * (len(operands) - 3),
        out_specs=(VMEM_SPEC,) * len(shapes),
        scratch_shapes=scratch,
        compiler_params=pltpu.CompilerParams(vmem_limit_bytes=36 << 20),
        cost_estimate=lasting(1),
        name="attend_backward",
    )(*operands)


def place_kernel(me_ref, *refs, first):
    out_ref = refs[-1]
    pieces = refs[:-1]
    size = out_ref.shape[0] // len(pieces)
    for order, piece in enumerate(pieces):
        at = pl.multiple_of((me_ref[0] ^ order) * size, size)
        out_ref[pl.ds(at, size), :] = piece[pl.ds(first, size), :]


def place(pieces, me, first=0, size=None):
    size = size or pieces[0].shape[0]
    width = pieces[0].shape[1]
    count = len(pieces)
    return pl.pallas_call(
        functools.partial(place_kernel, first=first),
        out_shape=jax.ShapeDtypeStruct((count * size, width), pieces[0].dtype),
        in_specs=[SMEM_SPEC] + [VMEM_SPEC] * count,
        out_specs=VMEM_SPEC,
        compiler_params=pltpu.CompilerParams(vmem_limit_bytes=8 << 20),
        cost_estimate=lasting(2),
        name="place",
    )(me[None], *pieces)


def swap_kernel(me_ref, rows_ref, out_ref, *, count):
    size = rows_ref.shape[0] // count
    for order in range(count):
        at = pl.multiple_of((me_ref[0] ^ order) * size, size)
        out_ref[pl.ds(order * size, size), :] = rows_ref[pl.ds(at, size), :]


def swap_order(rows, me, count=4):
    return pl.pallas_call(
        functools.partial(swap_kernel, count=count),
        out_shape=jax.ShapeDtypeStruct(rows.shape, rows.dtype),
        in_specs=[SMEM_SPEC, VMEM_SPEC],
        out_specs=VMEM_SPEC,
        compiler_params=pltpu.CompilerParams(vmem_limit_bytes=4 << 20),
        cost_estimate=lasting(1),
        name="swap_order",
    )(me[None], rows)


def multiply_kernel(*refs, at, depth, transposed):
    count = (len(refs) - 1) // 2
    weights_ref = refs[0]
    width = refs[-1].shape[1]
    chunk = min(256, width)

    def one_chunk(index, _):
        start = pl.multiple_of(index * chunk, chunk)
        if transposed:
            weights = weights_ref[pl.ds(start, chunk), pl.ds(at, depth)]
        else:
            weights = weights_ref[:, pl.ds(at + start, chunk)]
        for rows_ref, out_ref in zip(refs[1 : 1 + count], refs[1 + count :]):
            product_of = nt_product if transposed else nn_product
            out_ref[:, pl.ds(start, chunk)] = product_of(rows_ref[:, pl.ds(0, depth)], weights).astype(out_ref.dtype)
        return 0

    lax.fori_loop(0, width // chunk, one_chunk, 0)


def multiply(pieces, weights, at, width, kinds=jnp.bfloat16, transposed=False, depth=None):
    kinds = kinds if isinstance(kinds, (list, tuple)) else [kinds] * len(pieces)
    return pl.pallas_call(
        functools.partial(multiply_kernel, at=at, depth=depth or pieces[0].shape[1], transposed=transposed),
        out_shape=[jax.ShapeDtypeStruct((piece.shape[0], width), kind) for piece, kind in zip(pieces, kinds)],
        in_specs=[VMEM_SPEC] * (1 + len(pieces)),
        out_specs=[VMEM_SPEC] * len(pieces),
        compiler_params=pltpu.CompilerParams(vmem_limit_bytes=16 << 20),
        cost_estimate=lasting(2),
        name="multiply",
    )(weights, *pieces)


def weights_kernel(*refs, groups, chunk):
    out_ref = refs[-1]
    features = out_ref.shape[0]

    def one_chunk(index, _):
        at = pl.multiple_of(index * chunk, chunk)
        operand = 0
        column = 0
        for terms, width in groups:
            total = None
            for _ in range(terms):
                left_ref, right_ref = refs[operand], refs[operand + 1]
                operand += 2
                term = lax.dot_general(
                    left_ref[:, pl.ds(at, chunk)],
                    right_ref[:, pl.ds(0, width)],
                    (((0,), (0,)), ((), ())),
                    preferred_element_type=jnp.float32,
                )
                total = term if total is None else total + term
            out_ref[pl.ds(at, chunk), pl.ds(column, width)] = total.astype(jnp.bfloat16)
            column += width
        return 0

    lax.fori_loop(0, features // chunk, one_chunk, 0)


def weight_grads(groups, width=None):
    operands = [array for group in groups for pair in group for array in pair]
    features = operands[0].shape[1]
    shapes = tuple((len(group), width or group[0][1].shape[1]) for group in groups)
    return pl.pallas_call(
        functools.partial(weights_kernel, groups=shapes, chunk=256),
        out_shape=jax.ShapeDtypeStruct((features, sum(wide for _, wide in shapes)), jnp.bfloat16),
        in_specs=[VMEM_SPEC] * len(operands),
        out_specs=VMEM_SPEC,
        compiler_params=pltpu.CompilerParams(vmem_limit_bytes=32 << 20),
        cost_estimate=lasting(16 if width else 8),
        name="weight_grads",
    )(*operands)


def feed_kernel(*refs, hidden, padded):
    weights_ref = refs[0]
    rows_refs, top_refs = refs[1:3], refs[3:5]
    hidden_refs, gate_refs, up_refs, back_refs = refs[5:7], refs[7:9], refs[9:11], refs[11:13]
    gate_ref, wide_ref, down_ref = refs[13:]
    features = weights_ref.shape[0]
    for order, target in enumerate((gate_ref, wide_ref, down_ref)):
        target[:, pl.ds(0, hidden)] = weights_ref[:, pl.ds(order * hidden, hidden)]
        if padded > hidden:
            target[:, pl.ds(hidden, padded - hidden)] = jnp.zeros((features, padded - hidden), jnp.bfloat16)

    def one_chunk(index, _):
        lanes = pl.ds(pl.multiple_of(index * 256, 256), 256)
        for piece in range(2):
            gate = nn_product(rows_refs[piece][...], gate_ref[:, lanes])
            up = nn_product(rows_refs[piece][...], wide_ref[:, lanes])
            hidden_grad = nn_product(top_refs[piece][...], down_ref[:, lanes])
            gelu_value, gelu_slope = gelu_parts(gate)
            hidden_refs[piece][:, lanes] = low(gelu_value * up)
            gate_refs[piece][:, lanes] = low(hidden_grad * up * gelu_slope)
            up_refs[piece][:, lanes] = low(hidden_grad * gelu_value)
        return 0

    lax.fori_loop(0, padded // 256, one_chunk, 0)

    def one_back(index, _):
        part = pl.ds(pl.multiple_of(index * 256, 256), 256)
        for piece in range(2):
            back = nt_product(gate_refs[piece][...], gate_ref[part, :]) + nt_product(up_refs[piece][...], wide_ref[part, :])
            back_refs[piece][:, part] = back.astype(back_refs[piece].dtype)
        return 0

    lax.fori_loop(0, features // 256, one_back, 0)


def feed(rows, top, weights, hidden):
    size, features = rows[0].shape
    padded = (hidden + 255) // 256 * 256
    kept = [jax.ShapeDtypeStruct((size, padded), jnp.bfloat16)] * 6
    back = [jax.ShapeDtypeStruct((size, features), kind) for kind in (jnp.float32, jnp.bfloat16)]
    outs = pl.pallas_call(
        functools.partial(feed_kernel, hidden=hidden, padded=padded),
        out_shape=kept + back,
        in_specs=[VMEM_SPEC] * 5,
        out_specs=[VMEM_SPEC] * 8,
        scratch_shapes=[pltpu.VMEM((features, padded), jnp.bfloat16)] * 3,
        compiler_params=pltpu.CompilerParams(vmem_limit_bytes=32 << 20),
        cost_estimate=lasting(12),
        name="feed",
    )(weights, *rows, *top)
    return outs[0:2], outs[2:4], outs[4:6], outs[6:8]


ROW_TILE = 64


def join_kernel(*refs, terms):
    stream_ref, gain_ref = refs[terms : terms + 2]
    joined_ref, normed_ref = refs[terms + 2 :]

    def one_tile(index, _):
        tile = pl.ds(pl.multiple_of(index * ROW_TILE, ROW_TILE), ROW_TILE)
        rows = stream_ref[tile, :].astype(jnp.float32)
        for ref in refs[:terms]:
            rows = rows + ref[tile, :].astype(jnp.float32)
        joined_ref[tile, :] = rows
        normed_ref[tile, :] = low(rows * norm_scale(rows) * gain_ref[...])
        return 0

    lax.fori_loop(0, stream_ref.shape[0] // ROW_TILE, one_tile, 0)


def join(terms, stream, gain):
    return pl.pallas_call(
        functools.partial(join_kernel, terms=len(terms)),
        out_shape=[jax.ShapeDtypeStruct(stream.shape, kind) for kind in (jnp.float32, jnp.bfloat16)],
        in_specs=[VMEM_SPEC] * (len(terms) + 2),
        out_specs=[VMEM_SPEC] * 2,
        compiler_params=pltpu.CompilerParams(vmem_limit_bytes=12 << 20),
        cost_estimate=lasting(4),
        name="join",
    )(*terms, stream, gain[None])


def join_back_kernel(*refs, terms):
    stream_ref, upper_ref, gain_ref = refs[terms : terms + 3]
    total_ref, rounded_ref, gain_grad_ref = refs[terms + 3 :]
    gain_grad_ref[...] = jnp.zeros_like(gain_grad_ref)

    def one_tile(index, _):
        tile = pl.ds(pl.multiple_of(index * ROW_TILE, ROW_TILE), ROW_TILE)
        grads = refs[0][tile, :].astype(jnp.float32)
        for ref in refs[1:terms]:
            grads = grads + ref[tile, :].astype(jnp.float32)
        rows = stream_ref[tile, :].astype(jnp.float32)
        scale = norm_scale(rows)
        scaled = grads * gain_ref[...]
        row_grad = scale * scaled - rows * (scale * scale * scale) * jnp.mean(scaled * rows, axis=-1, keepdims=True)
        total = upper_ref[tile, :].astype(jnp.float32) + row_grad
        total_ref[tile, :] = total
        rounded_ref[tile, :] = low(total)
        gain_grad_ref[...] += jnp.sum(grads * rows * scale, axis=0, keepdims=True)
        return 0

    lax.fori_loop(0, stream_ref.shape[0] // ROW_TILE, one_tile, 0)


def join_back(terms, stream, upper, gain):
    total, rounded, gain_grad = pl.pallas_call(
        functools.partial(join_back_kernel, terms=len(terms)),
        out_shape=[
            jax.ShapeDtypeStruct(stream.shape, jnp.float32),
            jax.ShapeDtypeStruct(stream.shape, jnp.bfloat16),
            jax.ShapeDtypeStruct((1, stream.shape[1]), jnp.float32),
        ],
        in_specs=[VMEM_SPEC] * (len(terms) + 3),
        out_specs=[VMEM_SPEC] * 3,
        compiler_params=pltpu.CompilerParams(vmem_limit_bytes=16 << 20),
        cost_estimate=lasting(5),
        name="join_back",
    )(*terms, stream, upper, gain[None])
    return total, rounded, gain_grad[0]


def exchange(rows, axis, size, bits):
    return lax.ppermute(rows, axis, [(i, i ^ bits) for i in range(size)])


def to_core(rows):
    return exchange(rows, "mp", PEERS, 1)


def across(rows):
    return exchange(rows, "mp", PEERS, 2)


def after(value, *others):
    return lax.optimization_barrier((value, *others))[0]


def gather_four(rows):
    far = across(rows)
    return rows, to_core(rows), far, to_core(far)


def prepare(own, other):
    return low(own + to_core(low(other)).astype(jnp.float32))


def sum_core(own, other):
    return own + to_core(low(other)).astype(jnp.float32)


def gather_weights(weights):
    return lax.all_gather(low(jnp.concatenate(weights, axis=1)), "dp", axis=0, tiled=True)


def reduce_weights(grads):
    return lax.psum_scatter(grads, "dp", scatter_dimension=0, tiled=True).astype(jnp.float32)


def reduce_directly(grads, size):
    return lax.all_to_all(grads, "dp", split_axis=0, concat_axis=0, tiled=True)


def sum_parts(arrived, size):
    return jnp.sum(arrived.reshape(size, -1, arrived.shape[1]).astype(jnp.float32), axis=0)


def sum_everywhere(value, sizes):
    for axis in ("mp", "dp"):
        step = 1
        while step < sizes[axis]:
            value = value + exchange(value, axis, sizes[axis], step)
            step *= 2
    return value


def columns_of(array, widths):
    pieces = []
    at = 0
    for width in widths:
        pieces.append(array[:, at : at + width])
        at += width
    return pieces


def key_ranges(ids, key_ids, documents):
    numbers = jnp.arange(documents, dtype=jnp.int32)
    below = jnp.sum((key_ids[None, :] < numbers[:, None]).astype(jnp.int32), axis=1)
    upto = jnp.sum((key_ids[None, :] <= numbers[:, None]).astype(jnp.int32), axis=1)
    mine = (ids[None, :] == numbers[:, None]).astype(jnp.int32)
    return (jnp.sum(mine * below[:, None], axis=0), jnp.sum(mine * upto[:, None], axis=0))


def block_ranges(first, last, block, tall):
    return (first[::block] // tall, (last[block - 1 :: block] + tall - 1) // tall)


DOCUMENTS = 8
LONGEST = 768


def per_device(
    tokens,
    encoder_out,
    segments,
    encoder_segments,
    buckets,
    rel_table,
    gain_attend,
    gain_cross,
    gain_feed,
    self_query,
    self_key,
    self_value,
    self_output,
    cross_query,
    cross_key,
    cross_value,
    cross_output,
    w_gate,
    w_up,
    w_down,
    out_grad,
    *,
    sizes,
):
    parts = sizes["dp"]
    wide = self_query.shape[1]
    hidden_wide = w_gate.shape[1]
    heads = wide // DK
    block = 256
    own_rows = tokens.shape[0]
    me = lax.axis_index("mp")

    self_all = gather_weights([self_query, self_key, self_value, self_output.T])
    cross_all = gather_weights([cross_query, cross_key, cross_value, cross_output.T])
    feed_shard = low(jnp.concatenate([w_gate, w_up, w_down.T], axis=1))
    feed_all = lax.all_gather(feed_shard, "dp", axis=0, tiled=True)
    buckets_count = rel_table.shape[0]
    stream_zero = tokens.astype(jnp.float32)
    scale_zero = norm_scale(stream_zero)
    normed_zero = low(stream_zero * scale_zero * gain_attend)
    features = tokens.shape[1]
    encoder_rows = encoder_out.shape[0]
    ids = jnp.concatenate([segments, encoder_segments], axis=1)
    ids = jnp.pad(ids, ((0, 15), (0, features - ids.shape[1]))).astype(jnp.bfloat16)
    row_pieces = gather_four(jnp.concatenate([normed_zero, encoder_out, ids], axis=0))
    normed_one = [piece[:own_rows] for piece in row_pieces]
    encoder_all = place(row_pieces, me, own_rows, encoder_rows)
    top = list(gather_four(after(out_grad, *row_pieces)))

    id_rows = jnp.concatenate([piece[own_rows + encoder_rows :][:1] for piece in row_pieces], axis=0).astype(jnp.int32)
    near_ids = id_rows[:2, :own_rows].reshape(-1)
    ids = jnp.concatenate([lax.dynamic_slice_in_dim(id_rows, me ^ peer, 1, 0) for peer in range(PEERS)], axis=0)
    decoder_ids = ids[:, :own_rows].reshape(-1)
    encoder_ids = ids[:, own_rows : own_rows + encoder_rows].reshape(-1)
    length = decoder_ids.shape[0]
    self_first, unused = key_ranges(decoder_ids, decoder_ids, DOCUMENTS)
    self_last = jnp.arange(length, dtype=jnp.int32) + 1
    self_low, self_high = block_ranges(self_first, self_last, block, block)
    self_ranges = (self_low, self_high, self_first[None], self_last[None])
    cross_first, cross_last = key_ranges(near_ids, encoder_ids, DOCUMENTS)
    cross_low, cross_high = block_ranges(cross_first, cross_last, own_rows, block)
    cross_ranges = (cross_low, cross_high, cross_first[None], cross_last[None])

    offsets = min((LONGEST + block - 2) // block + 1, length // block)
    reach = offsets * block
    table_local = lax.dynamic_slice_in_dim(rel_table, me * heads, heads, 1)
    onehot = (buckets[None, :reach] == jnp.arange(buckets_count, dtype=jnp.int32)[:, None]).astype(jnp.float32)
    series = lax.dot_general(table_local, onehot, (((0,), (0,)), ((), ())), precision=lax.Precision.HIGHEST)
    bias = bias_tiles(jnp.pad(series, ((0, 0), (block, 0))), offsets, block)

    wider = [jnp.float32, jnp.bfloat16]
    qkv = multiply(normed_one, after(self_all, top[2], top[3], feed_shard), 0, 3 * wide)
    *context_one, context_one_t, totals_one = attend_forward(self_ranges, me, qkv, None, bias, heads, block, block)
    terms = multiply(context_one[2:], self_all, 3 * wide, features, wider, True)
    far_sum = across(prepare(*terms))
    terms = multiply(context_one[:2], self_all, 3 * wide, features, wider, True)
    far_sum = after(far_sum, terms[0])
    stream_one, normed_own = join([terms[0], to_core(terms[1]), far_sum], tokens, gain_cross)

    cross_other = across(after(cross_all, normed_own))
    cross_weights = [cross_all, cross_other]
    normed_two = [normed_own, to_core(normed_own)]
    still = jnp.zeros_like(me)
    queries_two, keys_values_two, contexts_two, backs_two = [], [], [], []
    for weights in cross_weights:
        queries_two.append(multiply(normed_two, weights, 0, wide))
        keys_values_two += multiply([encoder_all], weights, wide, 2 * wide)
        *context, context_t, totals = attend_forward(
            cross_ranges, still, queries_two[-1], keys_values_two[-1], None, heads, own_rows, block
        )
        contexts_two.append(context)
        backs_two.append((context_t, totals))
    terms = [multiply(context, weights, 3 * wide, features, wider, True) for context, weights in zip(contexts_two, cross_weights)]
    stream_two, normed_own = join(
        [terms[0][0], terms[1][0], to_core(terms[0][1] + terms[1][1])], stream_one, gain_feed
    )

    normed_three = [normed_own, to_core(normed_own)]
    hidden_near, gate_grad_near, up_grad_near, back_near = feed(normed_three, top[:2], feed_all, hidden_wide)
    far_own = after(across(normed_own), *hidden_near, *gate_grad_near, *up_grad_near, *back_near)
    normed_three += [far_own, to_core(far_own)]
    hidden_far, gate_grad_far, up_grad_far, back_far = feed(normed_three[2:], top[2:], feed_all, hidden_wide)
    far_ready = prepare(*back_far)
    far_sum = across(far_ready)
    top[3] = after(top[3], far_ready)
    hidden = hidden_near + hidden_far
    feed_grads = weight_grads(
        [
            list(zip(normed_three, gate_grad_near + gate_grad_far)),
            list(zip(normed_three, up_grad_near + up_grad_far)),
            list(zip(top, hidden)),
        ],
        hidden_wide,
    )
    far_sum = after(far_sum, feed_grads)
    feed_sums = lax.psum_scatter(feed_grads, "dp", scatter_dimension=0, tiled=True)
    stream_grad, grad_own, feed_gain_grad = join_back(
        [back_near[0], to_core(back_near[1]), far_sum], stream_two, out_grad, gain_feed
    )

    grad_two = [grad_own, to_core(grad_own)]
    query_grads, key_value_grads, backs = [], [], []
    for weights, queries, keys_values, back in zip(cross_weights, queries_two, keys_values_two, backs_two):
        context_grad = multiply(grad_two, weights, 3 * wide, wide)
        *query_grad, key_value_grad = attend_backward(
            cross_ranges, still, queries, keys_values, context_grad, *back, None, heads, own_rows, block
        )
        query_grads.append(query_grad)
        key_value_grads.append(key_value_grad)
        backs.append(multiply(query_grad, weights, 0, features, wider, True))
    stream_grad, grad_own, cross_gain_grad = join_back(
        [backs[0][0], backs[1][0], to_core(backs[0][1] + backs[1][1])], stream_one, stream_grad, gain_cross
    )

    grad_peer = to_core(grad_own)
    context_grad = multiply([grad_own, grad_peer], self_all, 3 * wide, wide)
    cross_grads = [
        weight_grads([list(zip(normed_two, query_grad)), [(encoder_all, key_value_grad)], list(zip(grad_two, context))])
        for query_grad, key_value_grad, context in zip(query_grads, key_value_grads, contexts_two)
    ]
    cross_far = across(cross_grads[1])
    layer_terms = multiply(hidden_far, feed_all, 2 * hidden_wide, features, wider, True, hidden_wide)
    layer_ready = prepare(*layer_terms)
    encoder_terms = [
        multiply([swap_order(key_value_grad, me)], weights, wide, features, jnp.bfloat16, True)[0]
        for key_value_grad, weights in zip(key_value_grads, cross_weights)
    ]
    encoder_terms = encoder_terms[0].astype(jnp.float32) + encoder_terms[1].astype(jnp.float32)
    encoder_terms = [encoder_terms[at : at + encoder_rows] for at in range(0, PEERS * encoder_rows, encoder_rows)]
    encoder_ready = prepare(encoder_terms[2], encoder_terms[3])
    grad_far = after(across(grad_own), *context_grad, *cross_grads, layer_ready, encoder_ready)
    grad_one = [grad_own, grad_peer, grad_far, to_core(grad_far)]
    context_grad = context_grad + multiply(grad_one[2:], self_all, 3 * wide, wide)
    *qkv_grad, diagonals = attend_backward(
        self_ranges, me, qkv, None, context_grad, context_one_t, totals_one, bias, heads, block, block
    )
    self_grads = weight_grads([list(zip(normed_one, qkv_grad)), list(zip(grad_one, context_one))])
    self_parts = reduce_directly(self_grads, parts)
    cross_far = after(cross_far, self_grads, feed_sums)
    cross_parts = lax.psum_scatter(
        low(cross_grads[0].astype(jnp.float32) + cross_far.astype(jnp.float32)), "dp", scatter_dimension=0, tiled=True
    )
    terms = multiply(qkv_grad[2:], self_all, 0, features, wider, True)
    far_sum = across(prepare(*terms))
    terms = multiply(qkv_grad[:2], self_all, 0, features, wider, True)
    tokens_grad, unused, attend_gain_grad = join_back(
        [terms[0], to_core(terms[1]), far_sum], tokens, stream_grad, gain_attend
    )

    ahead = jnp.moveaxis(diagonals[:, :, :block], 0, 1).reshape(heads, reach)
    behind = jnp.moveaxis(diagonals[1:, :, block:], 0, 1).reshape(heads, reach - block)
    series_grad = ahead + jnp.pad(behind, ((0, 0), (0, block)))
    table_grad = lax.dot_general(onehot, series_grad, (((1,), (1,)), ((), ())), precision=lax.Precision.HIGHEST)
    table_full = lax.dynamic_update_slice(jnp.zeros(rel_table.shape, jnp.float32), table_grad, (0, me * heads))
    small = jnp.concatenate([attend_gain_grad, cross_gain_grad, feed_gain_grad, table_full.reshape(-1)])
    small = sum_everywhere(small.reshape(-1, 128), sizes).reshape(-1)
    layer_far, encoder_far = across(after(layer_ready, far_sum)), across(after(encoder_ready, far_sum))
    small, layer_far, encoder_far = lax.optimization_barrier((small, layer_far, encoder_far))
    layer_terms = multiply(hidden_near, feed_all, 2 * hidden_wide, features, wider, True, hidden_wide)
    layer_out = low(stream_two + sum_core(*layer_terms) + layer_far.astype(jnp.float32))
    encoder_grad = sum_core(encoder_terms[0], encoder_terms[1]) + encoder_far.astype(jnp.float32)

    attend_gain_sum, cross_gain_sum, feed_gain_sum = (
        small[:features],
        small[features : 2 * features],
        small[2 * features : 3 * features],
    )
    table_sum = small[3 * features :].reshape(rel_table.shape)
    self_sums = sum_parts(self_parts, parts)
    cross_sums = cross_parts.astype(jnp.float32)
    feed_sums = feed_sums.astype(jnp.float32)
    query_one_sum, key_one_sum, value_one_sum, output_one_sum = columns_of(self_sums, [wide] * 4)
    query_two_sum, key_two_sum, value_two_sum, output_two_sum = columns_of(cross_sums, [wide] * 4)
    gate_sum, up_sum, down_sum = columns_of(feed_sums, [hidden_wide] * 3)
    return (
        layer_out,
        tokens_grad,
        encoder_grad,
        table_sum,
        attend_gain_sum,
        cross_gain_sum,
        feed_gain_sum,
        query_one_sum,
        key_one_sum,
        value_one_sum,
        output_one_sum.T,
        query_two_sum,
        key_two_sum,
        value_two_sum,
        output_two_sum.T,
        gate_sum,
        up_sum,
        down_sum.T,
    )


def solution(mesh):
    in_specs = (
        P(("dp", "mp"), None),
        P(("dp", "mp"), None),
        P("dp", "mp"),
        P("dp", "mp"),
        P(),
        P(),
        P(),
        P(),
        P(),
        P("dp", "mp"),
        P("dp", "mp"),
        P("dp", "mp"),
        P("mp", "dp"),
        P("dp", "mp"),
        P("dp", "mp"),
        P("dp", "mp"),
        P("mp", "dp"),
        P("dp", "mp"),
        P("dp", "mp"),
        P("mp", "dp"),
        P(("dp", "mp"), None),
    )
    out_specs = (
        P(("dp", "mp"), None),
        P(("dp", "mp"), None),
        P(("dp", "mp"), None),
        P(),
        P(),
        P(),
        P(),
        P("dp", "mp"),
        P("dp", "mp"),
        P("dp", "mp"),
        P("mp", "dp"),
        P("dp", "mp"),
        P("dp", "mp"),
        P("dp", "mp"),
        P("mp", "dp"),
        P("dp", "mp"),
        P("dp", "mp"),
        P("mp", "dp"),
    )
    return jax.shard_map(
        functools.partial(per_device, sizes=dict(mesh.shape)), mesh=mesh, in_specs=in_specs, out_specs=out_specs, check_vma=False
    )
```

```python
import functools
import jax
import jax.numpy as jnp
from jax import lax
from jax.experimental import pallas as pl
from jax.experimental.pallas import tpu as pltpu
from jax.sharding import PartitionSpec as P

DK = 64
PAIR = 2 * DK
NEG = -1e30
PEERS = 4

norm_eps = 1e-06
gelu_factor = 0.7978845608028654


def product(left, right):
    return jnp.dot(left, right, preferred_element_type=jnp.float32)


def rows_product(left, right):
    return lax.dot_general(left, right, (((0,), (0,)), ((), ())), preferred_element_type=jnp.float32)


def columns_product(left, right):
    return lax.dot_general(left, right, (((1,), (1,)), ((), ())), preferred_element_type=jnp.float32)


def norm_scale(rows):
    return lax.rsqrt(jnp.mean(rows * rows, axis=-1, keepdims=True) + norm_eps)


def gelu_parts(value):
    cubic = 0.044715 * value * value * value
    tangent = jnp.tanh(gelu_factor * (value + cubic))
    result = 0.5 * value * (1.0 + tangent)
    slope = 0.5 * (1.0 + tangent) + 0.5 * value * (1.0 - tangent * tangent) * gelu_factor * (
        1.0 + 3.0 * 0.044715 * value * value
    )
    return (result, slope)


def norm_back(grads, rows, scale, gain):
    scaled = grads * gain
    row_grad = scale * scaled - rows * (scale * scale * scale) * jnp.mean(scaled * rows, axis=-1, keepdims=True)
    gain_grad = jnp.sum(grads * rows * scale, axis=0)
    return (row_grad, gain_grad)


def low(value):
    return value.astype(jnp.bfloat16)


def nt_product(left, right):
    return lax.dot_general(left, right, (((1,), (1,)), ((), ())), preferred_element_type=jnp.float32)


def nn_product(left, right):
    return jnp.dot(left, right, preferred_element_type=jnp.float32)


def own_lanes(rows, head):
    lane = lax.broadcasted_iota(jnp.int32, rows.shape, 1)
    mine = (lane < DK) if head % 2 == 0 else (lane >= DK)
    return jnp.where(mine, rows, jnp.zeros_like(rows))


def bias_kernel(series_ref, tiles_ref, *, block):
    heads = series_ref.shape[0]
    for offset in range(tiles_ref.shape[0]):
        for head in range(heads):
            low = series_ref[pl.ds(head, 1), pl.ds(offset * block, block)]
            high = series_ref[pl.ds(head, 1), pl.ds((offset + 1) * block, block)]
            base = jnp.broadcast_to(jnp.concatenate([high, low], axis=1), (block, 2 * block))
            rolled = pltpu.roll(base, 0, 1, stride=1, stride_axis=0)
            tiles_ref[offset, head] = rolled[:, :block]


def bias_tiles(series, offsets, block):
    heads = series.shape[0]
    return pl.pallas_call(
        functools.partial(bias_kernel, block=block),
        out_shape=jax.ShapeDtypeStruct((offsets, heads, block, block), jnp.float32),
        compiler_params=pltpu.CompilerParams(vmem_limit_bytes=16 << 20),
        cost_estimate=lasting(4),
        name="bias_tiles",
    )(series)


def load_order(me, pieces, target_ref):
    size = pieces[0].shape[0]
    for order, piece in enumerate(pieces):
        at = pl.multiple_of((me ^ order) * size, size)
        target_ref[pl.ds(at, size), :] = piece[...]


def store_order(me, source_ref, pieces):
    size = pieces[0].shape[0]
    for order, piece in enumerate(pieces):
        at = pl.multiple_of((me ^ order) * size, size)
        piece[...] = source_ref[pl.ds(at, size), :].astype(jnp.bfloat16)


def forward_kernel(*refs, heads, block, tall, biased, at_key, at_value, pieces):
    low_ref, high_ref, me_ref, first_ref, last_ref, extra_ref = refs[:6]
    piece_refs = refs[6 : 6 + pieces]
    ctx_refs = refs[6 + pieces : 6 + 2 * pieces]
    ot_ref, lse_ref, acc_ref, vt_ref, q_ref, ctx_ref = refs[6 + 2 * pieces :]
    if biased:
        bias_ref, kv_ref = extra_ref, q_ref
    else:
        kv_ref = extra_ref
    load_order(me_ref[0], piece_refs, q_ref)
    rows = q_ref.shape[0]
    width = heads * DK
    key_iota = lax.broadcasted_iota(jnp.int32, (tall, block), 0)
    for tile in range(kv_ref.shape[0] // tall):
        vt_ref[:, pl.ds(tile * tall, tall)] = jnp.transpose(kv_ref[pl.ds(tile * tall, tall), pl.ds(at_value, width)])

    def one_block(index, _):
        start = pl.multiple_of(index * block, block)
        first = first_ref[:, pl.ds(start, block)]
        last = last_ref[:, pl.ds(start, block)]
        queries = [
            own_lanes(q_ref[pl.ds(start, block), pl.ds((head // 2) * PAIR, PAIR)], head) for head in range(heads)
        ]
        acc_ref[...] = jnp.zeros_like(acc_ref)

        def one_tile(tile, carry):
            at = pl.multiple_of(tile * tall, tall)
            valid = (key_iota >= first - at) & (key_iota < last - at)
            scores = []
            for head in range(heads):
                keys = kv_ref[pl.ds(at, tall), pl.ds(at_key + (head // 2) * PAIR, PAIR)]
                score = nt_product(keys, queries[head])
                if biased:
                    score = score + bias_ref[index - tile, head]
                scores.append(jnp.where(valid, score, NEG))
            results = []
            raised = []
            shrinks = []
            for head in range(heads):
                top, total = carry[head]
                new_top = jnp.maximum(top, jnp.max(scores[head], axis=0, keepdims=True))
                power = jnp.exp(scores[head] - new_top)
                shrink = jnp.exp(top - new_top)
                results.append((new_top, shrink * total + jnp.sum(power, axis=0, keepdims=True)))
                raised.append(power.astype(jnp.bfloat16))
                shrinks.append(shrink)
            for head in range(heads):
                mine = pl.ds(head * DK, DK)
                acc_ref[mine, :] = acc_ref[mine, :] * shrinks[head] + nn_product(
                    vt_ref[mine, pl.ds(at, tall)], raised[head]
                )
            return tuple(results)

        empty = tuple(
            (jnp.full((1, block), NEG, jnp.float32), jnp.zeros((1, block), jnp.float32)) for _ in range(heads)
        )
        stats = lax.fori_loop(low_ref[index], high_ref[index], one_tile, empty)
        for head in range(heads):
            top, total = stats[head]
            mine = pl.ds(head * DK, DK)
            acc_ref[mine, :] = acc_ref[mine, :] / total
            lse_ref[pl.ds(head, 1), pl.ds(start, block)] = top + jnp.log(total)
        ot_ref[:, pl.ds(start, block)] = acc_ref[...]
        ctx_ref[pl.ds(start, block), :] = jnp.transpose(acc_ref[...])
        return 0

    lax.fori_loop(0, rows // block, one_block, 0)
    store_order(me_ref[0], ctx_ref, ctx_refs)


def lasting(micros):
    return pl.CostEstimate(flops=int(micros * 1.1e9), bytes_accessed=1 << 10, transcendentals=0)


SMEM_SPEC = pl.BlockSpec(memory_space=pltpu.SMEM)
VMEM_SPEC = pl.BlockSpec(memory_space=pltpu.VMEM)


def attend_forward(ranges, me, queries, keys_values, bias, heads, block, tall):
    low_block, high_block, first, last = ranges
    pieces = len(queries)
    size, depth = queries[0].shape
    rows = pieces * size
    width = heads * DK
    biased = bias is not None
    at_key = width if biased else 0
    key_rows = rows if biased else keys_values.shape[0]
    operands = [low_block, high_block, me[None], first, last, bias if biased else keys_values, *queries]
    return pl.pallas_call(
        functools.partial(
            forward_kernel,
            heads=heads,
            block=block,
            tall=tall,
            biased=biased,
            at_key=at_key,
            at_value=at_key + width,
            pieces=pieces,
        ),
        out_shape=(
            *([jax.ShapeDtypeStruct((size, width), jnp.bfloat16)] * pieces),
            jax.ShapeDtypeStruct((width, rows), jnp.float32),
            jax.ShapeDtypeStruct((heads, rows), jnp.float32),
        ),
        in_specs=[SMEM_SPEC] * 3 + [VMEM_SPEC] * (len(operands) - 3),
        out_specs=(VMEM_SPEC,) * (pieces + 2),
        scratch_shapes=[
            pltpu.VMEM((width, block), jnp.float32),
            pltpu.VMEM((width, key_rows), jnp.bfloat16),
            pltpu.VMEM((rows, depth), jnp.bfloat16),
            pltpu.VMEM((rows, width), jnp.float32),
        ],
        compiler_params=pltpu.CompilerParams(vmem_limit_bytes=24 << 20),
        cost_estimate=lasting(14 if biased else 1),
        name="attend_forward",
    )(*operands)


def backward_kernel(*refs, heads, block, tall, biased, at_key, at_value, pieces):
    low_ref, high_ref, me_ref, ot_ref, lse_ref, first_ref, last_ref, extra_ref = refs[:8]
    piece_refs = refs[8 : 8 + pieces]
    g_refs = refs[8 + pieces : 8 + 2 * pieces]
    out_refs = refs[8 + 2 * pieces : 8 + 3 * pieces]
    refs = refs[8 + 3 * pieces :]
    if biased:
        diag_ref, dqt_ref, kt_ref, dka_ref, dva_ref, q_ref, g_ref, dq_ref = refs
        bias_ref = extra_ref
        kv_ref, dkv_ref = q_ref, dq_ref
    else:
        dkv_ref, dqt_ref, kt_ref, dka_ref, dva_ref, q_ref, g_ref, dq_ref = refs
        kv_ref = extra_ref
    load_order(me_ref[0], piece_refs, q_ref)
    load_order(me_ref[0], g_refs, g_ref)
    rows = q_ref.shape[0]
    width = heads * DK
    key_iota = lax.broadcasted_iota(jnp.int32, (tall, block), 0)
    for tile in range(kv_ref.shape[0] // tall):
        kt_ref[:, pl.ds(tile * tall, tall)] = jnp.transpose(kv_ref[pl.ds(tile * tall, tall), pl.ds(at_key, width)])
    dka_ref[...] = jnp.zeros_like(dka_ref)
    dva_ref[...] = jnp.zeros_like(dva_ref)
    if biased:
        diag_ref[...] = jnp.zeros_like(diag_ref)

    def one_block(index, _):
        start = pl.multiple_of(index * block, block)
        first = first_ref[:, pl.ds(start, block)]
        last = last_ref[:, pl.ds(start, block)]
        pairs = [pl.ds(pair * PAIR, PAIR) for pair in range(heads // 2)]
        queries = [own_lanes(q_ref[pl.ds(start, block), pairs[head // 2]], head) for head in range(heads)]
        grads = [own_lanes(g_ref[pl.ds(start, block), pairs[head // 2]], head) for head in range(heads)]
        shared = jnp.transpose(g_ref[pl.ds(start, block), :].astype(jnp.float32)) * ot_ref[:, pl.ds(start, block)]
        deltas = [jnp.sum(shared[head * DK : (head + 1) * DK], axis=0, keepdims=True) for head in range(heads)]
        totals = [lse_ref[pl.ds(head, 1), pl.ds(start, block)] for head in range(heads)]
        dqt_ref[...] = jnp.zeros_like(dqt_ref)

        def one_tile(tile, carry):
            at = pl.multiple_of(tile * tall, tall)
            valid = (key_iota >= first - at) & (key_iota < last - at)
            shares, score_grads = [], []
            for head in range(heads):
                pair = head // 2
                keys = kv_ref[pl.ds(at, tall), pl.ds(at_key + pair * PAIR, PAIR)]
                values = kv_ref[pl.ds(at, tall), pl.ds(at_value + pair * PAIR, PAIR)]
                scores = nt_product(keys, queries[head])
                share_grad = nt_product(values, grads[head])
                if biased:
                    scores = scores + bias_ref[index - tile, head]
                share = jnp.exp(jnp.where(valid, scores - totals[head], NEG))
                score_grad = (share * (share_grad - deltas[head])).astype(jnp.bfloat16)
                if biased:
                    diag_ref[index - tile, head] += score_grad.astype(jnp.float32)
                shares.append(share.astype(jnp.bfloat16))
                score_grads.append(score_grad)
            for pair in range(heads // 2):
                lanes = pl.ds(pair * PAIR, PAIR)
                one, two = 2 * pair, 2 * pair + 1
                dva_ref[pl.ds(at, tall), lanes] += nn_product(shares[one], grads[one]) + nn_product(shares[two], grads[two])
                dka_ref[pl.ds(at, tall), lanes] += nn_product(score_grads[one], queries[one]) + nn_product(
                    score_grads[two], queries[two]
                )
            for head in range(heads):
                mine = pl.ds(head * DK, DK)
                dqt_ref[mine, :] += nn_product(kt_ref[mine, pl.ds(at, tall)], score_grads[head])
            return carry

        lax.fori_loop(low_ref[index], high_ref[index], one_tile, 0)
        dq_ref[pl.ds(start, block), pl.ds(0, width)] = jnp.transpose(dqt_ref[...]).astype(jnp.bfloat16)
        return 0

    lax.fori_loop(0, rows // block, one_block, 0)
    dkv_ref[:, pl.ds(at_key, width)] = dka_ref[...].astype(jnp.bfloat16)
    dkv_ref[:, pl.ds(at_value, width)] = dva_ref[...].astype(jnp.bfloat16)
    store_order(me_ref[0], dq_ref, out_refs)


def diagonals_kernel(diag_ref, series_ref):
    offsets, heads, block, _ = diag_ref.shape

    def one_diagonal(index, _):
        offset, head = index >> (heads.bit_length() - 1), index & (heads - 1)
        slab = jnp.zeros((8, 2 * block), jnp.float32)
        for group in range(block // 8):
            piece = diag_ref[offset, head, pl.ds(8 * group, 8), :]
            wide = jnp.concatenate([piece, jnp.zeros_like(piece)], axis=1)
            slab = slab + (pltpu.roll(wide, 2 * block - 8 * group, 1) if group else wide)
        line = slab[0:1]
        for row in range(1, 8):
            line = line + pltpu.roll(slab[row : row + 1], 2 * block - row, 1)
        series_ref[offset, pl.ds(head, 1), :] = line
        return 0

    lax.fori_loop(0, offsets * heads, one_diagonal, 0)


def diagonal_sums(diagonals):
    offsets, heads, block, _ = diagonals.shape
    return pl.pallas_call(
        diagonals_kernel,
        out_shape=jax.ShapeDtypeStruct((offsets, heads, 2 * block), jnp.float32),
        in_specs=[VMEM_SPEC],
        out_specs=VMEM_SPEC,
        compiler_params=pltpu.CompilerParams(vmem_limit_bytes=8 << 20),
        cost_estimate=lasting(4),
        name="diagonal_sums",
    )(diagonals)


def attend_backward(ranges, me, queries, keys_values, grads, context_t, totals, bias, heads, block, tall):
    low_block, high_block, first, last = ranges
    pieces = len(queries)
    size, depth = queries[0].shape
    rows = pieces * size
    width = heads * DK
    biased = bias is not None
    at_key = width if biased else 0
    key_rows = rows if biased else keys_values.shape[0]
    operands = [low_block, high_block, me[None], context_t, totals, first, last, bias if biased else keys_values]
    operands += [*queries, *grads]
    shapes = [jax.ShapeDtypeStruct((size, depth), jnp.bfloat16)] * pieces
    scratch = [
        pltpu.VMEM((width, block), jnp.float32),
        pltpu.VMEM((width, key_rows), jnp.bfloat16),
        pltpu.VMEM((key_rows, width), jnp.float32),
        pltpu.VMEM((key_rows, width), jnp.float32),
        pltpu.VMEM((rows, depth), jnp.bfloat16),
        pltpu.VMEM((rows, width), jnp.bfloat16),
        pltpu.VMEM((rows, depth), jnp.bfloat16),
    ]
    if biased:
        shapes.append(jax.ShapeDtypeStruct(bias.shape, jnp.float32))
    else:
        shapes.append(jax.ShapeDtypeStruct((key_rows, 2 * width), jnp.bfloat16))
    return pl.pallas_call(
        functools.partial(
            backward_kernel,
            heads=heads,
            block=block,
            tall=tall,
            biased=biased,
            at_key=at_key,
            at_value=at_key + width,
            pieces=pieces,
        ),
        out_shape=tuple(shapes),
        in_specs=[SMEM_SPEC] * 3 + [VMEM_SPEC] * (len(operands) - 3),
        out_specs=(VMEM_SPEC,) * len(shapes),
        scratch_shapes=scratch,
        compiler_params=pltpu.CompilerParams(vmem_limit_bytes=36 << 20),
        cost_estimate=lasting(1),
        name="attend_backward",
    )(*operands)


def pack_kernel(*refs, turned):
    count = len(turned)
    out_ref, semaphores = refs[count], refs[-1]
    held = refs[count + 1 : -1]
    copies = [
        pltpu.make_async_copy(source, target, semaphores.at[order])
        for order, (source, target) in enumerate(zip(refs[:count], held))
    ]
    for copy in copies:
        copy.start()
    at = 0
    for copy, ref, turn in zip(copies, held, turned):
        copy.wait()
        piece = jnp.transpose(ref[...]) if turn else ref[...]
        out_ref[:, pl.ds(at, piece.shape[1])] = low(piece)
        at += piece.shape[1]


def pack(weights, turned):
    width = sum(weight.shape[0] if turn else weight.shape[1] for weight, turn in zip(weights, turned))
    rows = weights[0].shape[0]
    return pl.pallas_call(
        functools.partial(pack_kernel, turned=tuple(turned)),
        out_shape=jax.ShapeDtypeStruct((rows, width), jnp.bfloat16),
        in_specs=[pl.BlockSpec(memory_space=pltpu.HBM)] * len(weights),
        out_specs=VMEM_SPEC,
        scratch_shapes=[pltpu.VMEM(weight.shape, jnp.float32) for weight in weights]
        + [pltpu.SemaphoreType.DMA((len(weights),))],
        compiler_params=pltpu.CompilerParams(vmem_limit_bytes=12 << 20),
        cost_estimate=lasting(2),
        name="pack",
    )(*[pltpu.with_memory_space_constraint(weight, pltpu.HBM) for weight in weights])


def place_kernel(me_ref, *refs, first):
    out_ref = refs[-1]
    pieces = refs[:-1]
    size = out_ref.shape[0] // len(pieces)
    for order, piece in enumerate(pieces):
        at = pl.multiple_of((me_ref[0] ^ order) * size, size)
        out_ref[pl.ds(at, size), :] = piece[pl.ds(first, size), :]


def place(pieces, me, first=0, size=None):
    size = size or pieces[0].shape[0]
    width = pieces[0].shape[1]
    count = len(pieces)
    return pl.pallas_call(
        functools.partial(place_kernel, first=first),
        out_shape=jax.ShapeDtypeStruct((count * size, width), pieces[0].dtype),
        in_specs=[SMEM_SPEC] + [VMEM_SPEC] * count,
        out_specs=VMEM_SPEC,
        compiler_params=pltpu.CompilerParams(vmem_limit_bytes=8 << 20),
        cost_estimate=lasting(2),
        name="place",
    )(me[None], *pieces)


def swap_kernel(me_ref, rows_ref, out_ref, *, count):
    size = rows_ref.shape[0] // count
    for order in range(count):
        at = pl.multiple_of((me_ref[0] ^ order) * size, size)
        out_ref[pl.ds(order * size, size), :] = rows_ref[pl.ds(at, size), :]


def swap_order(rows, me, count=4):
    return pl.pallas_call(
        functools.partial(swap_kernel, count=count),
        out_shape=jax.ShapeDtypeStruct(rows.shape, rows.dtype),
        in_specs=[SMEM_SPEC, VMEM_SPEC],
        out_specs=VMEM_SPEC,
        compiler_params=pltpu.CompilerParams(vmem_limit_bytes=4 << 20),
        cost_estimate=lasting(1),
        name="swap_order",
    )(me[None], rows)


def multiply_kernel(*refs, at, depth, transposed):
    count = (len(refs) - 1) // 2
    weights_ref = refs[0]
    width = refs[-1].shape[1]
    chunk = min(256, width)

    def one_chunk(index, _):
        start = pl.multiple_of(index * chunk, chunk)
        if transposed:
            weights = weights_ref[pl.ds(start, chunk), pl.ds(at, depth)]
        else:
            weights = weights_ref[:, pl.ds(at + start, chunk)]
        for rows_ref, out_ref in zip(refs[1 : 1 + count], refs[1 + count :]):
            product_of = nt_product if transposed else nn_product
            out_ref[:, pl.ds(start, chunk)] = product_of(rows_ref[:, pl.ds(0, depth)], weights).astype(out_ref.dtype)
        return 0

    lax.fori_loop(0, width // chunk, one_chunk, 0)


def multiply(pieces, weights, at, width, kinds=jnp.bfloat16, transposed=False, depth=None):
    kinds = kinds if isinstance(kinds, (list, tuple)) else [kinds] * len(pieces)
    return pl.pallas_call(
        functools.partial(multiply_kernel, at=at, depth=depth or pieces[0].shape[1], transposed=transposed),
        out_shape=[jax.ShapeDtypeStruct((piece.shape[0], width), kind) for piece, kind in zip(pieces, kinds)],
        in_specs=[VMEM_SPEC] * (1 + len(pieces)),
        out_specs=[VMEM_SPEC] * len(pieces),
        compiler_params=pltpu.CompilerParams(vmem_limit_bytes=16 << 20),
        cost_estimate=lasting(2),
        name="multiply",
    )(weights, *pieces)


def weights_kernel(*refs, groups, chunk):
    out_ref = refs[-1]
    features = out_ref.shape[0]

    def one_chunk(index, _):
        at = pl.multiple_of(index * chunk, chunk)
        operand = 0
        column = 0
        for terms, width in groups:
            total = None
            for _ in range(terms):
                left_ref, right_ref = refs[operand], refs[operand + 1]
                operand += 2
                term = lax.dot_general(
                    left_ref[:, pl.ds(at, chunk)],
                    right_ref[:, pl.ds(0, width)],
                    (((0,), (0,)), ((), ())),
                    preferred_element_type=jnp.float32,
                )
                total = term if total is None else total + term
            out_ref[pl.ds(at, chunk), pl.ds(column, width)] = total.astype(jnp.bfloat16)
            column += width
        return 0

    lax.fori_loop(0, features // chunk, one_chunk, 0)


def weight_grads(groups, width=None):
    operands = [array for group in groups for pair in group for array in pair]
    features = operands[0].shape[1]
    shapes = tuple((len(group), width or group[0][1].shape[1]) for group in groups)
    return pl.pallas_call(
        functools.partial(weights_kernel, groups=shapes, chunk=256),
        out_shape=jax.ShapeDtypeStruct((features, sum(wide for _, wide in shapes)), jnp.bfloat16),
        in_specs=[VMEM_SPEC] * len(operands),
        out_specs=VMEM_SPEC,
        compiler_params=pltpu.CompilerParams(vmem_limit_bytes=32 << 20),
        cost_estimate=lasting(16 if width else 8),
        name="weight_grads",
    )(*operands)


def feed_kernel(*refs, hidden, padded):
    weights_ref = refs[0]
    rows_refs, top_refs = refs[1:3], refs[3:5]
    hidden_refs, gate_refs, up_refs, back_refs = refs[5:7], refs[7:9], refs[9:11], refs[11:13]
    gate_ref, wide_ref, down_ref = refs[13:]
    features = weights_ref.shape[0]
    for order, target in enumerate((gate_ref, wide_ref, down_ref)):
        target[:, pl.ds(0, hidden)] = weights_ref[:, pl.ds(order * hidden, hidden)]
        if padded > hidden:
            target[:, pl.ds(hidden, padded - hidden)] = jnp.zeros((features, padded - hidden), jnp.bfloat16)

    def one_chunk(index, _):
        lanes = pl.ds(pl.multiple_of(index * 256, 256), 256)
        for piece in range(2):
            gate = nn_product(rows_refs[piece][...], gate_ref[:, lanes])
            up = nn_product(rows_refs[piece][...], wide_ref[:, lanes])
            hidden_grad = nn_product(top_refs[piece][...], down_ref[:, lanes])
            gelu_value, gelu_slope = gelu_parts(gate)
            hidden_refs[piece][:, lanes] = low(gelu_value * up)
            gate_refs[piece][:, lanes] = low(hidden_grad * up * gelu_slope)
            up_refs[piece][:, lanes] = low(hidden_grad * gelu_value)
        return 0

    lax.fori_loop(0, padded // 256, one_chunk, 0)

    def one_back(index, _):
        part = pl.ds(pl.multiple_of(index * 256, 256), 256)
        for piece in range(2):
            back = nt_product(gate_refs[piece][...], gate_ref[part, :]) + nt_product(up_refs[piece][...], wide_ref[part, :])
            back_refs[piece][:, part] = back.astype(back_refs[piece].dtype)
        return 0

    lax.fori_loop(0, features // 256, one_back, 0)


def feed(rows, top, weights, hidden):
    size, features = rows[0].shape
    padded = (hidden + 255) // 256 * 256
    kept = [jax.ShapeDtypeStruct((size, padded), jnp.bfloat16)] * 6
    back = [jax.ShapeDtypeStruct((size, features), kind) for kind in (jnp.float32, jnp.bfloat16)]
    outs = pl.pallas_call(
        functools.partial(feed_kernel, hidden=hidden, padded=padded),
        out_shape=kept + back,
        in_specs=[VMEM_SPEC] * 5,
        out_specs=[VMEM_SPEC] * 8,
        scratch_shapes=[pltpu.VMEM((features, padded), jnp.bfloat16)] * 3,
        compiler_params=pltpu.CompilerParams(vmem_limit_bytes=32 << 20),
        cost_estimate=lasting(12),
        name="feed",
    )(weights, *rows, *top)
    return outs[0:2], outs[2:4], outs[4:6], outs[6:8]


ROW_TILE = 64


def join_kernel(*refs, terms):
    stream_ref, gain_ref = refs[terms : terms + 2]
    joined_ref, normed_ref = refs[terms + 2 :]

    def one_tile(index, _):
        tile = pl.ds(pl.multiple_of(index * ROW_TILE, ROW_TILE), ROW_TILE)
        rows = stream_ref[tile, :].astype(jnp.float32)
        for ref in refs[:terms]:
            rows = rows + ref[tile, :].astype(jnp.float32)
        joined_ref[tile, :] = rows
        normed_ref[tile, :] = low(rows * norm_scale(rows) * gain_ref[...])
        return 0

    lax.fori_loop(0, stream_ref.shape[0] // ROW_TILE, one_tile, 0)


def join(terms, stream, gain):
    return pl.pallas_call(
        functools.partial(join_kernel, terms=len(terms)),
        out_shape=[jax.ShapeDtypeStruct(stream.shape, kind) for kind in (jnp.float32, jnp.bfloat16)],
        in_specs=[VMEM_SPEC] * (len(terms) + 2),
        out_specs=[VMEM_SPEC] * 2,
        compiler_params=pltpu.CompilerParams(vmem_limit_bytes=12 << 20),
        cost_estimate=lasting(4),
        name="join",
    )(*terms, stream, gain[None])


def join_back_kernel(*refs, terms):
    stream_ref, upper_ref, gain_ref = refs[terms : terms + 3]
    total_ref, rounded_ref, gain_grad_ref = refs[terms + 3 :]
    gain_grad_ref[...] = jnp.zeros_like(gain_grad_ref)

    def one_tile(index, _):
        tile = pl.ds(pl.multiple_of(index * ROW_TILE, ROW_TILE), ROW_TILE)
        grads = refs[0][tile, :].astype(jnp.float32)
        for ref in refs[1:terms]:
            grads = grads + ref[tile, :].astype(jnp.float32)
        rows = stream_ref[tile, :].astype(jnp.float32)
        scale = norm_scale(rows)
        scaled = grads * gain_ref[...]
        row_grad = scale * scaled - rows * (scale * scale * scale) * jnp.mean(scaled * rows, axis=-1, keepdims=True)
        total = upper_ref[tile, :].astype(jnp.float32) + row_grad
        total_ref[tile, :] = total
        rounded_ref[tile, :] = low(total)
        gain_grad_ref[...] += jnp.sum(grads * rows * scale, axis=0, keepdims=True)
        return 0

    lax.fori_loop(0, stream_ref.shape[0] // ROW_TILE, one_tile, 0)


def join_back(terms, stream, upper, gain):
    total, rounded, gain_grad = pl.pallas_call(
        functools.partial(join_back_kernel, terms=len(terms)),
        out_shape=[
            jax.ShapeDtypeStruct(stream.shape, jnp.float32),
            jax.ShapeDtypeStruct(stream.shape, jnp.bfloat16),
            jax.ShapeDtypeStruct((1, stream.shape[1]), jnp.float32),
        ],
        in_specs=[VMEM_SPEC] * (len(terms) + 3),
        out_specs=[VMEM_SPEC] * 3,
        compiler_params=pltpu.CompilerParams(vmem_limit_bytes=16 << 20),
        cost_estimate=lasting(5),
        name="join_back",
    )(*terms, stream, upper, gain[None])
    return total, rounded, gain_grad[0]


def exchange(rows, axis, size, bits):
    return lax.ppermute(rows, axis, [(i, i ^ bits) for i in range(size)])


def to_core(rows):
    return exchange(rows, "mp", PEERS, 1)


def across(rows):
    return exchange(rows, "mp", PEERS, 2)


def after(value, *others):
    return lax.optimization_barrier((value, *others))[0]


def gather_four(rows):
    far = across(rows)
    return rows, to_core(rows), far, to_core(far)


def prepare(own, other):
    return low(own + to_core(low(other)).astype(jnp.float32))


def sum_core(own, other):
    return own + to_core(low(other)).astype(jnp.float32)


def reduce_directly(grads, size):
    return lax.all_to_all(grads, "dp", split_axis=0, concat_axis=0, tiled=True)


def sum_parts(arrived, size):
    return jnp.sum(arrived.reshape(size, -1, arrived.shape[1]).astype(jnp.float32), axis=0)


def sum_everywhere(value, sizes):
    for axis in ("mp", "dp"):
        step = 1
        while step < sizes[axis]:
            value = value + exchange(value, axis, sizes[axis], step)
            step *= 2
    return value


def columns_of(array, widths):
    pieces = []
    at = 0
    for width in widths:
        pieces.append(array[:, at : at + width])
        at += width
    return pieces


def key_ranges(ids, key_ids, documents):
    numbers = jnp.arange(documents, dtype=jnp.int32)
    below = jnp.sum((key_ids[None, :] < numbers[:, None]).astype(jnp.int32), axis=1)
    upto = jnp.sum((key_ids[None, :] <= numbers[:, None]).astype(jnp.int32), axis=1)
    mine = (ids[None, :] == numbers[:, None]).astype(jnp.int32)
    return (jnp.sum(mine * below[:, None], axis=0), jnp.sum(mine * upto[:, None], axis=0))


def block_ranges(first, last, block, tall):
    return (first[::block] // tall, (last[block - 1 :: block] + tall - 1) // tall)


DOCUMENTS = 8
LONGEST = 768


def per_device(
    tokens,
    encoder_out,
    segments,
    encoder_segments,
    buckets,
    rel_table,
    gain_attend,
    gain_cross,
    gain_feed,
    self_query,
    self_key,
    self_value,
    self_output,
    cross_query,
    cross_key,
    cross_value,
    cross_output,
    w_gate,
    w_up,
    w_down,
    out_grad,
    *,
    sizes,
):
    parts = sizes["dp"]
    wide = self_query.shape[1]
    hidden_wide = w_gate.shape[1]
    heads = wide // DK
    block = 256
    own_rows = tokens.shape[0]
    me = lax.axis_index("mp")

    attend_shard = pack(
        [self_query, self_key, self_value, self_output, cross_query, cross_output, cross_key, cross_value],
        [False, False, False, True, False, True, False, False],
    )
    attend_all = lax.all_gather(attend_shard, "dp", axis=0, tiled=True)
    feed_shard = pack([w_gate, w_up, w_down], [False, False, True])
    feed_all = lax.all_gather(feed_shard, "dp", axis=0, tiled=True)
    to_cross = 4 * wide

    buckets_count = rel_table.shape[0]
    stream_zero = tokens.astype(jnp.float32)
    scale_zero = norm_scale(stream_zero)
    normed_zero = low(stream_zero * scale_zero * gain_attend)
    features = tokens.shape[1]
    encoder_rows = encoder_out.shape[0]
    ids = jnp.concatenate([segments, encoder_segments], axis=1)
    ids = jnp.pad(ids, ((0, 15), (0, features - ids.shape[1]))).astype(jnp.bfloat16)
    row_pieces = gather_four(jnp.concatenate([encoder_out, ids], axis=0))
    normed_one = list(gather_four(normed_zero))
    encoder_all = place(row_pieces, me, 0, encoder_rows)
    top = list(gather_four(after(out_grad, normed_one[2], row_pieces[2])))

    id_rows = jnp.concatenate([piece[encoder_rows:][:1] for piece in row_pieces], axis=0).astype(jnp.int32)
    near_ids = id_rows[:2, :own_rows].reshape(-1)
    ids = jnp.concatenate([lax.dynamic_slice_in_dim(id_rows, me ^ peer, 1, 0) for peer in range(PEERS)], axis=0)
    decoder_ids = ids[:, :own_rows].reshape(-1)
    encoder_ids = ids[:, own_rows : own_rows + encoder_rows].reshape(-1)
    length = decoder_ids.shape[0]
    self_first, unused = key_ranges(decoder_ids, decoder_ids, DOCUMENTS)
    self_last = jnp.arange(length, dtype=jnp.int32) + 1
    self_low, self_high = block_ranges(self_first, self_last, block, block)
    self_ranges = (self_low, self_high, self_first[None], self_last[None])
    cross_first, cross_last = key_ranges(near_ids, encoder_ids, DOCUMENTS)
    cross_low, cross_high = block_ranges(cross_first, cross_last, own_rows, block)
    cross_ranges = (cross_low, cross_high, cross_first[None], cross_last[None])

    offsets = min((LONGEST + block - 2) // block + 1, length // block)
    reach = offsets * block
    table_local = lax.dynamic_slice_in_dim(rel_table, me * heads, heads, 1)
    onehot = (buckets[None, :reach] == jnp.arange(buckets_count, dtype=jnp.int32)[:, None]).astype(jnp.float32)
    series = lax.dot_general(table_local, onehot, (((0,), (0,)), ((), ())), precision=lax.Precision.HIGHEST)
    bias = bias_tiles(jnp.pad(series, ((0, 0), (block, 0))), offsets, block)

    wider = [jnp.float32, jnp.bfloat16]
    qkv = multiply(normed_one, after(attend_all, top[2], top[3], feed_shard), 0, 3 * wide)
    *context_one, context_one_t, totals_one = attend_forward(self_ranges, me, qkv, None, bias, heads, block, block)
    cross_other = across(attend_all[:, to_cross : to_cross + 2 * wide])
    context_one[2] = after(context_one[2], cross_other)
    terms = multiply(context_one[2:], attend_all, 3 * wide, features, wider, True)
    far_ready = prepare(*terms)
    far_sum = across(far_ready)
    keys_values = multiply([encoder_all], attend_all, to_cross + 2 * wide, 2 * wide)[0]
    keys_values_two = [keys_values, across(keys_values)]
    terms = multiply([after(context_one[0], far_ready), context_one[1]], attend_all, 3 * wide, features, wider, True)
    far_sum = after(far_sum, terms[0], keys_values_two[1])
    stream_one, normed_own = join([terms[0], to_core(terms[1]), far_sum], tokens, gain_cross)

    cross_weights = [(attend_all, to_cross), (cross_other, 0)]
    normed_two = [normed_own, to_core(normed_own)]
    still = jnp.zeros_like(me)
    queries_two, contexts_two, backs_two = [], [], []
    for (weights, at), keys_values in zip(cross_weights, keys_values_two):
        queries_two.append(multiply(normed_two, weights, at, wide))
        *context, context_t, totals = attend_forward(
            cross_ranges, still, queries_two[-1], keys_values, None, heads, own_rows, block
        )
        contexts_two.append(context)
        backs_two.append((context_t, totals))
    terms = [
        multiply(context, weights, at + wide, features, wider, True)
        for context, (weights, at) in zip(contexts_two, cross_weights)
    ]
    stream_two, normed_own = join(
        [terms[0][0], terms[1][0], to_core(terms[0][1] + terms[1][1])], stream_one, gain_feed
    )

    normed_three = [normed_own, to_core(normed_own)]
    hidden_near, gate_grad_near, up_grad_near, back_near = feed(normed_three, top[:2], feed_all, hidden_wide)
    far_own = after(across(normed_own), *hidden_near, *gate_grad_near, *up_grad_near, *back_near)
    normed_three += [far_own, to_core(far_own)]
    hidden_far, gate_grad_far, up_grad_far, back_far = feed(normed_three[2:], top[2:], feed_all, hidden_wide)
    far_ready = prepare(*back_far)
    far_sum = across(far_ready)
    top[3] = after(top[3], far_ready)
    hidden = hidden_near + hidden_far
    feed_grads = weight_grads(
        [
            list(zip(normed_three, gate_grad_near + gate_grad_far)),
            list(zip(normed_three, up_grad_near + up_grad_far)),
            list(zip(top, hidden)),
        ],
        hidden_wide,
    )
    far_sum = after(far_sum, feed_grads)
    feed_sums = lax.psum_scatter(feed_grads, "dp", scatter_dimension=0, tiled=True)
    stream_grad, grad_own, feed_gain_grad = join_back(
        [back_near[0], to_core(back_near[1]), far_sum], stream_two, out_grad, gain_feed
    )

    grad_two = [grad_own, to_core(grad_own)]
    query_grads, key_value_grads, backs = [], [], []
    for (weights, at), queries, keys_values, back in zip(cross_weights, queries_two, keys_values_two, backs_two):
        context_grad = multiply(grad_two, weights, at + wide, wide)
        *query_grad, key_value_grad = attend_backward(
            cross_ranges, still, queries, keys_values, context_grad, *back, None, heads, own_rows, block
        )
        query_grads.append(query_grad)
        key_value_grads.append(key_value_grad)
        backs.append(multiply(query_grad, weights, at, features, wider, True))
    key_value_far = across(key_value_grads[1])
    stream_grad, grad_own, cross_gain_grad = join_back(
        [backs[0][0], backs[1][0], to_core(backs[0][1] + backs[1][1])], stream_one, stream_grad, gain_cross
    )

    grad_peer = to_core(grad_own)
    context_grad = multiply([grad_own, grad_peer], attend_all, 3 * wide, wide)
    key_value_grad = low(key_value_grads[0].astype(jnp.float32) + key_value_far.astype(jnp.float32))
    cross_grads = [
        weight_grads([list(zip(normed_two, query_grad)), list(zip([grad_two[0], after(grad_two[1], grad_own)], context))])
        for query_grad, context in zip(query_grads, contexts_two)
    ]
    cross_far = across(cross_grads[1])
    key_value_weights = weight_grads([[(encoder_all, after(key_value_grad, grad_own))]])
    layer_terms = multiply(hidden_far, feed_all, 2 * hidden_wide, features, wider, True, hidden_wide)
    layer_ready = prepare(*layer_terms)
    encoder_terms = multiply(
        [after(swap_order(key_value_grad, me), grad_own)], attend_all, to_cross + 2 * wide, features, jnp.float32, True
    )[0]
    encoder_terms = [encoder_terms[at : at + encoder_rows] for at in range(0, PEERS * encoder_rows, encoder_rows)]
    encoder_ready = prepare(encoder_terms[2], encoder_terms[3])
    grad_far = after(across(grad_own), *context_grad, *cross_grads, key_value_weights, layer_ready, encoder_ready)
    grad_one = [grad_own, grad_peer, grad_far, to_core(grad_far)]
    context_grad = context_grad + multiply(grad_one[2:], attend_all, 3 * wide, wide)
    *qkv_grad, diagonals = attend_backward(
        self_ranges, me, qkv, None, context_grad, context_one_t, totals_one, bias, heads, block, block
    )
    self_grads = weight_grads([list(zip(normed_one, qkv_grad)), list(zip(grad_one, context_one))])
    self_parts = lax.psum_scatter(self_grads, "dp", scatter_dimension=0, tiled=True)
    qkv_grad[2] = after(qkv_grad[2], self_grads, feed_sums)
    terms = multiply(qkv_grad[2:], attend_all, 0, features, wider, True)
    far_ready = prepare(*terms)
    far_sum = across(far_ready)
    cross_far = after(cross_far, self_grads)
    cross_parts = reduce_directly(
        jnp.concatenate([low(cross_grads[0].astype(jnp.float32) + cross_far.astype(jnp.float32)), key_value_weights], axis=1),
        parts,
    )
    terms = multiply(qkv_grad[:2], attend_all, 0, features, wider, True)
    tokens_grad, unused, attend_gain_grad = join_back(
        [terms[0], to_core(terms[1]), far_sum], tokens, stream_grad, gain_attend
    )

    diagonals = diagonal_sums(after(diagonals, far_ready))
    ahead = jnp.moveaxis(diagonals[:, :, :block], 0, 1).reshape(heads, reach)
    behind = jnp.moveaxis(diagonals[1:, :, block:], 0, 1).reshape(heads, reach - block)
    series_grad = ahead + jnp.pad(behind, ((0, 0), (0, block)))
    table_grad = lax.dot_general(onehot, series_grad, (((1,), (1,)), ((), ())), precision=lax.Precision.HIGHEST)
    table_full = lax.dynamic_update_slice(jnp.zeros(rel_table.shape, jnp.float32), table_grad, (0, me * heads))
    small = jnp.concatenate([attend_gain_grad, cross_gain_grad, feed_gain_grad, table_full.reshape(-1)])
    small = sum_everywhere(small.reshape(-1, 128), sizes).reshape(-1)
    layer_far, encoder_far = across(after(layer_ready, far_sum)), across(after(encoder_ready, far_sum))
    small, layer_far, encoder_far, self_parts, cross_parts = lax.optimization_barrier(
        (small, layer_far, encoder_far, self_parts, cross_parts)
    )
    layer_terms = multiply(hidden_near, feed_all, 2 * hidden_wide, features, wider, True, hidden_wide)
    layer_out = low(stream_two + sum_core(*layer_terms) + layer_far.astype(jnp.float32))
    encoder_grad = sum_core(encoder_terms[0], encoder_terms[1]) + encoder_far.astype(jnp.float32)

    attend_gain_sum, cross_gain_sum, feed_gain_sum = (
        small[:features],
        small[features : 2 * features],
        small[2 * features : 3 * features],
    )
    table_sum = small[3 * features :].reshape(rel_table.shape)
    self_sums = self_parts.astype(jnp.float32)
    cross_sums = sum_parts(cross_parts, parts)
    feed_sums = feed_sums.astype(jnp.float32)
    query_one_sum, key_one_sum, value_one_sum, output_one_sum = columns_of(self_sums, [wide] * 4)
    query_two_sum, output_two_sum, key_two_sum, value_two_sum = columns_of(cross_sums, [wide] * 4)
    gate_sum, up_sum, down_sum = columns_of(feed_sums, [hidden_wide] * 3)
    return (
        layer_out,
        tokens_grad,
        encoder_grad,
        table_sum,
        attend_gain_sum,
        cross_gain_sum,
        feed_gain_sum,
        query_one_sum,
        key_one_sum,
        value_one_sum,
        output_one_sum.T,
        query_two_sum,
        key_two_sum,
        value_two_sum,
        output_two_sum.T,
        gate_sum,
        up_sum,
        down_sum.T,
    )


def solution(mesh):
    in_specs = (
        P(("dp", "mp"), None),
        P(("dp", "mp"), None),
        P("dp", "mp"),
        P("dp", "mp"),
        P(),
        P(),
        P(),
        P(),
        P(),
        P("dp", "mp"),
        P("dp", "mp"),
        P("dp", "mp"),
        P("mp", "dp"),
        P("dp", "mp"),
        P("dp", "mp"),
        P("dp", "mp"),
        P("mp", "dp"),
        P("dp", "mp"),
        P("dp", "mp"),
        P("mp", "dp"),
        P(("dp", "mp"), None),
    )
    out_specs = (
        P(("dp", "mp"), None),
        P(("dp", "mp"), None),
        P(("dp", "mp"), None),
        P(),
        P(),
        P(),
        P(),
        P("dp", "mp"),
        P("dp", "mp"),
        P("dp", "mp"),
        P("mp", "dp"),
        P("dp", "mp"),
        P("dp", "mp"),
        P("dp", "mp"),
        P("mp", "dp"),
        P("dp", "mp"),
        P("dp", "mp"),
        P("mp", "dp"),
    )
    return jax.shard_map(
        functools.partial(per_device, sizes=dict(mesh.shape)), mesh=mesh, in_specs=in_specs, out_specs=out_specs, check_vma=False
    )
```

```python
import functools
import jax
import jax.numpy as jnp
from jax import lax
from jax.experimental import pallas as pl
from jax.experimental.pallas import tpu as pltpu
from jax.sharding import PartitionSpec as P

DK = 64
PAIR = 2 * DK
NEG = -1e30
PEERS = 4

norm_eps = 1e-06
gelu_factor = 0.7978845608028654


def product(left, right):
    return jnp.dot(left, right, preferred_element_type=jnp.float32)


def rows_product(left, right):
    return lax.dot_general(left, right, (((0,), (0,)), ((), ())), preferred_element_type=jnp.float32)


def columns_product(left, right):
    return lax.dot_general(left, right, (((1,), (1,)), ((), ())), preferred_element_type=jnp.float32)


def norm_scale(rows):
    return lax.rsqrt(jnp.mean(rows * rows, axis=-1, keepdims=True) + norm_eps)


def gelu_parts(value):
    cubic = 0.044715 * value * value * value
    tangent = jnp.tanh(gelu_factor * (value + cubic))
    result = 0.5 * value * (1.0 + tangent)
    slope = 0.5 * (1.0 + tangent) + 0.5 * value * (1.0 - tangent * tangent) * gelu_factor * (
        1.0 + 3.0 * 0.044715 * value * value
    )
    return (result, slope)


def norm_back(grads, rows, scale, gain):
    scaled = grads * gain
    row_grad = scale * scaled - rows * (scale * scale * scale) * jnp.mean(scaled * rows, axis=-1, keepdims=True)
    gain_grad = jnp.sum(grads * rows * scale, axis=0)
    return (row_grad, gain_grad)


def low(value):
    return value.astype(jnp.bfloat16)


def nt_product(left, right):
    return lax.dot_general(left, right, (((1,), (1,)), ((), ())), preferred_element_type=jnp.float32)


def nn_product(left, right):
    return jnp.dot(left, right, preferred_element_type=jnp.float32)


def own_lanes(rows, head):
    lane = lax.broadcasted_iota(jnp.int32, rows.shape, 1)
    mine = (lane < DK) if head % 2 == 0 else (lane >= DK)
    return jnp.where(mine, rows, jnp.zeros_like(rows))


def bias_kernel(series_ref, tiles_ref, *, block):
    heads = series_ref.shape[0]
    for offset in range(tiles_ref.shape[0]):
        for head in range(heads):
            low = series_ref[pl.ds(head, 1), pl.ds(offset * block, block)]
            high = series_ref[pl.ds(head, 1), pl.ds((offset + 1) * block, block)]
            base = jnp.broadcast_to(jnp.concatenate([high, low], axis=1), (block, 2 * block))
            rolled = pltpu.roll(base, 0, 1, stride=1, stride_axis=0)
            tiles_ref[offset, head] = rolled[:, :block]


def bias_tiles(series, offsets, block):
    heads = series.shape[0]
    return pl.pallas_call(
        functools.partial(bias_kernel, block=block),
        out_shape=jax.ShapeDtypeStruct((offsets, heads, block, block), jnp.float32),
        compiler_params=pltpu.CompilerParams(vmem_limit_bytes=16 << 20),
        cost_estimate=lasting(4),
        name="bias_tiles",
    )(series)


def load_order(me, pieces, target_ref):
    size = pieces[0].shape[0]
    for order, piece in enumerate(pieces):
        at = pl.multiple_of((me ^ order) * size, size)
        target_ref[pl.ds(at, size), :] = piece[...]


def store_order(me, source_ref, pieces):
    size = pieces[0].shape[0]
    for order, piece in enumerate(pieces):
        at = pl.multiple_of((me ^ order) * size, size)
        piece[...] = source_ref[pl.ds(at, size), :].astype(jnp.bfloat16)


def forward_kernel(*refs, heads, block, tall, biased, at_key, at_value, pieces):
    low_ref, high_ref, me_ref, first_ref, last_ref, extra_ref = refs[:6]
    piece_refs = refs[6 : 6 + pieces]
    ctx_refs = refs[6 + pieces : 6 + 2 * pieces]
    ot_ref, lse_ref, acc_ref, vt_ref, q_ref, ctx_ref = refs[6 + 2 * pieces :]
    if biased:
        bias_ref, kv_ref = extra_ref, q_ref
    else:
        kv_ref = extra_ref
    load_order(me_ref[0], piece_refs, q_ref)
    rows = q_ref.shape[0]
    width = heads * DK
    key_iota = lax.broadcasted_iota(jnp.int32, (tall, block), 0)
    for tile in range(kv_ref.shape[0] // tall):
        vt_ref[:, pl.ds(tile * tall, tall)] = jnp.transpose(kv_ref[pl.ds(tile * tall, tall), pl.ds(at_value, width)])

    def one_block(index, _):
        start = pl.multiple_of(index * block, block)
        first = first_ref[:, pl.ds(start, block)]
        last = last_ref[:, pl.ds(start, block)]
        queries = [
            own_lanes(q_ref[pl.ds(start, block), pl.ds((head // 2) * PAIR, PAIR)], head) for head in range(heads)
        ]
        acc_ref[...] = jnp.zeros_like(acc_ref)

        def one_tile(tile, carry):
            at = pl.multiple_of(tile * tall, tall)
            valid = (key_iota >= first - at) & (key_iota < last - at)
            scores = []
            for head in range(heads):
                keys = kv_ref[pl.ds(at, tall), pl.ds(at_key + (head // 2) * PAIR, PAIR)]
                score = nt_product(keys, queries[head])
                if biased:
                    score = score + bias_ref[index - tile, head]
                scores.append(jnp.where(valid, score, NEG))
            results = []
            raised = []
            shrinks = []
            for head in range(heads):
                top, total = carry[head]
                new_top = jnp.maximum(top, jnp.max(scores[head], axis=0, keepdims=True))
                power = jnp.exp(scores[head] - new_top)
                shrink = jnp.exp(top - new_top)
                results.append((new_top, shrink * total + jnp.sum(power, axis=0, keepdims=True)))
                raised.append(power.astype(jnp.bfloat16))
                shrinks.append(shrink)
            for head in range(heads):
                mine = pl.ds(head * DK, DK)
                acc_ref[mine, :] = acc_ref[mine, :] * shrinks[head] + nn_product(
                    vt_ref[mine, pl.ds(at, tall)], raised[head]
                )
            return tuple(results)

        empty = tuple(
            (jnp.full((1, block), NEG, jnp.float32), jnp.zeros((1, block), jnp.float32)) for _ in range(heads)
        )
        stats = lax.fori_loop(low_ref[index], high_ref[index], one_tile, empty)
        for head in range(heads):
            top, total = stats[head]
            mine = pl.ds(head * DK, DK)
            acc_ref[mine, :] = acc_ref[mine, :] / total
            lse_ref[pl.ds(head, 1), pl.ds(start, block)] = top + jnp.log(total)
        ot_ref[:, pl.ds(start, block)] = acc_ref[...]
        ctx_ref[pl.ds(start, block), :] = jnp.transpose(acc_ref[...])
        return 0

    lax.fori_loop(0, rows // block, one_block, 0)
    store_order(me_ref[0], ctx_ref, ctx_refs)


def lasting(micros):
    return pl.CostEstimate(flops=int(micros * 1.1e9), bytes_accessed=1 << 10, transcendentals=0)


SMEM_SPEC = pl.BlockSpec(memory_space=pltpu.SMEM)
VMEM_SPEC = pl.BlockSpec(memory_space=pltpu.VMEM)


def attend_forward(ranges, me, queries, keys_values, bias, heads, block, tall):
    low_block, high_block, first, last = ranges
    pieces = len(queries)
    size, depth = queries[0].shape
    rows = pieces * size
    width = heads * DK
    biased = bias is not None
    at_key = width if biased else 0
    key_rows = rows if biased else keys_values.shape[0]
    operands = [low_block, high_block, me[None], first, last, bias if biased else keys_values, *queries]
    return pl.pallas_call(
        functools.partial(
            forward_kernel,
            heads=heads,
            block=block,
            tall=tall,
            biased=biased,
            at_key=at_key,
            at_value=at_key + width,
            pieces=pieces,
        ),
        out_shape=(
            *([jax.ShapeDtypeStruct((size, width), jnp.bfloat16)] * pieces),
            jax.ShapeDtypeStruct((width, rows), jnp.float32),
            jax.ShapeDtypeStruct((heads, rows), jnp.float32),
        ),
        in_specs=[SMEM_SPEC] * 3 + [VMEM_SPEC] * (len(operands) - 3),
        out_specs=(VMEM_SPEC,) * (pieces + 2),
        scratch_shapes=[
            pltpu.VMEM((width, block), jnp.float32),
            pltpu.VMEM((width, key_rows), jnp.bfloat16),
            pltpu.VMEM((rows, depth), jnp.bfloat16),
            pltpu.VMEM((rows, width), jnp.float32),
        ],
        compiler_params=pltpu.CompilerParams(vmem_limit_bytes=24 << 20),
        cost_estimate=lasting(14 if biased else 1),
        name="attend_forward",
    )(*operands)


def backward_kernel(*refs, heads, block, tall, biased, at_key, at_value, pieces):
    low_ref, high_ref, me_ref, ot_ref, lse_ref, first_ref, last_ref, extra_ref = refs[:8]
    piece_refs = refs[8 : 8 + pieces]
    g_refs = refs[8 + pieces : 8 + 2 * pieces]
    out_refs = refs[8 + 2 * pieces : 8 + 3 * pieces]
    refs = refs[8 + 3 * pieces :]
    if biased:
        diag_ref, dqt_ref, kt_ref, dka_ref, dva_ref, q_ref, g_ref, dq_ref = refs
        bias_ref = extra_ref
        kv_ref, dkv_ref = q_ref, dq_ref
    else:
        dkv_ref, dqt_ref, kt_ref, dka_ref, dva_ref, q_ref, g_ref, dq_ref = refs
        kv_ref = extra_ref
    load_order(me_ref[0], piece_refs, q_ref)
    load_order(me_ref[0], g_refs, g_ref)
    rows = q_ref.shape[0]
    width = heads * DK
    key_iota = lax.broadcasted_iota(jnp.int32, (tall, block), 0)
    for tile in range(kv_ref.shape[0] // tall):
        kt_ref[:, pl.ds(tile * tall, tall)] = jnp.transpose(kv_ref[pl.ds(tile * tall, tall), pl.ds(at_key, width)])
    dka_ref[...] = jnp.zeros_like(dka_ref)
    dva_ref[...] = jnp.zeros_like(dva_ref)
    if biased:
        diag_ref[...] = jnp.zeros_like(diag_ref)

    def one_block(index, _):
        start = pl.multiple_of(index * block, block)
        first = first_ref[:, pl.ds(start, block)]
        last = last_ref[:, pl.ds(start, block)]
        pairs = [pl.ds(pair * PAIR, PAIR) for pair in range(heads // 2)]
        queries = [own_lanes(q_ref[pl.ds(start, block), pairs[head // 2]], head) for head in range(heads)]
        grads = [own_lanes(g_ref[pl.ds(start, block), pairs[head // 2]], head) for head in range(heads)]
        shared = jnp.transpose(g_ref[pl.ds(start, block), :].astype(jnp.float32)) * ot_ref[:, pl.ds(start, block)]
        deltas = [jnp.sum(shared[head * DK : (head + 1) * DK], axis=0, keepdims=True) for head in range(heads)]
        totals = [lse_ref[pl.ds(head, 1), pl.ds(start, block)] for head in range(heads)]
        dqt_ref[...] = jnp.zeros_like(dqt_ref)

        def one_tile(tile, carry):
            at = pl.multiple_of(tile * tall, tall)
            valid = (key_iota >= first - at) & (key_iota < last - at)
            shares, score_grads = [], []
            for head in range(heads):
                pair = head // 2
                keys = kv_ref[pl.ds(at, tall), pl.ds(at_key + pair * PAIR, PAIR)]
                values = kv_ref[pl.ds(at, tall), pl.ds(at_value + pair * PAIR, PAIR)]
                scores = nt_product(keys, queries[head])
                share_grad = nt_product(values, grads[head])
                if biased:
                    scores = scores + bias_ref[index - tile, head]
                share = jnp.exp(jnp.where(valid, scores - totals[head], NEG))
                score_grad = (share * (share_grad - deltas[head])).astype(jnp.bfloat16)
                if biased:
                    diag_ref[index - tile, head] += score_grad.astype(jnp.float32)
                shares.append(share.astype(jnp.bfloat16))
                score_grads.append(score_grad)
            for pair in range(heads // 2):
                lanes = pl.ds(pair * PAIR, PAIR)
                one, two = 2 * pair, 2 * pair + 1
                dva_ref[pl.ds(at, tall), lanes] += nn_product(shares[one], grads[one]) + nn_product(shares[two], grads[two])
                dka_ref[pl.ds(at, tall), lanes] += nn_product(score_grads[one], queries[one]) + nn_product(
                    score_grads[two], queries[two]
                )
            for head in range(heads):
                mine = pl.ds(head * DK, DK)
                dqt_ref[mine, :] += nn_product(kt_ref[mine, pl.ds(at, tall)], score_grads[head])
            return carry

        lax.fori_loop(low_ref[index], high_ref[index], one_tile, 0)
        dq_ref[pl.ds(start, block), pl.ds(0, width)] = jnp.transpose(dqt_ref[...]).astype(jnp.bfloat16)
        return 0

    lax.fori_loop(0, rows // block, one_block, 0)
    dkv_ref[:, pl.ds(at_key, width)] = dka_ref[...].astype(jnp.bfloat16)
    dkv_ref[:, pl.ds(at_value, width)] = dva_ref[...].astype(jnp.bfloat16)
    store_order(me_ref[0], dq_ref, out_refs)


def diagonals_kernel(diag_ref, series_ref):
    offsets, heads, block, _ = diag_ref.shape

    def one_diagonal(index, _):
        offset, head = index >> (heads.bit_length() - 1), index & (heads - 1)
        slab = jnp.zeros((8, 2 * block), jnp.float32)
        for group in range(block // 8):
            piece = diag_ref[offset, head, pl.ds(8 * group, 8), :]
            wide = jnp.concatenate([piece, jnp.zeros_like(piece)], axis=1)
            slab = slab + (pltpu.roll(wide, 2 * block - 8 * group, 1) if group else wide)
        line = slab[0:1]
        for row in range(1, 8):
            line = line + pltpu.roll(slab[row : row + 1], 2 * block - row, 1)
        series_ref[offset, pl.ds(head, 1), :] = line
        return 0

    lax.fori_loop(0, offsets * heads, one_diagonal, 0)


def diagonal_sums(diagonals):
    offsets, heads, block, _ = diagonals.shape
    return pl.pallas_call(
        diagonals_kernel,
        out_shape=jax.ShapeDtypeStruct((offsets, heads, 2 * block), jnp.float32),
        in_specs=[VMEM_SPEC],
        out_specs=VMEM_SPEC,
        compiler_params=pltpu.CompilerParams(vmem_limit_bytes=8 << 20),
        cost_estimate=lasting(4),
        name="diagonal_sums",
    )(diagonals)


def attend_backward(ranges, me, queries, keys_values, grads, context_t, totals, bias, heads, block, tall):
    low_block, high_block, first, last = ranges
    pieces = len(queries)
    size, depth = queries[0].shape
    rows = pieces * size
    width = heads * DK
    biased = bias is not None
    at_key = width if biased else 0
    key_rows = rows if biased else keys_values.shape[0]
    operands = [low_block, high_block, me[None], context_t, totals, first, last, bias if biased else keys_values]
    operands += [*queries, *grads]
    shapes = [jax.ShapeDtypeStruct((size, depth), jnp.bfloat16)] * pieces
    scratch = [
        pltpu.VMEM((width, block), jnp.float32),
        pltpu.VMEM((width, key_rows), jnp.bfloat16),
        pltpu.VMEM((key_rows, width), jnp.float32),
        pltpu.VMEM((key_rows, width), jnp.float32),
        pltpu.VMEM((rows, depth), jnp.bfloat16),
        pltpu.VMEM((rows, width), jnp.bfloat16),
        pltpu.VMEM((rows, depth), jnp.bfloat16),
    ]
    if biased:
        shapes.append(jax.ShapeDtypeStruct(bias.shape, jnp.float32))
    else:
        shapes.append(jax.ShapeDtypeStruct((key_rows, 2 * width), jnp.bfloat16))
    return pl.pallas_call(
        functools.partial(
            backward_kernel,
            heads=heads,
            block=block,
            tall=tall,
            biased=biased,
            at_key=at_key,
            at_value=at_key + width,
            pieces=pieces,
        ),
        out_shape=tuple(shapes),
        in_specs=[SMEM_SPEC] * 3 + [VMEM_SPEC] * (len(operands) - 3),
        out_specs=(VMEM_SPEC,) * len(shapes),
        scratch_shapes=scratch,
        compiler_params=pltpu.CompilerParams(vmem_limit_bytes=36 << 20),
        cost_estimate=lasting(4),
        name="attend_backward",
    )(*operands)


def pack_kernel(*refs, turned):
    count = len(turned)
    out_ref, semaphores = refs[count], refs[-1]
    held = refs[count + 1 : -1]
    copies = [
        pltpu.make_async_copy(source, target, semaphores.at[order])
        for order, (source, target) in enumerate(zip(refs[:count], held))
    ]
    for copy in copies:
        copy.start()
    at = 0
    for copy, ref, turn in zip(copies, held, turned):
        copy.wait()
        piece = jnp.transpose(ref[...]) if turn else ref[...]
        out_ref[:, pl.ds(at, piece.shape[1])] = low(piece)
        at += piece.shape[1]


def pack(weights, turned):
    width = sum(weight.shape[0] if turn else weight.shape[1] for weight, turn in zip(weights, turned))
    rows = weights[0].shape[0]
    return pl.pallas_call(
        functools.partial(pack_kernel, turned=tuple(turned)),
        out_shape=jax.ShapeDtypeStruct((rows, width), jnp.bfloat16),
        in_specs=[pl.BlockSpec(memory_space=pltpu.HBM)] * len(weights),
        out_specs=VMEM_SPEC,
        scratch_shapes=[pltpu.VMEM(weight.shape, jnp.float32) for weight in weights]
        + [pltpu.SemaphoreType.DMA((len(weights),))],
        compiler_params=pltpu.CompilerParams(vmem_limit_bytes=12 << 20),
        cost_estimate=lasting(2),
        name="pack",
    )(*[pltpu.with_memory_space_constraint(weight, pltpu.HBM) for weight in weights])


def unpack_kernel(rows_ref, *refs, turned):
    at = 0
    for ref, turn in zip(refs, turned):
        width = ref.shape[0] if turn else ref.shape[1]
        piece = rows_ref[:, pl.ds(at, width)].astype(jnp.float32)
        ref[...] = jnp.transpose(piece) if turn else piece
        at += width


def unpack(rows, widths, turned):
    shapes = [(width, rows.shape[0]) if turn else (rows.shape[0], width) for width, turn in zip(widths, turned)]
    return pl.pallas_call(
        functools.partial(unpack_kernel, turned=tuple(turned)),
        out_shape=[jax.ShapeDtypeStruct(shape, jnp.float32) for shape in shapes],
        in_specs=[VMEM_SPEC],
        out_specs=[VMEM_SPEC] * len(widths),
        compiler_params=pltpu.CompilerParams(vmem_limit_bytes=8 << 20),
        cost_estimate=lasting(9),
        name="unpack",
    )(rows)


def place_kernel(me_ref, *refs, first):
    out_ref = refs[-1]
    pieces = refs[:-1]
    size = out_ref.shape[0] // len(pieces)
    for order, piece in enumerate(pieces):
        at = pl.multiple_of((me_ref[0] ^ order) * size, size)
        out_ref[pl.ds(at, size), :] = piece[pl.ds(first, size), :]


def place(pieces, me, first=0, size=None):
    size = size or pieces[0].shape[0]
    width = pieces[0].shape[1]
    count = len(pieces)
    return pl.pallas_call(
        functools.partial(place_kernel, first=first),
        out_shape=jax.ShapeDtypeStruct((count * size, width), pieces[0].dtype),
        in_specs=[SMEM_SPEC] + [VMEM_SPEC] * count,
        out_specs=VMEM_SPEC,
        compiler_params=pltpu.CompilerParams(vmem_limit_bytes=8 << 20),
        cost_estimate=lasting(2),
        name="place",
    )(me[None], *pieces)


def swap_kernel(me_ref, rows_ref, out_ref, *, count):
    size = rows_ref.shape[0] // count
    for order in range(count):
        at = pl.multiple_of((me_ref[0] ^ order) * size, size)
        out_ref[pl.ds(order * size, size), :] = rows_ref[pl.ds(at, size), :]


def swap_order(rows, me, count=4):
    return pl.pallas_call(
        functools.partial(swap_kernel, count=count),
        out_shape=jax.ShapeDtypeStruct(rows.shape, rows.dtype),
        in_specs=[SMEM_SPEC, VMEM_SPEC],
        out_specs=VMEM_SPEC,
        compiler_params=pltpu.CompilerParams(vmem_limit_bytes=4 << 20),
        cost_estimate=lasting(1),
        name="swap_order",
    )(me[None], rows)


def multiply_kernel(*refs, at, depth, transposed):
    count = (len(refs) - 1) // 2
    weights_ref = refs[0]
    width = refs[-1].shape[1]
    chunk = min(256, width)

    def one_chunk(index, _):
        start = pl.multiple_of(index * chunk, chunk)
        if transposed:
            weights = weights_ref[pl.ds(start, chunk), pl.ds(at, depth)]
        else:
            weights = weights_ref[:, pl.ds(at + start, chunk)]
        for rows_ref, out_ref in zip(refs[1 : 1 + count], refs[1 + count :]):
            product_of = nt_product if transposed else nn_product
            out_ref[:, pl.ds(start, chunk)] = product_of(rows_ref[:, pl.ds(0, depth)], weights).astype(out_ref.dtype)
        return 0

    lax.fori_loop(0, width // chunk, one_chunk, 0)


def multiply(pieces, weights, at, width, kinds=jnp.bfloat16, transposed=False, depth=None):
    kinds = kinds if isinstance(kinds, (list, tuple)) else [kinds] * len(pieces)
    return pl.pallas_call(
        functools.partial(multiply_kernel, at=at, depth=depth or pieces[0].shape[1], transposed=transposed),
        out_shape=[jax.ShapeDtypeStruct((piece.shape[0], width), kind) for piece, kind in zip(pieces, kinds)],
        in_specs=[VMEM_SPEC] * (1 + len(pieces)),
        out_specs=[VMEM_SPEC] * len(pieces),
        compiler_params=pltpu.CompilerParams(vmem_limit_bytes=16 << 20),
        cost_estimate=lasting(2),
        name="multiply",
    )(weights, *pieces)


def weights_kernel(*refs, groups, chunk):
    out_ref = refs[-1]
    features = out_ref.shape[0]

    def one_chunk(index, _):
        at = pl.multiple_of(index * chunk, chunk)
        operand = 0
        column = 0
        for terms, width in groups:
            total = None
            for _ in range(terms):
                left_ref, right_ref = refs[operand], refs[operand + 1]
                operand += 2
                term = lax.dot_general(
                    left_ref[:, pl.ds(at, chunk)],
                    right_ref[:, pl.ds(0, width)],
                    (((0,), (0,)), ((), ())),
                    preferred_element_type=jnp.float32,
                )
                total = term if total is None else total + term
            out_ref[pl.ds(at, chunk), pl.ds(column, width)] = total.astype(jnp.bfloat16)
            column += width
        return 0

    lax.fori_loop(0, features // chunk, one_chunk, 0)


def weight_grads(groups, width=None):
    operands = [array for group in groups for pair in group for array in pair]
    features = operands[0].shape[1]
    shapes = tuple((len(group), width or group[0][1].shape[1]) for group in groups)
    return pl.pallas_call(
        functools.partial(weights_kernel, groups=shapes, chunk=256),
        out_shape=jax.ShapeDtypeStruct((features, sum(wide for _, wide in shapes)), jnp.bfloat16),
        in_specs=[VMEM_SPEC] * len(operands),
        out_specs=VMEM_SPEC,
        compiler_params=pltpu.CompilerParams(vmem_limit_bytes=32 << 20),
        cost_estimate=lasting(16 if width else 8),
        name="weight_grads",
    )(*operands)


def feed_kernel(*refs, hidden, padded):
    weights_ref = refs[0]
    rows_refs, top_refs = refs[1:3], refs[3:5]
    hidden_refs, gate_refs, up_refs, back_refs = refs[5:7], refs[7:9], refs[9:11], refs[11:13]
    gate_ref, wide_ref, down_ref = refs[13:]
    features = weights_ref.shape[0]
    for order, target in enumerate((gate_ref, wide_ref, down_ref)):
        target[:, pl.ds(0, hidden)] = weights_ref[:, pl.ds(order * hidden, hidden)]
        if padded > hidden:
            target[:, pl.ds(hidden, padded - hidden)] = jnp.zeros((features, padded - hidden), jnp.bfloat16)

    def one_chunk(index, _):
        lanes = pl.ds(pl.multiple_of(index * 256, 256), 256)
        for piece in range(2):
            gate = nn_product(rows_refs[piece][...], gate_ref[:, lanes])
            up = nn_product(rows_refs[piece][...], wide_ref[:, lanes])
            hidden_grad = nn_product(top_refs[piece][...], down_ref[:, lanes])
            gelu_value, gelu_slope = gelu_parts(gate)
            hidden_refs[piece][:, lanes] = low(gelu_value * up)
            gate_refs[piece][:, lanes] = low(hidden_grad * up * gelu_slope)
            up_refs[piece][:, lanes] = low(hidden_grad * gelu_value)
        return 0

    lax.fori_loop(0, padded // 256, one_chunk, 0)

    def one_back(index, _):
        part = pl.ds(pl.multiple_of(index * 256, 256), 256)
        for piece in range(2):
            back = nt_product(gate_refs[piece][...], gate_ref[part, :]) + nt_product(up_refs[piece][...], wide_ref[part, :])
            back_refs[piece][:, part] = back.astype(back_refs[piece].dtype)
        return 0

    lax.fori_loop(0, features // 256, one_back, 0)


def feed(rows, top, weights, hidden):
    size, features = rows[0].shape
    padded = (hidden + 255) // 256 * 256
    kept = [jax.ShapeDtypeStruct((size, padded), jnp.bfloat16)] * 6
    back = [jax.ShapeDtypeStruct((size, features), kind) for kind in (jnp.float32, jnp.bfloat16)]
    outs = pl.pallas_call(
        functools.partial(feed_kernel, hidden=hidden, padded=padded),
        out_shape=kept + back,
        in_specs=[VMEM_SPEC] * 5,
        out_specs=[VMEM_SPEC] * 8,
        scratch_shapes=[pltpu.VMEM((features, padded), jnp.bfloat16)] * 3,
        compiler_params=pltpu.CompilerParams(vmem_limit_bytes=32 << 20),
        cost_estimate=lasting(12),
        name="feed",
    )(weights, *rows, *top)
    return outs[0:2], outs[2:4], outs[4:6], outs[6:8]


ROW_TILE = 64


def join_kernel(*refs, terms):
    stream_ref, gain_ref = refs[terms : terms + 2]
    joined_ref, normed_ref = refs[terms + 2 :]

    def one_tile(index, _):
        tile = pl.ds(pl.multiple_of(index * ROW_TILE, ROW_TILE), ROW_TILE)
        rows = stream_ref[tile, :].astype(jnp.float32)
        for ref in refs[:terms]:
            rows = rows + ref[tile, :].astype(jnp.float32)
        joined_ref[tile, :] = rows
        normed_ref[tile, :] = low(rows * norm_scale(rows) * gain_ref[...])
        return 0

    lax.fori_loop(0, stream_ref.shape[0] // ROW_TILE, one_tile, 0)


def join(terms, stream, gain):
    return pl.pallas_call(
        functools.partial(join_kernel, terms=len(terms)),
        out_shape=[jax.ShapeDtypeStruct(stream.shape, kind) for kind in (jnp.float32, jnp.bfloat16)],
        in_specs=[VMEM_SPEC] * (len(terms) + 2),
        out_specs=[VMEM_SPEC] * 2,
        compiler_params=pltpu.CompilerParams(vmem_limit_bytes=12 << 20),
        cost_estimate=lasting(4),
        name="join",
    )(*terms, stream, gain[None])


def join_back_kernel(*refs, terms):
    stream_ref, upper_ref, gain_ref = refs[terms : terms + 3]
    total_ref, rounded_ref, gain_grad_ref = refs[terms + 3 :]
    gain_grad_ref[...] = jnp.zeros_like(gain_grad_ref)

    def one_tile(index, _):
        tile = pl.ds(pl.multiple_of(index * ROW_TILE, ROW_TILE), ROW_TILE)
        grads = refs[0][tile, :].astype(jnp.float32)
        for ref in refs[1:terms]:
            grads = grads + ref[tile, :].astype(jnp.float32)
        rows = stream_ref[tile, :].astype(jnp.float32)
        scale = norm_scale(rows)
        scaled = grads * gain_ref[...]
        row_grad = scale * scaled - rows * (scale * scale * scale) * jnp.mean(scaled * rows, axis=-1, keepdims=True)
        total = upper_ref[tile, :].astype(jnp.float32) + row_grad
        total_ref[tile, :] = total
        rounded_ref[tile, :] = low(total)
        gain_grad_ref[...] += jnp.sum(grads * rows * scale, axis=0, keepdims=True)
        return 0

    lax.fori_loop(0, stream_ref.shape[0] // ROW_TILE, one_tile, 0)


def join_back(terms, stream, upper, gain):
    total, rounded, gain_grad = pl.pallas_call(
        functools.partial(join_back_kernel, terms=len(terms)),
        out_shape=[
            jax.ShapeDtypeStruct(stream.shape, jnp.float32),
            jax.ShapeDtypeStruct(stream.shape, jnp.bfloat16),
            jax.ShapeDtypeStruct((1, stream.shape[1]), jnp.float32),
        ],
        in_specs=[VMEM_SPEC] * (len(terms) + 3),
        out_specs=[VMEM_SPEC] * 3,
        compiler_params=pltpu.CompilerParams(vmem_limit_bytes=16 << 20),
        cost_estimate=lasting(5),
        name="join_back",
    )(*terms, stream, upper, gain[None])
    return total, rounded, gain_grad[0]


def exchange(rows, axis, size, bits):
    return lax.ppermute(rows, axis, [(i, i ^ bits) for i in range(size)])


def to_core(rows):
    return exchange(rows, "mp", PEERS, 1)


def across(rows):
    return exchange(rows, "mp", PEERS, 2)


def after(value, *others):
    return lax.optimization_barrier((value, *others))[0]


def gather_four(rows):
    far = across(rows)
    return rows, to_core(rows), far, to_core(far)


def prepare(own, other):
    return low(own + to_core(low(other)).astype(jnp.float32))


def sum_core(own, other):
    return own + to_core(low(other)).astype(jnp.float32)


def reduce_directly(grads, size):
    return lax.all_to_all(grads, "dp", split_axis=0, concat_axis=0, tiled=True)


def sum_parts(arrived, size):
    return jnp.sum(arrived.reshape(size, -1, arrived.shape[1]).astype(jnp.float32), axis=0)


def sum_everywhere(value, sizes):
    for axis in ("mp", "dp"):
        step = 1
        while step < sizes[axis]:
            value = value + exchange(value, axis, sizes[axis], step)
            step *= 2
    return value


def columns_of(array, widths):
    pieces = []
    at = 0
    for width in widths:
        pieces.append(array[:, at : at + width])
        at += width
    return pieces


def key_ranges(ids, key_ids, documents):
    numbers = jnp.arange(documents, dtype=jnp.int32)
    below = jnp.sum((key_ids[None, :] < numbers[:, None]).astype(jnp.int32), axis=1)
    upto = jnp.sum((key_ids[None, :] <= numbers[:, None]).astype(jnp.int32), axis=1)
    mine = (ids[None, :] == numbers[:, None]).astype(jnp.int32)
    return (jnp.sum(mine * below[:, None], axis=0), jnp.sum(mine * upto[:, None], axis=0))


def block_ranges(first, last, block, tall):
    return (first[::block] // tall, (last[block - 1 :: block] + tall - 1) // tall)


DOCUMENTS = 8
LONGEST = 768


def per_device(
    tokens,
    encoder_out,
    segments,
    encoder_segments,
    buckets,
    rel_table,
    gain_attend,
    gain_cross,
    gain_feed,
    self_query,
    self_key,
    self_value,
    self_output,
    cross_query,
    cross_key,
    cross_value,
    cross_output,
    w_gate,
    w_up,
    w_down,
    out_grad,
    *,
    sizes,
):
    parts = sizes["dp"]
    wide = self_query.shape[1]
    hidden_wide = w_gate.shape[1]
    heads = wide // DK
    block = 256
    own_rows = tokens.shape[0]
    me = lax.axis_index("mp")

    attend_shard = pack(
        [self_query, self_key, self_value, self_output, cross_query, cross_output, cross_key, cross_value],
        [False, False, False, True, False, True, False, False],
    )
    attend_all = lax.all_gather(attend_shard, "dp", axis=0, tiled=True)
    feed_shard = pack([w_gate, w_up, w_down], [False, False, True])
    feed_all = lax.all_gather(feed_shard, "dp", axis=0, tiled=True)
    to_cross = 4 * wide

    buckets_count = rel_table.shape[0]
    stream_zero = tokens.astype(jnp.float32)
    scale_zero = norm_scale(stream_zero)
    normed_zero = low(stream_zero * scale_zero * gain_attend)
    features = tokens.shape[1]
    encoder_rows = encoder_out.shape[0]
    ids = jnp.concatenate([segments, encoder_segments], axis=1)
    ids = jnp.pad(ids, ((0, 15), (0, features - ids.shape[1]))).astype(jnp.bfloat16)
    row_pieces = gather_four(jnp.concatenate([encoder_out, ids], axis=0))
    normed_one = list(gather_four(normed_zero))
    encoder_all = place(row_pieces, me, 0, encoder_rows)
    top = list(gather_four(after(out_grad, normed_one[2], row_pieces[2])))

    id_rows = jnp.concatenate([piece[encoder_rows:][:1] for piece in row_pieces], axis=0).astype(jnp.int32)
    near_ids = id_rows[:2, :own_rows].reshape(-1)
    ids = jnp.concatenate([lax.dynamic_slice_in_dim(id_rows, me ^ peer, 1, 0) for peer in range(PEERS)], axis=0)
    decoder_ids = ids[:, :own_rows].reshape(-1)
    encoder_ids = ids[:, own_rows : own_rows + encoder_rows].reshape(-1)
    length = decoder_ids.shape[0]
    self_first, unused = key_ranges(decoder_ids, decoder_ids, DOCUMENTS)
    self_last = jnp.arange(length, dtype=jnp.int32) + 1
    self_low, self_high = block_ranges(self_first, self_last, block, block)
    self_ranges = (self_low, self_high, self_first[None], self_last[None])
    cross_first, cross_last = key_ranges(near_ids, encoder_ids, DOCUMENTS)
    cross_low, cross_high = block_ranges(cross_first, cross_last, own_rows, block)
    cross_ranges = (cross_low, cross_high, cross_first[None], cross_last[None])

    offsets = min((LONGEST + block - 2) // block + 1, length // block)
    reach = offsets * block
    table_local = lax.dynamic_slice_in_dim(rel_table, me * heads, heads, 1)
    onehot = (buckets[None, :reach] == jnp.arange(buckets_count, dtype=jnp.int32)[:, None]).astype(jnp.float32)
    series = lax.dot_general(table_local, onehot, (((0,), (0,)), ((), ())), precision=lax.Precision.HIGHEST)
    bias = bias_tiles(jnp.pad(series, ((0, 0), (block, 0))), offsets, block)

    wider = [jnp.float32, jnp.bfloat16]
    qkv = multiply(normed_one, after(attend_all, top[2], top[3], feed_shard), 0, 3 * wide)
    *context_one, context_one_t, totals_one = attend_forward(self_ranges, me, qkv, None, bias, heads, block, block)
    cross_other = across(attend_all[:, to_cross : to_cross + 2 * wide])
    context_one[2] = after(context_one[2], cross_other)
    terms = multiply(context_one[2:], attend_all, 3 * wide, features, wider, True)
    far_ready = prepare(*terms)
    far_sum = across(far_ready)
    keys_values = multiply([encoder_all], attend_all, to_cross + 2 * wide, 2 * wide)[0]
    keys_values_two = [keys_values, across(keys_values)]
    terms = multiply([after(context_one[0], far_ready), context_one[1]], attend_all, 3 * wide, features, wider, True)
    far_sum = after(far_sum, terms[0], keys_values_two[1])
    stream_one, normed_own = join([terms[0], to_core(terms[1]), far_sum], tokens, gain_cross)

    cross_weights = [(attend_all, to_cross), (cross_other, 0)]
    normed_two = [normed_own, to_core(normed_own)]
    still = jnp.zeros_like(me)
    queries_two, contexts_two, backs_two = [], [], []
    for (weights, at), keys_values in zip(cross_weights, keys_values_two):
        queries_two.append(multiply(normed_two, weights, at, wide))
        *context, context_t, totals = attend_forward(
            cross_ranges, still, queries_two[-1], keys_values, None, heads, own_rows, block
        )
        contexts_two.append(context)
        backs_two.append((context_t, totals))
    terms = [
        multiply(context, weights, at + wide, features, wider, True)
        for context, (weights, at) in zip(contexts_two, cross_weights)
    ]
    stream_two, normed_own = join(
        [terms[0][0], terms[1][0], to_core(terms[0][1] + terms[1][1])], stream_one, gain_feed
    )

    normed_three = [normed_own, to_core(normed_own)]
    hidden_near, gate_grad_near, up_grad_near, back_near = feed(normed_three, top[:2], feed_all, hidden_wide)
    far_own = after(across(normed_own), *hidden_near, *gate_grad_near, *up_grad_near, *back_near)
    normed_three += [far_own, to_core(far_own)]
    hidden_far, gate_grad_far, up_grad_far, back_far = feed(normed_three[2:], top[2:], feed_all, hidden_wide)
    far_ready = prepare(*back_far)
    far_sum = across(far_ready)
    top[3] = after(top[3], far_ready)
    hidden = hidden_near + hidden_far
    feed_grads = weight_grads(
        [
            list(zip(normed_three, gate_grad_near + gate_grad_far)),
            list(zip(normed_three, up_grad_near + up_grad_far)),
            list(zip(top, hidden)),
        ],
        hidden_wide,
    )
    far_sum = after(far_sum, feed_grads)
    feed_sums = lax.psum_scatter(feed_grads, "dp", scatter_dimension=0, tiled=True)
    stream_grad, grad_own, feed_gain_grad = join_back(
        [back_near[0], to_core(back_near[1]), far_sum], stream_two, out_grad, gain_feed
    )

    grad_two = [grad_own, to_core(grad_own)]
    query_grads, key_value_grads, backs = [], [], []
    for (weights, at), queries, keys_values, back in zip(cross_weights, queries_two, keys_values_two, backs_two):
        context_grad = multiply(grad_two, weights, at + wide, wide)
        *query_grad, key_value_grad = attend_backward(
            cross_ranges, still, queries, keys_values, context_grad, *back, None, heads, own_rows, block
        )
        query_grads.append(query_grad)
        key_value_grads.append(key_value_grad)
        backs.append(multiply(query_grad, weights, at, features, wider, True))
    stream_grad, grad_own, cross_gain_grad = join_back(
        [backs[0][0], backs[1][0], to_core(backs[0][1] + backs[1][1])], stream_one, stream_grad, gain_cross
    )

    grad_peer = to_core(grad_own)
    context_grad = multiply([grad_own, grad_peer], attend_all, 3 * wide, wide)
    cross_grads = [
        weight_grads([list(zip(normed_two, query_grad)), list(zip([grad_two[0], after(grad_two[1], grad_own)], context))])
        for query_grad, context in zip(query_grads, contexts_two)
    ]
    cross_far = across(jnp.concatenate([cross_grads[1], key_value_grads[1]], axis=0))
    layer_terms = multiply(hidden_far, feed_all, 2 * hidden_wide, features, wider, True, hidden_wide)
    layer_ready = prepare(*layer_terms)
    grad_far = after(across(grad_own), *context_grad, *cross_grads, layer_ready)
    grad_one = [grad_own, grad_peer, grad_far, to_core(grad_far)]
    context_grad = context_grad + multiply(grad_one[2:], attend_all, 3 * wide, wide)
    *qkv_grad, diagonals = attend_backward(
        self_ranges, me, qkv, None, context_grad, context_one_t, totals_one, bias, heads, block, block
    )
    self_grads = weight_grads([list(zip(normed_one, qkv_grad)), list(zip(grad_one, context_one))])
    self_parts = lax.psum_scatter(self_grads, "dp", scatter_dimension=0, tiled=True)
    qkv_grad[2] = after(qkv_grad[2], self_grads, feed_sums)
    terms = multiply(qkv_grad[2:], attend_all, 0, features, wider, True)
    far_ready = prepare(*terms)
    far_sum = across(far_ready)
    cross_far = after(cross_far, self_grads, feed_sums)
    key_value_grad = low(key_value_grads[0].astype(jnp.float32) + cross_far[features:].astype(jnp.float32))
    key_value_weights = weight_grads([[(encoder_all, key_value_grad)]])
    cross_total = low(cross_grads[0].astype(jnp.float32) + cross_far[:features].astype(jnp.float32))
    cross_parts = reduce_directly(jnp.concatenate([cross_total, key_value_weights], axis=1), parts)
    qkv_grad[0] = after(qkv_grad[0], far_ready)
    terms = multiply(qkv_grad[:2], attend_all, 0, features, wider, True)
    tokens_grad, unused, attend_gain_grad = join_back(
        [terms[0], to_core(terms[1]), far_sum], tokens, stream_grad, gain_attend
    )

    diagonals = diagonal_sums(after(diagonals, far_ready))
    ahead = jnp.moveaxis(diagonals[:, :, :block], 0, 1).reshape(heads, reach)
    behind = jnp.moveaxis(diagonals[1:, :, block:], 0, 1).reshape(heads, reach - block)
    series_grad = ahead + jnp.pad(behind, ((0, 0), (0, block)))
    table_grad = lax.dot_general(onehot, series_grad, (((1,), (1,)), ((), ())), precision=lax.Precision.HIGHEST)
    table_full = lax.dynamic_update_slice(jnp.zeros(rel_table.shape, jnp.float32), table_grad, (0, me * heads))
    small = jnp.concatenate([attend_gain_grad, cross_gain_grad, feed_gain_grad, table_full.reshape(-1)])
    small = sum_everywhere(small.reshape(-1, 128), sizes).reshape(-1)
    encoder_terms = multiply(
        [after(swap_order(key_value_grad, me), far_ready)], attend_all, to_cross + 2 * wide, features, jnp.float32, True
    )[0]
    encoder_terms = [encoder_terms[at : at + encoder_rows] for at in range(0, PEERS * encoder_rows, encoder_rows)]
    encoder_ready = prepare(encoder_terms[2], encoder_terms[3])
    layer_far, encoder_far = across(after(layer_ready, far_sum)), across(after(encoder_ready, far_sum))
    small, layer_far, encoder_far, cross_parts = lax.optimization_barrier((small, layer_far, encoder_far, cross_parts))
    layer_terms = multiply(hidden_near, feed_all, 2 * hidden_wide, features, wider, True, hidden_wide)
    layer_out = low(stream_two + sum_core(*layer_terms) + layer_far.astype(jnp.float32))
    encoder_grad = sum_core(encoder_terms[0], encoder_terms[1]) + encoder_far.astype(jnp.float32)

    attend_gain_sum, cross_gain_sum, feed_gain_sum = (
        small[:features],
        small[features : 2 * features],
        small[2 * features : 3 * features],
    )
    table_sum = small[3 * features :].reshape(rel_table.shape)
    cross_sums = sum_parts(cross_parts, parts)
    self_parts = after(self_parts, small, layer_out, encoder_grad, cross_sums)
    query_one_sum, key_one_sum, value_one_sum, output_one_sum = unpack(
        self_parts, [wide] * 4, [False, False, False, True]
    )
    query_two_sum, output_two_sum, key_two_sum, value_two_sum = columns_of(cross_sums, [wide] * 4)
    gate_sum, up_sum, down_sum = unpack(feed_sums, [hidden_wide] * 3, [False, False, True])
    return (
        layer_out,
        tokens_grad,
        encoder_grad,
        table_sum,
        attend_gain_sum,
        cross_gain_sum,
        feed_gain_sum,
        query_one_sum,
        key_one_sum,
        value_one_sum,
        output_one_sum,
        query_two_sum,
        key_two_sum,
        value_two_sum,
        output_two_sum.T,
        gate_sum,
        up_sum,
        down_sum,
    )


def solution(mesh):
    in_specs = (
        P(("dp", "mp"), None),
        P(("dp", "mp"), None),
        P("dp", "mp"),
        P("dp", "mp"),
        P(),
        P(),
        P(),
        P(),
        P(),
        P("dp", "mp"),
        P("dp", "mp"),
        P("dp", "mp"),
        P("mp", "dp"),
        P("dp", "mp"),
        P("dp", "mp"),
        P("dp", "mp"),
        P("mp", "dp"),
        P("dp", "mp"),
        P("dp", "mp"),
        P("mp", "dp"),
        P(("dp", "mp"), None),
    )
    out_specs = (
        P(("dp", "mp"), None),
        P(("dp", "mp"), None),
        P(("dp", "mp"), None),
        P(),
        P(),
        P(),
        P(),
        P("dp", "mp"),
        P("dp", "mp"),
        P("dp", "mp"),
        P("mp", "dp"),
        P("dp", "mp"),
        P("dp", "mp"),
        P("dp", "mp"),
        P("mp", "dp"),
        P("dp", "mp"),
        P("dp", "mp"),
        P("mp", "dp"),
    )
    return jax.shard_map(
        functools.partial(per_device, sizes=dict(mesh.shape)), mesh=mesh, in_specs=in_specs, out_specs=out_specs, check_vma=False
    )
```

```python
import functools
import jax
import jax.numpy as jnp
from jax import lax
from jax.experimental import pallas as pl
from jax.experimental.pallas import tpu as pltpu
from jax.sharding import PartitionSpec as P

DK = 64
PAIR = 2 * DK
NEG = -1e30
PEERS = 4

norm_eps = 1e-06
gelu_factor = 0.7978845608028654


def product(left, right):
    return jnp.dot(left, right, preferred_element_type=jnp.float32)


def rows_product(left, right):
    return lax.dot_general(left, right, (((0,), (0,)), ((), ())), preferred_element_type=jnp.float32)


def columns_product(left, right):
    return lax.dot_general(left, right, (((1,), (1,)), ((), ())), preferred_element_type=jnp.float32)


def norm_scale(rows):
    return lax.rsqrt(jnp.mean(rows * rows, axis=-1, keepdims=True) + norm_eps)


def gelu_parts(value):
    cubic = 0.044715 * value * value * value
    tangent = jnp.tanh(gelu_factor * (value + cubic))
    result = 0.5 * value * (1.0 + tangent)
    slope = 0.5 * (1.0 + tangent) + 0.5 * value * (1.0 - tangent * tangent) * gelu_factor * (
        1.0 + 3.0 * 0.044715 * value * value
    )
    return (result, slope)


def norm_back(grads, rows, scale, gain):
    scaled = grads * gain
    row_grad = scale * scaled - rows * (scale * scale * scale) * jnp.mean(scaled * rows, axis=-1, keepdims=True)
    gain_grad = jnp.sum(grads * rows * scale, axis=0)
    return (row_grad, gain_grad)


def low(value):
    return value.astype(jnp.bfloat16)


def nt_product(left, right):
    return lax.dot_general(left, right, (((1,), (1,)), ((), ())), preferred_element_type=jnp.float32)


def nn_product(left, right):
    return jnp.dot(left, right, preferred_element_type=jnp.float32)


def own_lanes(rows, head):
    lane = lax.broadcasted_iota(jnp.int32, rows.shape, 1)
    mine = (lane < DK) if head % 2 == 0 else (lane >= DK)
    return jnp.where(mine, rows, jnp.zeros_like(rows))


def bias_kernel(series_ref, tiles_ref, *, block):
    heads = series_ref.shape[0]
    for offset in range(tiles_ref.shape[0]):
        for head in range(heads):
            low = series_ref[pl.ds(head, 1), pl.ds(offset * block, block)]
            high = series_ref[pl.ds(head, 1), pl.ds((offset + 1) * block, block)]
            base = jnp.broadcast_to(jnp.concatenate([high, low], axis=1), (block, 2 * block))
            rolled = pltpu.roll(base, 0, 1, stride=1, stride_axis=0)
            tiles_ref[offset, head] = rolled[:, :block]


def bias_tiles(series, offsets, block):
    heads = series.shape[0]
    return pl.pallas_call(
        functools.partial(bias_kernel, block=block),
        out_shape=jax.ShapeDtypeStruct((offsets, heads, block, block), jnp.float32),
        compiler_params=pltpu.CompilerParams(vmem_limit_bytes=16 << 20),
        cost_estimate=lasting(4),
        name="bias_tiles",
    )(series)


def load_order(me, pieces, target_ref):
    size = pieces[0].shape[0]
    for order, piece in enumerate(pieces):
        at = pl.multiple_of((me ^ order) * size, size)
        target_ref[pl.ds(at, size), :] = piece[...]


def store_order(me, source_ref, pieces):
    size = pieces[0].shape[0]
    for order, piece in enumerate(pieces):
        at = pl.multiple_of((me ^ order) * size, size)
        piece[...] = source_ref[pl.ds(at, size), :].astype(jnp.bfloat16)


def forward_kernel(*refs, heads, block, tall, biased, at_key, at_value, pieces):
    low_ref, high_ref, me_ref, first_ref, last_ref, extra_ref = refs[:6]
    piece_refs = refs[6 : 6 + pieces]
    ctx_refs = refs[6 + pieces : 6 + 2 * pieces]
    ot_ref, lse_ref, acc_ref, vt_ref, q_ref, ctx_ref = refs[6 + 2 * pieces :]
    if biased:
        bias_ref, kv_ref = extra_ref, q_ref
    else:
        kv_ref = extra_ref
    load_order(me_ref[0], piece_refs, q_ref)
    rows = q_ref.shape[0]
    width = heads * DK
    key_iota = lax.broadcasted_iota(jnp.int32, (tall, block), 0)
    for tile in range(kv_ref.shape[0] // tall):
        vt_ref[:, pl.ds(tile * tall, tall)] = jnp.transpose(kv_ref[pl.ds(tile * tall, tall), pl.ds(at_value, width)])

    def one_block(index, _):
        start = pl.multiple_of(index * block, block)
        first = first_ref[:, pl.ds(start, block)]
        last = last_ref[:, pl.ds(start, block)]
        queries = [
            own_lanes(q_ref[pl.ds(start, block), pl.ds((head // 2) * PAIR, PAIR)], head) for head in range(heads)
        ]
        acc_ref[...] = jnp.zeros_like(acc_ref)

        def one_tile(tile, carry):
            at = pl.multiple_of(tile * tall, tall)
            valid = (key_iota >= first - at) & (key_iota < last - at)
            scores = []
            for head in range(heads):
                keys = kv_ref[pl.ds(at, tall), pl.ds(at_key + (head // 2) * PAIR, PAIR)]
                score = nt_product(keys, queries[head])
                if biased:
                    score = score + bias_ref[index - tile, head]
                scores.append(jnp.where(valid, score, NEG))
            results = []
            raised = []
            shrinks = []
            for head in range(heads):
                top, total = carry[head]
                new_top = jnp.maximum(top, jnp.max(scores[head], axis=0, keepdims=True))
                power = jnp.exp(scores[head] - new_top)
                shrink = jnp.exp(top - new_top)
                results.append((new_top, shrink * total + jnp.sum(power, axis=0, keepdims=True)))
                raised.append(power.astype(jnp.bfloat16))
                shrinks.append(shrink)
            for head in range(heads):
                mine = pl.ds(head * DK, DK)
                acc_ref[mine, :] = acc_ref[mine, :] * shrinks[head] + nn_product(
                    vt_ref[mine, pl.ds(at, tall)], raised[head]
                )
            return tuple(results)

        empty = tuple(
            (jnp.full((1, block), NEG, jnp.float32), jnp.zeros((1, block), jnp.float32)) for _ in range(heads)
        )
        stats = lax.fori_loop(low_ref[index], high_ref[index], one_tile, empty)
        for head in range(heads):
            top, total = stats[head]
            mine = pl.ds(head * DK, DK)
            acc_ref[mine, :] = acc_ref[mine, :] / total
            lse_ref[pl.ds(head, 1), pl.ds(start, block)] = top + jnp.log(total)
        ot_ref[:, pl.ds(start, block)] = acc_ref[...]
        ctx_ref[pl.ds(start, block), :] = jnp.transpose(acc_ref[...])
        return 0

    lax.fori_loop(0, rows // block, one_block, 0)
    store_order(me_ref[0], ctx_ref, ctx_refs)


def lasting(micros):
    return pl.CostEstimate(flops=int(micros * 1.1e9), bytes_accessed=1 << 10, transcendentals=0)


SMEM_SPEC = pl.BlockSpec(memory_space=pltpu.SMEM)
VMEM_SPEC = pl.BlockSpec(memory_space=pltpu.VMEM)


def attend_forward(ranges, me, queries, keys_values, bias, heads, block, tall):
    low_block, high_block, first, last = ranges
    pieces = len(queries)
    size, depth = queries[0].shape
    rows = pieces * size
    width = heads * DK
    biased = bias is not None
    at_key = width if biased else 0
    key_rows = rows if biased else keys_values.shape[0]
    operands = [low_block, high_block, me[None], first, last, bias if biased else keys_values, *queries]
    return pl.pallas_call(
        functools.partial(
            forward_kernel,
            heads=heads,
            block=block,
            tall=tall,
            biased=biased,
            at_key=at_key,
            at_value=at_key + width,
            pieces=pieces,
        ),
        out_shape=(
            *([jax.ShapeDtypeStruct((size, width), jnp.bfloat16)] * pieces),
            jax.ShapeDtypeStruct((width, rows), jnp.float32),
            jax.ShapeDtypeStruct((heads, rows), jnp.float32),
        ),
        in_specs=[SMEM_SPEC] * 3 + [VMEM_SPEC] * (len(operands) - 3),
        out_specs=(VMEM_SPEC,) * (pieces + 2),
        scratch_shapes=[
            pltpu.VMEM((width, block), jnp.float32),
            pltpu.VMEM((width, key_rows), jnp.bfloat16),
            pltpu.VMEM((rows, depth), jnp.bfloat16),
            pltpu.VMEM((rows, width), jnp.float32),
        ],
        compiler_params=pltpu.CompilerParams(vmem_limit_bytes=24 << 20),
        cost_estimate=lasting(14 if biased else 1),
        name="attend_forward",
    )(*operands)


def backward_kernel(*refs, heads, block, tall, biased, at_key, at_value, pieces):
    low_ref, high_ref, me_ref, ot_ref, lse_ref, first_ref, last_ref, extra_ref = refs[:8]
    piece_refs = refs[8 : 8 + pieces]
    g_refs = refs[8 + pieces : 8 + 2 * pieces]
    out_refs = refs[8 + 2 * pieces : 8 + 3 * pieces]
    refs = refs[8 + 3 * pieces :]
    if biased:
        diag_ref, dqt_ref, kt_ref, dka_ref, dva_ref, q_ref, g_ref, dq_ref = refs
        bias_ref = extra_ref
        kv_ref, dkv_ref = q_ref, dq_ref
    else:
        dkv_ref, dqt_ref, kt_ref, dka_ref, dva_ref, q_ref, g_ref, dq_ref = refs
        kv_ref = extra_ref
    load_order(me_ref[0], piece_refs, q_ref)
    load_order(me_ref[0], g_refs, g_ref)
    rows = q_ref.shape[0]
    width = heads * DK
    key_iota = lax.broadcasted_iota(jnp.int32, (tall, block), 0)
    for tile in range(kv_ref.shape[0] // tall):
        kt_ref[:, pl.ds(tile * tall, tall)] = jnp.transpose(kv_ref[pl.ds(tile * tall, tall), pl.ds(at_key, width)])
    dka_ref[...] = jnp.zeros_like(dka_ref)
    dva_ref[...] = jnp.zeros_like(dva_ref)
    if biased:
        diag_ref[...] = jnp.zeros_like(diag_ref)

    def one_block(index, _):
        start = pl.multiple_of(index * block, block)
        first = first_ref[:, pl.ds(start, block)]
        last = last_ref[:, pl.ds(start, block)]
        pairs = [pl.ds(pair * PAIR, PAIR) for pair in range(heads // 2)]
        queries = [own_lanes(q_ref[pl.ds(start, block), pairs[head // 2]], head) for head in range(heads)]
        grads = [own_lanes(g_ref[pl.ds(start, block), pairs[head // 2]], head) for head in range(heads)]
        shared = jnp.transpose(g_ref[pl.ds(start, block), :].astype(jnp.float32)) * ot_ref[:, pl.ds(start, block)]
        deltas = [jnp.sum(shared[head * DK : (head + 1) * DK], axis=0, keepdims=True) for head in range(heads)]
        totals = [lse_ref[pl.ds(head, 1), pl.ds(start, block)] for head in range(heads)]
        dqt_ref[...] = jnp.zeros_like(dqt_ref)

        def one_tile(tile, carry):
            at = pl.multiple_of(tile * tall, tall)
            valid = (key_iota >= first - at) & (key_iota < last - at)
            shares, score_grads = [], []
            for head in range(heads):
                pair = head // 2
                keys = kv_ref[pl.ds(at, tall), pl.ds(at_key + pair * PAIR, PAIR)]
                values = kv_ref[pl.ds(at, tall), pl.ds(at_value + pair * PAIR, PAIR)]
                scores = nt_product(keys, queries[head])
                share_grad = nt_product(values, grads[head])
                if biased:
                    scores = scores + bias_ref[index - tile, head]
                share = jnp.exp(jnp.where(valid, scores - totals[head], NEG))
                score_grad = (share * (share_grad - deltas[head])).astype(jnp.bfloat16)
                if biased:
                    diag_ref[index - tile, head] += score_grad.astype(jnp.float32)
                shares.append(share.astype(jnp.bfloat16))
                score_grads.append(score_grad)
            for pair in range(heads // 2):
                lanes = pl.ds(pair * PAIR, PAIR)
                one, two = 2 * pair, 2 * pair + 1
                dva_ref[pl.ds(at, tall), lanes] += nn_product(shares[one], grads[one]) + nn_product(shares[two], grads[two])
                dka_ref[pl.ds(at, tall), lanes] += nn_product(score_grads[one], queries[one]) + nn_product(
                    score_grads[two], queries[two]
                )
            for head in range(heads):
                mine = pl.ds(head * DK, DK)
                dqt_ref[mine, :] += nn_product(kt_ref[mine, pl.ds(at, tall)], score_grads[head])
            return carry

        lax.fori_loop(low_ref[index], high_ref[index], one_tile, 0)
        dq_ref[pl.ds(start, block), pl.ds(0, width)] = jnp.transpose(dqt_ref[...]).astype(jnp.bfloat16)
        return 0

    lax.fori_loop(0, rows // block, one_block, 0)
    dkv_ref[:, pl.ds(at_key, width)] = dka_ref[...].astype(jnp.bfloat16)
    dkv_ref[:, pl.ds(at_value, width)] = dva_ref[...].astype(jnp.bfloat16)
    store_order(me_ref[0], dq_ref, out_refs)


def diagonals_kernel(diag_ref, series_ref):
    offsets, heads, block, _ = diag_ref.shape

    def one_diagonal(index, _):
        offset, head = index >> (heads.bit_length() - 1), index & (heads - 1)
        slab = jnp.zeros((8, 2 * block), jnp.float32)
        for group in range(block // 8):
            piece = diag_ref[offset, head, pl.ds(8 * group, 8), :]
            wide = jnp.concatenate([piece, jnp.zeros_like(piece)], axis=1)
            slab = slab + (pltpu.roll(wide, 2 * block - 8 * group, 1) if group else wide)
        line = slab[0:1]
        for row in range(1, 8):
            line = line + pltpu.roll(slab[row : row + 1], 2 * block - row, 1)
        series_ref[offset, pl.ds(head, 1), :] = line
        return 0

    lax.fori_loop(0, offsets * heads, one_diagonal, 0)


def diagonal_sums(diagonals):
    offsets, heads, block, _ = diagonals.shape
    return pl.pallas_call(
        diagonals_kernel,
        out_shape=jax.ShapeDtypeStruct((offsets, heads, 2 * block), jnp.float32),
        in_specs=[VMEM_SPEC],
        out_specs=VMEM_SPEC,
        compiler_params=pltpu.CompilerParams(vmem_limit_bytes=8 << 20),
        cost_estimate=lasting(4),
        name="diagonal_sums",
    )(diagonals)


def attend_backward(ranges, me, queries, keys_values, grads, context_t, totals, bias, heads, block, tall):
    low_block, high_block, first, last = ranges
    pieces = len(queries)
    size, depth = queries[0].shape
    rows = pieces * size
    width = heads * DK
    biased = bias is not None
    at_key = width if biased else 0
    key_rows = rows if biased else keys_values.shape[0]
    operands = [low_block, high_block, me[None], context_t, totals, first, last, bias if biased else keys_values]
    operands += [*queries, *grads]
    shapes = [jax.ShapeDtypeStruct((size, depth), jnp.bfloat16)] * pieces
    scratch = [
        pltpu.VMEM((width, block), jnp.float32),
        pltpu.VMEM((width, key_rows), jnp.bfloat16),
        pltpu.VMEM((key_rows, width), jnp.float32),
        pltpu.VMEM((key_rows, width), jnp.float32),
        pltpu.VMEM((rows, depth), jnp.bfloat16),
        pltpu.VMEM((rows, width), jnp.bfloat16),
        pltpu.VMEM((rows, depth), jnp.bfloat16),
    ]
    if biased:
        shapes.append(jax.ShapeDtypeStruct(bias.shape, jnp.float32))
    else:
        shapes.append(jax.ShapeDtypeStruct((key_rows, 2 * width), jnp.bfloat16))
    return pl.pallas_call(
        functools.partial(
            backward_kernel,
            heads=heads,
            block=block,
            tall=tall,
            biased=biased,
            at_key=at_key,
            at_value=at_key + width,
            pieces=pieces,
        ),
        out_shape=tuple(shapes),
        in_specs=[SMEM_SPEC] * 3 + [VMEM_SPEC] * (len(operands) - 3),
        out_specs=(VMEM_SPEC,) * len(shapes),
        scratch_shapes=scratch,
        compiler_params=pltpu.CompilerParams(vmem_limit_bytes=36 << 20),
        cost_estimate=lasting(4),
        name="attend_backward",
    )(*operands)


def pack_kernel(*refs, turned):
    count = len(turned)
    out_ref, semaphores = refs[count], refs[-1]
    held = refs[count + 1 : -1]
    copies = [
        pltpu.make_async_copy(source, target, semaphores.at[order])
        for order, (source, target) in enumerate(zip(refs[:count], held))
    ]
    for copy in copies:
        copy.start()
    at = 0
    for copy, ref, turn in zip(copies, held, turned):
        copy.wait()
        piece = jnp.transpose(ref[...]) if turn else ref[...]
        out_ref[:, pl.ds(at, piece.shape[1])] = low(piece)
        at += piece.shape[1]


def pack(weights, turned):
    width = sum(weight.shape[0] if turn else weight.shape[1] for weight, turn in zip(weights, turned))
    rows = weights[0].shape[0]
    return pl.pallas_call(
        functools.partial(pack_kernel, turned=tuple(turned)),
        out_shape=jax.ShapeDtypeStruct((rows, width), jnp.bfloat16),
        in_specs=[pl.BlockSpec(memory_space=pltpu.HBM)] * len(weights),
        out_specs=VMEM_SPEC,
        scratch_shapes=[pltpu.VMEM(weight.shape, jnp.float32) for weight in weights]
        + [pltpu.SemaphoreType.DMA((len(weights),))],
        compiler_params=pltpu.CompilerParams(vmem_limit_bytes=12 << 20),
        cost_estimate=lasting(2),
        name="pack",
    )(*[pltpu.with_memory_space_constraint(weight, pltpu.HBM) for weight in weights])


def unpack_kernel(rows_ref, *refs, turned):
    at = 0
    for ref, turn in zip(refs, turned):
        width = ref.shape[0] if turn else ref.shape[1]
        piece = rows_ref[:, pl.ds(at, width)].astype(jnp.float32)
        ref[...] = jnp.transpose(piece) if turn else piece
        at += width


def unpack(rows, widths, turned):
    shapes = [(width, rows.shape[0]) if turn else (rows.shape[0], width) for width, turn in zip(widths, turned)]
    return pl.pallas_call(
        functools.partial(unpack_kernel, turned=tuple(turned)),
        out_shape=[jax.ShapeDtypeStruct(shape, jnp.float32) for shape in shapes],
        in_specs=[VMEM_SPEC],
        out_specs=[VMEM_SPEC] * len(widths),
        compiler_params=pltpu.CompilerParams(vmem_limit_bytes=8 << 20),
        cost_estimate=lasting(9),
        name="unpack",
    )(rows)


def place_kernel(me_ref, *refs, first):
    out_ref = refs[-1]
    pieces = refs[:-1]
    size = out_ref.shape[0] // len(pieces)
    for order, piece in enumerate(pieces):
        at = pl.multiple_of((me_ref[0] ^ order) * size, size)
        out_ref[pl.ds(at, size), :] = piece[pl.ds(first, size), :]


def place(pieces, me, first=0, size=None):
    size = size or pieces[0].shape[0]
    width = pieces[0].shape[1]
    count = len(pieces)
    return pl.pallas_call(
        functools.partial(place_kernel, first=first),
        out_shape=jax.ShapeDtypeStruct((count * size, width), pieces[0].dtype),
        in_specs=[SMEM_SPEC] + [VMEM_SPEC] * count,
        out_specs=VMEM_SPEC,
        compiler_params=pltpu.CompilerParams(vmem_limit_bytes=8 << 20),
        cost_estimate=lasting(2),
        name="place",
    )(me[None], *pieces)


def swap_kernel(me_ref, rows_ref, out_ref, *, count):
    size = rows_ref.shape[0] // count
    for order in range(count):
        at = pl.multiple_of((me_ref[0] ^ order) * size, size)
        out_ref[pl.ds(order * size, size), :] = rows_ref[pl.ds(at, size), :]


def swap_order(rows, me, count=4):
    return pl.pallas_call(
        functools.partial(swap_kernel, count=count),
        out_shape=jax.ShapeDtypeStruct(rows.shape, rows.dtype),
        in_specs=[SMEM_SPEC, VMEM_SPEC],
        out_specs=VMEM_SPEC,
        compiler_params=pltpu.CompilerParams(vmem_limit_bytes=4 << 20),
        cost_estimate=lasting(1),
        name="swap_order",
    )(me[None], rows)


def multiply_kernel(*refs, at, depth, transposed):
    count = (len(refs) - 1) // 2
    weights_ref = refs[0]
    width = refs[-1].shape[1]
    chunk = min(256, width)

    def one_chunk(index, _):
        start = pl.multiple_of(index * chunk, chunk)
        if transposed:
            weights = weights_ref[pl.ds(start, chunk), pl.ds(at, depth)]
        else:
            weights = weights_ref[:, pl.ds(at + start, chunk)]
        for rows_ref, out_ref in zip(refs[1 : 1 + count], refs[1 + count :]):
            product_of = nt_product if transposed else nn_product
            out_ref[:, pl.ds(start, chunk)] = product_of(rows_ref[:, pl.ds(0, depth)], weights).astype(out_ref.dtype)
        return 0

    lax.fori_loop(0, width // chunk, one_chunk, 0)


def multiply(pieces, weights, at, width, kinds=jnp.bfloat16, transposed=False, depth=None):
    kinds = kinds if isinstance(kinds, (list, tuple)) else [kinds] * len(pieces)
    return pl.pallas_call(
        functools.partial(multiply_kernel, at=at, depth=depth or pieces[0].shape[1], transposed=transposed),
        out_shape=[jax.ShapeDtypeStruct((piece.shape[0], width), kind) for piece, kind in zip(pieces, kinds)],
        in_specs=[VMEM_SPEC] * (1 + len(pieces)),
        out_specs=[VMEM_SPEC] * len(pieces),
        compiler_params=pltpu.CompilerParams(vmem_limit_bytes=16 << 20),
        cost_estimate=lasting(2),
        name="multiply",
    )(weights, *pieces)


def weights_kernel(*refs, groups, chunk):
    out_ref = refs[-1]
    features = out_ref.shape[0]

    def one_chunk(index, _):
        at = pl.multiple_of(index * chunk, chunk)
        operand = 0
        column = 0
        for terms, width in groups:
            total = None
            for _ in range(terms):
                left_ref, right_ref = refs[operand], refs[operand + 1]
                operand += 2
                term = lax.dot_general(
                    left_ref[:, pl.ds(at, chunk)],
                    right_ref[:, pl.ds(0, width)],
                    (((0,), (0,)), ((), ())),
                    preferred_element_type=jnp.float32,
                )
                total = term if total is None else total + term
            out_ref[pl.ds(at, chunk), pl.ds(column, width)] = total.astype(jnp.bfloat16)
            column += width
        return 0

    lax.fori_loop(0, features // chunk, one_chunk, 0)


def weight_grads(groups, width=None):
    operands = [array for group in groups for pair in group for array in pair]
    features = operands[0].shape[1]
    shapes = tuple((len(group), width or group[0][1].shape[1]) for group in groups)
    return pl.pallas_call(
        functools.partial(weights_kernel, groups=shapes, chunk=256),
        out_shape=jax.ShapeDtypeStruct((features, sum(wide for _, wide in shapes)), jnp.bfloat16),
        in_specs=[VMEM_SPEC] * len(operands),
        out_specs=VMEM_SPEC,
        compiler_params=pltpu.CompilerParams(vmem_limit_bytes=32 << 20),
        cost_estimate=lasting(16 if width else 8),
        name="weight_grads",
    )(*operands)


def feed_kernel(*refs, hidden, padded):
    weights_ref = refs[0]
    rows_refs, top_refs = refs[1:3], refs[3:5]
    hidden_refs, gate_refs, up_refs, back_refs = refs[5:7], refs[7:9], refs[9:11], refs[11:13]
    gate_ref, wide_ref, down_ref = refs[13:]
    features = weights_ref.shape[0]
    for order, target in enumerate((gate_ref, wide_ref, down_ref)):
        target[:, pl.ds(0, hidden)] = weights_ref[:, pl.ds(order * hidden, hidden)]
        if padded > hidden:
            target[:, pl.ds(hidden, padded - hidden)] = jnp.zeros((features, padded - hidden), jnp.bfloat16)

    def one_chunk(index, _):
        lanes = pl.ds(pl.multiple_of(index * 256, 256), 256)
        for piece in range(2):
            gate = nn_product(rows_refs[piece][...], gate_ref[:, lanes])
            up = nn_product(rows_refs[piece][...], wide_ref[:, lanes])
            hidden_grad = nn_product(top_refs[piece][...], down_ref[:, lanes])
            gelu_value, gelu_slope = gelu_parts(gate)
            hidden_refs[piece][:, lanes] = low(gelu_value * up)
            gate_refs[piece][:, lanes] = low(hidden_grad * up * gelu_slope)
            up_refs[piece][:, lanes] = low(hidden_grad * gelu_value)
        return 0

    lax.fori_loop(0, padded // 256, one_chunk, 0)

    def one_back(index, _):
        part = pl.ds(pl.multiple_of(index * 256, 256), 256)
        for piece in range(2):
            back = nt_product(gate_refs[piece][...], gate_ref[part, :]) + nt_product(up_refs[piece][...], wide_ref[part, :])
            back_refs[piece][:, part] = back.astype(back_refs[piece].dtype)
        return 0

    lax.fori_loop(0, features // 256, one_back, 0)


def feed(rows, top, weights, hidden):
    size, features = rows[0].shape
    padded = (hidden + 255) // 256 * 256
    kept = [jax.ShapeDtypeStruct((size, padded), jnp.bfloat16)] * 6
    back = [jax.ShapeDtypeStruct((size, features), kind) for kind in (jnp.float32, jnp.bfloat16)]
    outs = pl.pallas_call(
        functools.partial(feed_kernel, hidden=hidden, padded=padded),
        out_shape=kept + back,
        in_specs=[VMEM_SPEC] * 5,
        out_specs=[VMEM_SPEC] * 8,
        scratch_shapes=[pltpu.VMEM((features, padded), jnp.bfloat16)] * 3,
        compiler_params=pltpu.CompilerParams(vmem_limit_bytes=32 << 20),
        cost_estimate=lasting(12),
        name="feed",
    )(weights, *rows, *top)
    return outs[0:2], outs[2:4], outs[4:6], outs[6:8]


ROW_TILE = 64


def join_kernel(*refs, terms):
    stream_ref, gain_ref = refs[terms : terms + 2]
    joined_ref, normed_ref = refs[terms + 2 :]

    def one_tile(index, _):
        tile = pl.ds(pl.multiple_of(index * ROW_TILE, ROW_TILE), ROW_TILE)
        rows = stream_ref[tile, :].astype(jnp.float32)
        for ref in refs[:terms]:
            rows = rows + ref[tile, :].astype(jnp.float32)
        joined_ref[tile, :] = rows
        normed_ref[tile, :] = low(rows * norm_scale(rows) * gain_ref[...])
        return 0

    lax.fori_loop(0, stream_ref.shape[0] // ROW_TILE, one_tile, 0)


def join(terms, stream, gain):
    return pl.pallas_call(
        functools.partial(join_kernel, terms=len(terms)),
        out_shape=[jax.ShapeDtypeStruct(stream.shape, kind) for kind in (jnp.float32, jnp.bfloat16)],
        in_specs=[VMEM_SPEC] * (len(terms) + 2),
        out_specs=[VMEM_SPEC] * 2,
        compiler_params=pltpu.CompilerParams(vmem_limit_bytes=12 << 20),
        cost_estimate=lasting(4),
        name="join",
    )(*terms, stream, gain[None])


def join_back_kernel(*refs, terms):
    stream_ref, upper_ref, gain_ref = refs[terms : terms + 3]
    total_ref, rounded_ref, gain_grad_ref = refs[terms + 3 :]
    gain_grad_ref[...] = jnp.zeros_like(gain_grad_ref)

    def one_tile(index, _):
        tile = pl.ds(pl.multiple_of(index * ROW_TILE, ROW_TILE), ROW_TILE)
        grads = refs[0][tile, :].astype(jnp.float32)
        for ref in refs[1:terms]:
            grads = grads + ref[tile, :].astype(jnp.float32)
        rows = stream_ref[tile, :].astype(jnp.float32)
        scale = norm_scale(rows)
        scaled = grads * gain_ref[...]
        row_grad = scale * scaled - rows * (scale * scale * scale) * jnp.mean(scaled * rows, axis=-1, keepdims=True)
        total = upper_ref[tile, :].astype(jnp.float32) + row_grad
        total_ref[tile, :] = total
        rounded_ref[tile, :] = low(total)
        gain_grad_ref[...] += jnp.sum(grads * rows * scale, axis=0, keepdims=True)
        return 0

    lax.fori_loop(0, stream_ref.shape[0] // ROW_TILE, one_tile, 0)


def join_back(terms, stream, upper, gain):
    total, rounded, gain_grad = pl.pallas_call(
        functools.partial(join_back_kernel, terms=len(terms)),
        out_shape=[
            jax.ShapeDtypeStruct(stream.shape, jnp.float32),
            jax.ShapeDtypeStruct(stream.shape, jnp.bfloat16),
            jax.ShapeDtypeStruct((1, stream.shape[1]), jnp.float32),
        ],
        in_specs=[VMEM_SPEC] * (len(terms) + 3),
        out_specs=[VMEM_SPEC] * 3,
        compiler_params=pltpu.CompilerParams(vmem_limit_bytes=16 << 20),
        cost_estimate=lasting(5),
        name="join_back",
    )(*terms, stream, upper, gain[None])
    return total, rounded, gain_grad[0]


def exchange(rows, axis, size, bits):
    return lax.ppermute(rows, axis, [(i, i ^ bits) for i in range(size)])


def to_core(rows):
    return exchange(rows, "mp", PEERS, 1)


def across(rows):
    return exchange(rows, "mp", PEERS, 2)


def after(value, *others):
    return lax.optimization_barrier((value, *others))[0]


def gather_four(rows):
    far = across(rows)
    return rows, to_core(rows), far, to_core(far)


def prepare(own, other):
    return low(own + to_core(low(other)).astype(jnp.float32))


def sum_core(own, other):
    return own + to_core(low(other)).astype(jnp.float32)


def split_kernel(me_ref, own_ref, far_ref, rest_ref, kept_ref, sent_ref, *, size):
    rows = own_ref.shape[0] // size
    wide = own_ref.shape[1]
    for order in range(size):
        at = pl.ds(pl.multiple_of((me_ref[0] ^ order) * rows, rows), rows)
        out_ref = sent_ref if order & 1 else kept_ref
        to = pl.ds((order >> 1) * rows, rows)
        out_ref[to, pl.ds(0, wide)] = low(own_ref[at, :].astype(jnp.float32) + far_ref[at, :].astype(jnp.float32))
        out_ref[to, pl.ds(wide, wide)] = rest_ref[at, :]


def split(own, far, rest, size, dp_index):
    half = jax.ShapeDtypeStruct((own.shape[0] // 2, 2 * own.shape[1]), jnp.bfloat16)
    return pl.pallas_call(
        functools.partial(split_kernel, size=size),
        out_shape=[half, half],
        in_specs=[SMEM_SPEC] + [VMEM_SPEC] * 3,
        out_specs=[VMEM_SPEC] * 2,
        compiler_params=pltpu.CompilerParams(vmem_limit_bytes=8 << 20),
        cost_estimate=lasting(2),
        name="split",
    )(dp_index[None], own, far, rest)


def reduce_in_steps(kept, sent, size):
    arrived = exchange(sent, "dp", size, 1)
    kept = low(kept.astype(jnp.float32) + arrived.astype(jnp.float32)).reshape(size // 2, -1, kept.shape[1])
    return [kept[0]] + [exchange(kept[order], "dp", size, 2 * order) for order in range(1, size // 2)]


def sum_everywhere(value, sizes):
    for axis in ("dp", "mp"):
        step = sizes[axis] // 2
        while step:
            value = value + exchange(value, axis, sizes[axis], step)
            step //= 2
    return value


def columns_of(array, widths):
    pieces = []
    at = 0
    for width in widths:
        pieces.append(array[:, at : at + width])
        at += width
    return pieces


def key_ranges(ids, key_ids, documents):
    numbers = jnp.arange(documents, dtype=jnp.int32)
    below = jnp.sum((key_ids[None, :] < numbers[:, None]).astype(jnp.int32), axis=1)
    upto = jnp.sum((key_ids[None, :] <= numbers[:, None]).astype(jnp.int32), axis=1)
    mine = (ids[None, :] == numbers[:, None]).astype(jnp.int32)
    return (jnp.sum(mine * below[:, None], axis=0), jnp.sum(mine * upto[:, None], axis=0))


def block_ranges(first, last, block, tall):
    return (first[::block] // tall, (last[block - 1 :: block] + tall - 1) // tall)


DOCUMENTS = 8
LONGEST = 768


def per_device(
    tokens,
    encoder_out,
    segments,
    encoder_segments,
    buckets,
    rel_table,
    gain_attend,
    gain_cross,
    gain_feed,
    self_query,
    self_key,
    self_value,
    self_output,
    cross_query,
    cross_key,
    cross_value,
    cross_output,
    w_gate,
    w_up,
    w_down,
    out_grad,
    *,
    sizes,
):
    parts = sizes["dp"]
    wide = self_query.shape[1]
    hidden_wide = w_gate.shape[1]
    heads = wide // DK
    block = 256
    own_rows = tokens.shape[0]
    me = lax.axis_index("mp")
    dp_index = lax.axis_index("dp")

    attend_shard = pack(
        [self_query, self_key, self_value, self_output, cross_query, cross_output, cross_key, cross_value],
        [False, False, False, True, False, True, False, False],
    )
    attend_all = lax.all_gather(attend_shard, "dp", axis=0, tiled=True)
    feed_shard = pack([w_gate, w_up, w_down], [False, False, True])
    feed_all = lax.all_gather(feed_shard, "dp", axis=0, tiled=True)
    to_cross = 4 * wide

    buckets_count = rel_table.shape[0]
    stream_zero = tokens.astype(jnp.float32)
    scale_zero = norm_scale(stream_zero)
    normed_zero = low(stream_zero * scale_zero * gain_attend)
    features = tokens.shape[1]
    encoder_rows = encoder_out.shape[0]
    ids = jnp.concatenate([segments, encoder_segments], axis=1)
    ids = jnp.pad(ids, ((0, 15), (0, features - ids.shape[1]))).astype(jnp.bfloat16)
    row_pieces = gather_four(jnp.concatenate([encoder_out, ids], axis=0))
    normed_one = list(gather_four(normed_zero))
    encoder_all = place(row_pieces, me, 0, encoder_rows)
    top = list(gather_four(after(out_grad, normed_one[2], row_pieces[2])))

    id_rows = jnp.concatenate([piece[encoder_rows:][:1] for piece in row_pieces], axis=0).astype(jnp.int32)
    near_ids = id_rows[:2, :own_rows].reshape(-1)
    ids = jnp.concatenate([lax.dynamic_slice_in_dim(id_rows, me ^ peer, 1, 0) for peer in range(PEERS)], axis=0)
    decoder_ids = ids[:, :own_rows].reshape(-1)
    encoder_ids = ids[:, own_rows : own_rows + encoder_rows].reshape(-1)
    length = decoder_ids.shape[0]
    self_first, unused = key_ranges(decoder_ids, decoder_ids, DOCUMENTS)
    self_last = jnp.arange(length, dtype=jnp.int32) + 1
    self_low, self_high = block_ranges(self_first, self_last, block, block)
    self_ranges = (self_low, self_high, self_first[None], self_last[None])
    cross_first, cross_last = key_ranges(near_ids, encoder_ids, DOCUMENTS)
    cross_low, cross_high = block_ranges(cross_first, cross_last, own_rows, block)
    cross_ranges = (cross_low, cross_high, cross_first[None], cross_last[None])

    offsets = min((LONGEST + block - 2) // block + 1, length // block)
    reach = offsets * block
    table_local = lax.dynamic_slice_in_dim(rel_table, me * heads, heads, 1)
    onehot = (buckets[None, :reach] == jnp.arange(buckets_count, dtype=jnp.int32)[:, None]).astype(jnp.float32)
    series = lax.dot_general(table_local, onehot, (((0,), (0,)), ((), ())), precision=lax.Precision.HIGHEST)
    bias = bias_tiles(jnp.pad(series, ((0, 0), (block, 0))), offsets, block)

    wider = [jnp.float32, jnp.bfloat16]
    qkv = multiply(normed_one, after(attend_all, top[2], top[3], feed_shard), 0, 3 * wide)
    *context_one, context_one_t, totals_one = attend_forward(self_ranges, me, qkv, None, bias, heads, block, block)
    cross_other = across(attend_all[:, to_cross : to_cross + 2 * wide])
    context_one[2] = after(context_one[2], cross_other)
    terms = multiply(context_one[2:], attend_all, 3 * wide, features, wider, True)
    far_ready = prepare(*terms)
    far_sum = across(far_ready)
    keys_values = multiply([encoder_all], attend_all, to_cross + 2 * wide, 2 * wide)[0]
    keys_values_two = [keys_values, across(keys_values)]
    terms = multiply([after(context_one[0], far_ready), context_one[1]], attend_all, 3 * wide, features, wider, True)
    far_sum = after(far_sum, terms[0], keys_values_two[1])
    stream_one, normed_own = join([terms[0], to_core(terms[1]), far_sum], tokens, gain_cross)

    cross_weights = [(attend_all, to_cross), (cross_other, 0)]
    normed_two = [normed_own, to_core(normed_own)]
    still = jnp.zeros_like(me)
    queries_two, contexts_two, backs_two = [], [], []
    for (weights, at), keys_values in zip(cross_weights, keys_values_two):
        queries_two.append(multiply(normed_two, weights, at, wide))
        *context, context_t, totals = attend_forward(
            cross_ranges, still, queries_two[-1], keys_values, None, heads, own_rows, block
        )
        contexts_two.append(context)
        backs_two.append((context_t, totals))
    terms = [
        multiply(context, weights, at + wide, features, wider, True)
        for context, (weights, at) in zip(contexts_two, cross_weights)
    ]
    stream_two, normed_own = join(
        [terms[0][0], terms[1][0], to_core(terms[0][1] + terms[1][1])], stream_one, gain_feed
    )

    normed_three = [normed_own, to_core(normed_own)]
    hidden_near, gate_grad_near, up_grad_near, back_near = feed(normed_three, top[:2], feed_all, hidden_wide)
    far_own = after(across(normed_own), *hidden_near, *gate_grad_near, *up_grad_near, *back_near)
    normed_three += [far_own, to_core(far_own)]
    hidden_far, gate_grad_far, up_grad_far, back_far = feed(normed_three[2:], top[2:], feed_all, hidden_wide)
    far_ready = prepare(*back_far)
    far_sum = across(far_ready)
    top[3] = after(top[3], far_ready)
    hidden = hidden_near + hidden_far
    feed_grads = weight_grads(
        [
            list(zip(normed_three, gate_grad_near + gate_grad_far)),
            list(zip(normed_three, up_grad_near + up_grad_far)),
            list(zip(top, hidden)),
        ],
        hidden_wide,
    )
    far_sum = after(far_sum, feed_grads)
    feed_sums = lax.psum_scatter(feed_grads, "dp", scatter_dimension=0, tiled=True)
    stream_grad, grad_own, feed_gain_grad = join_back(
        [back_near[0], to_core(back_near[1]), far_sum], stream_two, out_grad, gain_feed
    )

    grad_two = [grad_own, to_core(grad_own)]
    query_grads, key_value_grads, backs = [], [], []
    for (weights, at), queries, keys_values, back in zip(cross_weights, queries_two, keys_values_two, backs_two):
        context_grad = multiply(grad_two, weights, at + wide, wide)
        *query_grad, key_value_grad = attend_backward(
            cross_ranges, still, queries, keys_values, context_grad, *back, None, heads, own_rows, block
        )
        query_grads.append(query_grad)
        key_value_grads.append(key_value_grad)
        backs.append(multiply(query_grad, weights, at, features, wider, True))
    stream_grad, grad_own, cross_gain_grad = join_back(
        [backs[0][0], backs[1][0], to_core(backs[0][1] + backs[1][1])], stream_one, stream_grad, gain_cross
    )

    grad_peer = to_core(grad_own)
    context_grad = multiply([grad_own, grad_peer], attend_all, 3 * wide, wide)
    cross_grads = [
        weight_grads([list(zip(normed_two, query_grad)), list(zip([grad_two[0], after(grad_two[1], grad_own)], context))])
        for query_grad, context in zip(query_grads, contexts_two)
    ]
    cross_far = across(jnp.concatenate([cross_grads[1], key_value_grads[1]], axis=0))
    layer_terms = multiply(hidden_far, feed_all, 2 * hidden_wide, features, wider, True, hidden_wide)
    layer_ready = prepare(*layer_terms)
    grad_far = after(across(grad_own), *context_grad, *cross_grads, layer_ready)
    grad_one = [grad_own, grad_peer, grad_far, to_core(grad_far)]
    context_grad = context_grad + multiply(grad_one[2:], attend_all, 3 * wide, wide)
    *qkv_grad, diagonals = attend_backward(
        self_ranges, me, qkv, None, context_grad, context_one_t, totals_one, bias, heads, block, block
    )
    self_grads = weight_grads([list(zip(normed_one, qkv_grad)), list(zip(grad_one, context_one))])
    self_parts = lax.psum_scatter(self_grads, "dp", scatter_dimension=0, tiled=True)
    qkv_grad[2] = after(qkv_grad[2], self_grads, feed_sums)
    terms = multiply(qkv_grad[2:], attend_all, 0, features, wider, True)
    far_ready = prepare(*terms)
    far_sum = across(far_ready)
    cross_far = after(cross_far, self_grads, feed_sums)
    key_value_grad = low(key_value_grads[0].astype(jnp.float32) + cross_far[features:].astype(jnp.float32))
    key_value_weights = weight_grads([[(encoder_all, key_value_grad)]])
    cross_parts = reduce_in_steps(
        *split(cross_grads[0], cross_far, key_value_weights, parts, dp_index), parts
    )
    qkv_grad[0] = after(qkv_grad[0], far_ready)
    terms = multiply(qkv_grad[:2], attend_all, 0, features, wider, True)
    tokens_grad, unused, attend_gain_grad = join_back(
        [terms[0], to_core(terms[1]), far_sum], tokens, stream_grad, gain_attend
    )

    diagonals = diagonal_sums(after(diagonals, far_ready))
    ahead = jnp.moveaxis(diagonals[:, :, :block], 0, 1).reshape(heads, reach)
    behind = jnp.moveaxis(diagonals[1:, :, block:], 0, 1).reshape(heads, reach - block)
    series_grad = ahead + jnp.pad(behind, ((0, 0), (0, block)))
    table_grad = lax.dot_general(onehot, series_grad, (((1,), (1,)), ((), ())), precision=lax.Precision.HIGHEST)
    table_full = lax.dynamic_update_slice(jnp.zeros(rel_table.shape, jnp.float32), table_grad, (0, me * heads))
    small = jnp.concatenate([attend_gain_grad, cross_gain_grad, feed_gain_grad, table_full.reshape(-1)])
    small = sum_everywhere(small.reshape(-1, 128), sizes).reshape(-1)
    encoder_terms = multiply(
        [after(swap_order(key_value_grad, me), far_ready)], attend_all, to_cross + 2 * wide, features, jnp.float32, True
    )[0]
    encoder_terms = [encoder_terms[at : at + encoder_rows] for at in range(0, PEERS * encoder_rows, encoder_rows)]
    encoder_ready = prepare(encoder_terms[2], encoder_terms[3])
    layer_far, encoder_far = across(after(layer_ready, far_sum)), across(after(encoder_ready, far_sum))
    small, layer_far, encoder_far = lax.optimization_barrier((small, layer_far, encoder_far))
    layer_terms = multiply([after(hidden_near[0], far_ready), hidden_near[1]], feed_all, 2 * hidden_wide, features, wider, True, hidden_wide)
    layer_out = low(stream_two + sum_core(*layer_terms) + layer_far.astype(jnp.float32))
    encoder_grad = sum_core(encoder_terms[0], encoder_terms[1]) + encoder_far.astype(jnp.float32)

    attend_gain_sum, cross_gain_sum, feed_gain_sum = (
        small[:features],
        small[features : 2 * features],
        small[2 * features : 3 * features],
    )
    table_sum = small[3 * features :].reshape(rel_table.shape)
    cross_sums = sum(part.astype(jnp.float32) for part in cross_parts)
    self_parts = after(self_parts, small, layer_out, encoder_grad, cross_sums)
    query_one_sum, key_one_sum, value_one_sum, output_one_sum = unpack(
        self_parts, [wide] * 4, [False, False, False, True]
    )
    query_two_sum, output_two_sum, key_two_sum, value_two_sum = columns_of(cross_sums, [wide] * 4)
    gate_sum, up_sum, down_sum = unpack(feed_sums, [hidden_wide] * 3, [False, False, True])
    return (
        layer_out,
        tokens_grad,
        encoder_grad,
        table_sum,
        attend_gain_sum,
        cross_gain_sum,
        feed_gain_sum,
        query_one_sum,
        key_one_sum,
        value_one_sum,
        output_one_sum,
        query_two_sum,
        key_two_sum,
        value_two_sum,
        output_two_sum.T,
        gate_sum,
        up_sum,
        down_sum,
    )


def solution(mesh):
    in_specs = (
        P(("dp", "mp"), None),
        P(("dp", "mp"), None),
        P("dp", "mp"),
        P("dp", "mp"),
        P(),
        P(),
        P(),
        P(),
        P(),
        P("dp", "mp"),
        P("dp", "mp"),
        P("dp", "mp"),
        P("mp", "dp"),
        P("dp", "mp"),
        P("dp", "mp"),
        P("dp", "mp"),
        P("mp", "dp"),
        P("dp", "mp"),
        P("dp", "mp"),
        P("mp", "dp"),
        P(("dp", "mp"), None),
    )
    out_specs = (
        P(("dp", "mp"), None),
        P(("dp", "mp"), None),
        P(("dp", "mp"), None),
        P(),
        P(),
        P(),
        P(),
        P("dp", "mp"),
        P("dp", "mp"),
        P("dp", "mp"),
        P("mp", "dp"),
        P("dp", "mp"),
        P("dp", "mp"),
        P("dp", "mp"),
        P("mp", "dp"),
        P("dp", "mp"),
        P("dp", "mp"),
        P("mp", "dp"),
    )
    return jax.shard_map(
        functools.partial(per_device, sizes=dict(mesh.shape)), mesh=mesh, in_specs=in_specs, out_specs=out_specs, check_vma=False
    )
```

```python
import functools
import jax
import jax.numpy as jnp
from jax import lax
from jax.experimental import pallas as pl
from jax.experimental.pallas import tpu as pltpu
from jax.sharding import PartitionSpec as P

DK = 64
PAIR = 2 * DK
NEG = -1e30
PEERS = 4

norm_eps = 1e-06
gelu_factor = 0.7978845608028654


def product(left, right):
    return jnp.dot(left, right, preferred_element_type=jnp.float32)


def rows_product(left, right):
    return lax.dot_general(left, right, (((0,), (0,)), ((), ())), preferred_element_type=jnp.float32)


def columns_product(left, right):
    return lax.dot_general(left, right, (((1,), (1,)), ((), ())), preferred_element_type=jnp.float32)


def norm_scale(rows):
    return lax.rsqrt(jnp.mean(rows * rows, axis=-1, keepdims=True) + norm_eps)


def gelu_parts(value):
    cubic = 0.044715 * value * value * value
    tangent = jnp.tanh(gelu_factor * (value + cubic))
    result = 0.5 * value * (1.0 + tangent)
    slope = 0.5 * (1.0 + tangent) + 0.5 * value * (1.0 - tangent * tangent) * gelu_factor * (
        1.0 + 3.0 * 0.044715 * value * value
    )
    return (result, slope)


def norm_back(grads, rows, scale, gain):
    scaled = grads * gain
    row_grad = scale * scaled - rows * (scale * scale * scale) * jnp.mean(scaled * rows, axis=-1, keepdims=True)
    gain_grad = jnp.sum(grads * rows * scale, axis=0)
    return (row_grad, gain_grad)


def low(value):
    return value.astype(jnp.bfloat16)


def nt_product(left, right):
    return lax.dot_general(left, right, (((1,), (1,)), ((), ())), preferred_element_type=jnp.float32)


def nn_product(left, right):
    return jnp.dot(left, right, preferred_element_type=jnp.float32)


def own_lanes(rows, head):
    lane = lax.broadcasted_iota(jnp.int32, rows.shape, 1)
    mine = (lane < DK) if head % 2 == 0 else (lane >= DK)
    return jnp.where(mine, rows, jnp.zeros_like(rows))


def bias_kernel(series_ref, tiles_ref, *, block):
    heads = series_ref.shape[0]
    for offset in range(tiles_ref.shape[0]):
        for head in range(heads):
            low = series_ref[pl.ds(head, 1), pl.ds(offset * block, block)]
            high = series_ref[pl.ds(head, 1), pl.ds((offset + 1) * block, block)]
            base = jnp.broadcast_to(jnp.concatenate([high, low], axis=1), (block, 2 * block))
            rolled = pltpu.roll(base, 0, 1, stride=1, stride_axis=0)
            tiles_ref[offset, head] = rolled[:, :block]


def bias_tiles(series, offsets, block):
    heads = series.shape[0]
    return pl.pallas_call(
        functools.partial(bias_kernel, block=block),
        out_shape=jax.ShapeDtypeStruct((offsets, heads, block, block), jnp.float32),
        compiler_params=pltpu.CompilerParams(vmem_limit_bytes=16 << 20),
        cost_estimate=lasting(4),
        name="bias_tiles",
    )(series)


def load_order(me, pieces, target_ref):
    size = pieces[0].shape[0]
    for order, piece in enumerate(pieces):
        at = pl.multiple_of((me ^ order) * size, size)
        target_ref[pl.ds(at, size), :] = piece[...]


def store_order(me, source_ref, pieces):
    size = pieces[0].shape[0]
    for order, piece in enumerate(pieces):
        at = pl.multiple_of((me ^ order) * size, size)
        piece[...] = source_ref[pl.ds(at, size), :].astype(jnp.bfloat16)


def forward_kernel(*refs, heads, block, tall, biased, at_key, at_value, pieces):
    low_ref, high_ref, me_ref, first_ref, last_ref, extra_ref = refs[:6]
    piece_refs = refs[6 : 6 + pieces]
    ctx_refs = refs[6 + pieces : 6 + 2 * pieces]
    ot_ref, lse_ref, acc_ref, vt_ref, q_ref, ctx_ref = refs[6 + 2 * pieces :]
    if biased:
        bias_ref, kv_ref = extra_ref, q_ref
    else:
        kv_ref = extra_ref
    load_order(me_ref[0], piece_refs, q_ref)
    rows = q_ref.shape[0]
    width = heads * DK
    key_iota = lax.broadcasted_iota(jnp.int32, (tall, block), 0)
    for tile in range(kv_ref.shape[0] // tall):
        vt_ref[:, pl.ds(tile * tall, tall)] = jnp.transpose(kv_ref[pl.ds(tile * tall, tall), pl.ds(at_value, width)])

    def one_block(index, _):
        start = pl.multiple_of(index * block, block)
        first = first_ref[:, pl.ds(start, block)]
        last = last_ref[:, pl.ds(start, block)]
        queries = [
            own_lanes(q_ref[pl.ds(start, block), pl.ds((head // 2) * PAIR, PAIR)], head) for head in range(heads)
        ]
        acc_ref[...] = jnp.zeros_like(acc_ref)

        def one_tile(tile, carry):
            at = pl.multiple_of(tile * tall, tall)
            valid = (key_iota >= first - at) & (key_iota < last - at)
            scores = []
            for head in range(heads):
                keys = kv_ref[pl.ds(at, tall), pl.ds(at_key + (head // 2) * PAIR, PAIR)]
                score = nt_product(keys, queries[head])
                if biased:
                    score = score + bias_ref[index - tile, head]
                scores.append(jnp.where(valid, score, NEG))
            results = []
            raised = []
            shrinks = []
            for head in range(heads):
                top, total = carry[head]
                new_top = jnp.maximum(top, jnp.max(scores[head], axis=0, keepdims=True))
                power = jnp.exp(scores[head] - new_top)
                shrink = jnp.exp(top - new_top)
                results.append((new_top, shrink * total + jnp.sum(power, axis=0, keepdims=True)))
                raised.append(power.astype(jnp.bfloat16))
                shrinks.append(shrink)
            for head in range(heads):
                mine = pl.ds(head * DK, DK)
                acc_ref[mine, :] = acc_ref[mine, :] * shrinks[head] + nn_product(
                    vt_ref[mine, pl.ds(at, tall)], raised[head]
                )
            return tuple(results)

        empty = tuple(
            (jnp.full((1, block), NEG, jnp.float32), jnp.zeros((1, block), jnp.float32)) for _ in range(heads)
        )
        stats = lax.fori_loop(low_ref[index], high_ref[index], one_tile, empty)
        for head in range(heads):
            top, total = stats[head]
            mine = pl.ds(head * DK, DK)
            acc_ref[mine, :] = acc_ref[mine, :] / total
            lse_ref[pl.ds(head, 1), pl.ds(start, block)] = top + jnp.log(total)
        ot_ref[:, pl.ds(start, block)] = acc_ref[...]
        ctx_ref[pl.ds(start, block), :] = jnp.transpose(acc_ref[...])
        return 0

    lax.fori_loop(0, rows // block, one_block, 0)
    store_order(me_ref[0], ctx_ref, ctx_refs)


def lasting(micros):
    return pl.CostEstimate(flops=int(micros * 1.1e9), bytes_accessed=1 << 10, transcendentals=0)


SMEM_SPEC = pl.BlockSpec(memory_space=pltpu.SMEM)
VMEM_SPEC = pl.BlockSpec(memory_space=pltpu.VMEM)


def attend_forward(ranges, me, queries, keys_values, bias, heads, block, tall):
    low_block, high_block, first, last = ranges
    pieces = len(queries)
    size, depth = queries[0].shape
    rows = pieces * size
    width = heads * DK
    biased = bias is not None
    at_key = width if biased else 0
    key_rows = rows if biased else keys_values.shape[0]
    operands = [low_block, high_block, me[None], first, last, bias if biased else keys_values, *queries]
    return pl.pallas_call(
        functools.partial(
            forward_kernel,
            heads=heads,
            block=block,
            tall=tall,
            biased=biased,
            at_key=at_key,
            at_value=at_key + width,
            pieces=pieces,
        ),
        out_shape=(
            *([jax.ShapeDtypeStruct((size, width), jnp.bfloat16)] * pieces),
            jax.ShapeDtypeStruct((width, rows), jnp.float32),
            jax.ShapeDtypeStruct((heads, rows), jnp.float32),
        ),
        in_specs=[SMEM_SPEC] * 3 + [VMEM_SPEC] * (len(operands) - 3),
        out_specs=(VMEM_SPEC,) * (pieces + 2),
        scratch_shapes=[
            pltpu.VMEM((width, block), jnp.float32),
            pltpu.VMEM((width, key_rows), jnp.bfloat16),
            pltpu.VMEM((rows, depth), jnp.bfloat16),
            pltpu.VMEM((rows, width), jnp.float32),
        ],
        compiler_params=pltpu.CompilerParams(vmem_limit_bytes=24 << 20),
        cost_estimate=lasting(14 if biased else 1),
        name="attend_forward",
    )(*operands)


def backward_kernel(*refs, heads, block, tall, biased, at_key, at_value, pieces):
    low_ref, high_ref, me_ref, ot_ref, lse_ref, first_ref, last_ref, extra_ref = refs[:8]
    piece_refs = refs[8 : 8 + pieces]
    g_refs = refs[8 + pieces : 8 + 2 * pieces]
    out_refs = refs[8 + 2 * pieces : 8 + 3 * pieces]
    refs = refs[8 + 3 * pieces :]
    if biased:
        diag_ref, dqt_ref, kt_ref, dka_ref, dva_ref, q_ref, g_ref, dq_ref = refs
        bias_ref = extra_ref
        kv_ref, dkv_ref = q_ref, dq_ref
    else:
        dkv_ref, dqt_ref, kt_ref, dka_ref, dva_ref, q_ref, g_ref, dq_ref = refs
        kv_ref = extra_ref
    load_order(me_ref[0], piece_refs, q_ref)
    load_order(me_ref[0], g_refs, g_ref)
    rows = q_ref.shape[0]
    width = heads * DK
    key_iota = lax.broadcasted_iota(jnp.int32, (tall, block), 0)
    for tile in range(kv_ref.shape[0] // tall):
        kt_ref[:, pl.ds(tile * tall, tall)] = jnp.transpose(kv_ref[pl.ds(tile * tall, tall), pl.ds(at_key, width)])
    dka_ref[...] = jnp.zeros_like(dka_ref)
    dva_ref[...] = jnp.zeros_like(dva_ref)
    if biased:
        diag_ref[...] = jnp.zeros_like(diag_ref)

    def one_block(index, _):
        start = pl.multiple_of(index * block, block)
        first = first_ref[:, pl.ds(start, block)]
        last = last_ref[:, pl.ds(start, block)]
        pairs = [pl.ds(pair * PAIR, PAIR) for pair in range(heads // 2)]
        queries = [own_lanes(q_ref[pl.ds(start, block), pairs[head // 2]], head) for head in range(heads)]
        grads = [own_lanes(g_ref[pl.ds(start, block), pairs[head // 2]], head) for head in range(heads)]
        shared = jnp.transpose(g_ref[pl.ds(start, block), :].astype(jnp.float32)) * ot_ref[:, pl.ds(start, block)]
        deltas = [jnp.sum(shared[head * DK : (head + 1) * DK], axis=0, keepdims=True) for head in range(heads)]
        totals = [lse_ref[pl.ds(head, 1), pl.ds(start, block)] for head in range(heads)]
        dqt_ref[...] = jnp.zeros_like(dqt_ref)

        def one_tile(tile, carry):
            at = pl.multiple_of(tile * tall, tall)
            valid = (key_iota >= first - at) & (key_iota < last - at)
            shares, score_grads = [], []
            for head in range(heads):
                pair = head // 2
                keys = kv_ref[pl.ds(at, tall), pl.ds(at_key + pair * PAIR, PAIR)]
                values = kv_ref[pl.ds(at, tall), pl.ds(at_value + pair * PAIR, PAIR)]
                scores = nt_product(keys, queries[head])
                share_grad = nt_product(values, grads[head])
                if biased:
                    scores = scores + bias_ref[index - tile, head]
                share = jnp.exp(jnp.where(valid, scores - totals[head], NEG))
                score_grad = (share * (share_grad - deltas[head])).astype(jnp.bfloat16)
                if biased:
                    diag_ref[index - tile, head] += score_grad.astype(jnp.float32)
                shares.append(share.astype(jnp.bfloat16))
                score_grads.append(score_grad)
            for pair in range(heads // 2):
                lanes = pl.ds(pair * PAIR, PAIR)
                one, two = 2 * pair, 2 * pair + 1
                dva_ref[pl.ds(at, tall), lanes] += nn_product(shares[one], grads[one]) + nn_product(shares[two], grads[two])
                dka_ref[pl.ds(at, tall), lanes] += nn_product(score_grads[one], queries[one]) + nn_product(
                    score_grads[two], queries[two]
                )
            for head in range(heads):
                mine = pl.ds(head * DK, DK)
                dqt_ref[mine, :] += nn_product(kt_ref[mine, pl.ds(at, tall)], score_grads[head])
            return carry

        lax.fori_loop(low_ref[index], high_ref[index], one_tile, 0)
        dq_ref[pl.ds(start, block), pl.ds(0, width)] = jnp.transpose(dqt_ref[...]).astype(jnp.bfloat16)
        return 0

    lax.fori_loop(0, rows // block, one_block, 0)
    dkv_ref[:, pl.ds(at_key, width)] = dka_ref[...].astype(jnp.bfloat16)
    dkv_ref[:, pl.ds(at_value, width)] = dva_ref[...].astype(jnp.bfloat16)
    store_order(me_ref[0], dq_ref, out_refs)


def diagonals_kernel(diag_ref, series_ref):
    offsets, heads, block, _ = diag_ref.shape

    def one_diagonal(index, _):
        offset, head = index >> (heads.bit_length() - 1), index & (heads - 1)
        slab = jnp.zeros((8, 2 * block), jnp.float32)
        for group in range(block // 8):
            piece = diag_ref[offset, head, pl.ds(8 * group, 8), :]
            wide = jnp.concatenate([piece, jnp.zeros_like(piece)], axis=1)
            slab = slab + (pltpu.roll(wide, 2 * block - 8 * group, 1) if group else wide)
        line = slab[0:1]
        for row in range(1, 8):
            line = line + pltpu.roll(slab[row : row + 1], 2 * block - row, 1)
        series_ref[offset, pl.ds(head, 1), :] = line
        return 0

    lax.fori_loop(0, offsets * heads, one_diagonal, 0)


def diagonal_sums(diagonals):
    offsets, heads, block, _ = diagonals.shape
    return pl.pallas_call(
        diagonals_kernel,
        out_shape=jax.ShapeDtypeStruct((offsets, heads, 2 * block), jnp.float32),
        in_specs=[VMEM_SPEC],
        out_specs=VMEM_SPEC,
        compiler_params=pltpu.CompilerParams(vmem_limit_bytes=8 << 20),
        cost_estimate=lasting(4),
        name="diagonal_sums",
    )(diagonals)


def attend_backward(ranges, me, queries, keys_values, grads, context_t, totals, bias, heads, block, tall):
    low_block, high_block, first, last = ranges
    pieces = len(queries)
    size, depth = queries[0].shape
    rows = pieces * size
    width = heads * DK
    biased = bias is not None
    at_key = width if biased else 0
    key_rows = rows if biased else keys_values.shape[0]
    operands = [low_block, high_block, me[None], context_t, totals, first, last, bias if biased else keys_values]
    operands += [*queries, *grads]
    shapes = [jax.ShapeDtypeStruct((size, depth), jnp.bfloat16)] * pieces
    scratch = [
        pltpu.VMEM((width, block), jnp.float32),
        pltpu.VMEM((width, key_rows), jnp.bfloat16),
        pltpu.VMEM((key_rows, width), jnp.float32),
        pltpu.VMEM((key_rows, width), jnp.float32),
        pltpu.VMEM((rows, depth), jnp.bfloat16),
        pltpu.VMEM((rows, width), jnp.bfloat16),
        pltpu.VMEM((rows, depth), jnp.bfloat16),
    ]
    if biased:
        shapes.append(jax.ShapeDtypeStruct(bias.shape, jnp.float32))
    else:
        shapes.append(jax.ShapeDtypeStruct((key_rows, 2 * width), jnp.bfloat16))
    return pl.pallas_call(
        functools.partial(
            backward_kernel,
            heads=heads,
            block=block,
            tall=tall,
            biased=biased,
            at_key=at_key,
            at_value=at_key + width,
            pieces=pieces,
        ),
        out_shape=tuple(shapes),
        in_specs=[SMEM_SPEC] * 3 + [VMEM_SPEC] * (len(operands) - 3),
        out_specs=(VMEM_SPEC,) * len(shapes),
        scratch_shapes=scratch,
        compiler_params=pltpu.CompilerParams(vmem_limit_bytes=36 << 20),
        cost_estimate=lasting(4),
        name="attend_backward",
    )(*operands)


def pack_kernel(*refs, turned):
    count = len(turned)
    out_ref, semaphores = refs[count], refs[-1]
    held = refs[count + 1 : -1]
    copies = [
        pltpu.make_async_copy(source, target, semaphores.at[order])
        for order, (source, target) in enumerate(zip(refs[:count], held))
    ]
    for copy in copies:
        copy.start()
    at = 0
    for copy, ref, turn in zip(copies, held, turned):
        copy.wait()
        piece = jnp.transpose(ref[...]) if turn else ref[...]
        out_ref[:, pl.ds(at, piece.shape[1])] = low(piece)
        at += piece.shape[1]


def pack(weights, turned):
    width = sum(weight.shape[0] if turn else weight.shape[1] for weight, turn in zip(weights, turned))
    rows = weights[0].shape[1] if turned[0] else weights[0].shape[0]
    return pl.pallas_call(
        functools.partial(pack_kernel, turned=tuple(turned)),
        out_shape=jax.ShapeDtypeStruct((rows, width), jnp.bfloat16),
        in_specs=[pl.BlockSpec(memory_space=pltpu.HBM)] * len(weights),
        out_specs=VMEM_SPEC,
        scratch_shapes=[pltpu.VMEM(weight.shape, jnp.float32) for weight in weights]
        + [pltpu.SemaphoreType.DMA((len(weights),))],
        compiler_params=pltpu.CompilerParams(vmem_limit_bytes=12 << 20),
        cost_estimate=lasting(2),
        name="pack",
    )(*[pltpu.with_memory_space_constraint(weight, pltpu.HBM) for weight in weights])


def unpack_kernel(rows_ref, *refs, turned):
    at = 0
    for ref, turn in zip(refs, turned):
        width = ref.shape[0] if turn else ref.shape[1]
        piece = rows_ref[:, pl.ds(at, width)].astype(jnp.float32)
        ref[...] = jnp.transpose(piece) if turn else piece
        at += width


def unpack(rows, widths, turned):
    shapes = [(width, rows.shape[0]) if turn else (rows.shape[0], width) for width, turn in zip(widths, turned)]
    return pl.pallas_call(
        functools.partial(unpack_kernel, turned=tuple(turned)),
        out_shape=[jax.ShapeDtypeStruct(shape, jnp.float32) for shape in shapes],
        in_specs=[VMEM_SPEC],
        out_specs=[VMEM_SPEC] * len(widths),
        compiler_params=pltpu.CompilerParams(vmem_limit_bytes=8 << 20),
        cost_estimate=lasting(9),
        name="unpack",
    )(rows)


def place_kernel(me_ref, *refs, first):
    out_ref = refs[-1]
    pieces = refs[:-1]
    size = out_ref.shape[0] // len(pieces)
    for order, piece in enumerate(pieces):
        at = pl.multiple_of((me_ref[0] ^ order) * size, size)
        out_ref[pl.ds(at, size), :] = piece[pl.ds(first, size), :]


def place(pieces, me, first=0, size=None):
    size = size or pieces[0].shape[0]
    width = pieces[0].shape[1]
    count = len(pieces)
    return pl.pallas_call(
        functools.partial(place_kernel, first=first),
        out_shape=jax.ShapeDtypeStruct((count * size, width), pieces[0].dtype),
        in_specs=[SMEM_SPEC] + [VMEM_SPEC] * count,
        out_specs=VMEM_SPEC,
        compiler_params=pltpu.CompilerParams(vmem_limit_bytes=8 << 20),
        cost_estimate=lasting(2),
        name="place",
    )(me[None], *pieces)


def swap_kernel(me_ref, rows_ref, out_ref, *, count):
    size = rows_ref.shape[0] // count
    for order in range(count):
        at = pl.multiple_of((me_ref[0] ^ order) * size, size)
        out_ref[pl.ds(order * size, size), :] = rows_ref[pl.ds(at, size), :]


def swap_order(rows, me, count=4):
    return pl.pallas_call(
        functools.partial(swap_kernel, count=count),
        out_shape=jax.ShapeDtypeStruct(rows.shape, rows.dtype),
        in_specs=[SMEM_SPEC, VMEM_SPEC],
        out_specs=VMEM_SPEC,
        compiler_params=pltpu.CompilerParams(vmem_limit_bytes=4 << 20),
        cost_estimate=lasting(1),
        name="swap_order",
    )(me[None], rows)


def multiply_kernel(*refs, at, depth, transposed):
    count = (len(refs) - 1) // 2
    weights_ref = refs[0]
    width = refs[-1].shape[1]
    chunk = min(256, width)

    def one_chunk(index, _):
        start = pl.multiple_of(index * chunk, chunk)
        if transposed:
            weights = weights_ref[pl.ds(start, chunk), pl.ds(at, depth)]
        else:
            weights = weights_ref[:, pl.ds(at + start, chunk)]
        for rows_ref, out_ref in zip(refs[1 : 1 + count], refs[1 + count :]):
            product_of = nt_product if transposed else nn_product
            out_ref[:, pl.ds(start, chunk)] = product_of(rows_ref[:, pl.ds(0, depth)], weights).astype(out_ref.dtype)
        return 0

    lax.fori_loop(0, width // chunk, one_chunk, 0)


def multiply(pieces, weights, at, width, kinds=jnp.bfloat16, transposed=False, depth=None):
    kinds = kinds if isinstance(kinds, (list, tuple)) else [kinds] * len(pieces)
    return pl.pallas_call(
        functools.partial(multiply_kernel, at=at, depth=depth or pieces[0].shape[1], transposed=transposed),
        out_shape=[jax.ShapeDtypeStruct((piece.shape[0], width), kind) for piece, kind in zip(pieces, kinds)],
        in_specs=[VMEM_SPEC] * (1 + len(pieces)),
        out_specs=[VMEM_SPEC] * len(pieces),
        compiler_params=pltpu.CompilerParams(vmem_limit_bytes=16 << 20),
        cost_estimate=lasting(2),
        name="multiply",
    )(weights, *pieces)


def weights_kernel(*refs, groups, chunk):
    out_ref = refs[-1]
    features = out_ref.shape[0]

    def one_chunk(index, _):
        at = pl.multiple_of(index * chunk, chunk)
        operand = 0
        column = 0
        for terms, width in groups:
            total = None
            for _ in range(terms):
                left_ref, right_ref = refs[operand], refs[operand + 1]
                operand += 2
                term = lax.dot_general(
                    left_ref[:, pl.ds(at, chunk)],
                    right_ref[:, pl.ds(0, width)],
                    (((0,), (0,)), ((), ())),
                    preferred_element_type=jnp.float32,
                )
                total = term if total is None else total + term
            out_ref[pl.ds(at, chunk), pl.ds(column, width)] = total.astype(jnp.bfloat16)
            column += width
        return 0

    lax.fori_loop(0, features // chunk, one_chunk, 0)


def weight_grads(groups, width=None):
    operands = [array for group in groups for pair in group for array in pair]
    features = operands[0].shape[1]
    shapes = tuple((len(group), width or group[0][1].shape[1]) for group in groups)
    return pl.pallas_call(
        functools.partial(weights_kernel, groups=shapes, chunk=256),
        out_shape=jax.ShapeDtypeStruct((features, sum(wide for _, wide in shapes)), jnp.bfloat16),
        in_specs=[VMEM_SPEC] * len(operands),
        out_specs=VMEM_SPEC,
        compiler_params=pltpu.CompilerParams(vmem_limit_bytes=32 << 20),
        cost_estimate=lasting(16 if width else 8),
        name="weight_grads",
    )(*operands)


def feed_kernel(*refs, hidden, padded):
    weights_ref = refs[0]
    rows_refs, top_refs = refs[1:3], refs[3:5]
    hidden_refs, gate_refs, up_refs, back_refs = refs[5:7], refs[7:9], refs[9:11], refs[11:13]
    gate_ref, wide_ref, down_ref = refs[13:]
    features = weights_ref.shape[0]
    for order, target in enumerate((gate_ref, wide_ref, down_ref)):
        target[:, pl.ds(0, hidden)] = weights_ref[:, pl.ds(order * hidden, hidden)]
        if padded > hidden:
            target[:, pl.ds(hidden, padded - hidden)] = jnp.zeros((features, padded - hidden), jnp.bfloat16)

    def one_chunk(index, _):
        lanes = pl.ds(pl.multiple_of(index * 256, 256), 256)
        for piece in range(2):
            gate = nn_product(rows_refs[piece][...], gate_ref[:, lanes])
            up = nn_product(rows_refs[piece][...], wide_ref[:, lanes])
            hidden_grad = nn_product(top_refs[piece][...], down_ref[:, lanes])
            gelu_value, gelu_slope = gelu_parts(gate)
            hidden_refs[piece][:, lanes] = low(gelu_value * up)
            gate_refs[piece][:, lanes] = low(hidden_grad * up * gelu_slope)
            up_refs[piece][:, lanes] = low(hidden_grad * gelu_value)
        return 0

    lax.fori_loop(0, padded // 256, one_chunk, 0)

    def one_back(index, _):
        part = pl.ds(pl.multiple_of(index * 256, 256), 256)
        for piece in range(2):
            back = nt_product(gate_refs[piece][...], gate_ref[part, :]) + nt_product(up_refs[piece][...], wide_ref[part, :])
            back_refs[piece][:, part] = back.astype(back_refs[piece].dtype)
        return 0

    lax.fori_loop(0, features // 256, one_back, 0)


def feed(rows, top, weights, hidden):
    size, features = rows[0].shape
    padded = (hidden + 255) // 256 * 256
    kept = [jax.ShapeDtypeStruct((size, padded), jnp.bfloat16)] * 6
    back = [jax.ShapeDtypeStruct((size, features), kind) for kind in (jnp.float32, jnp.bfloat16)]
    outs = pl.pallas_call(
        functools.partial(feed_kernel, hidden=hidden, padded=padded),
        out_shape=kept + back,
        in_specs=[VMEM_SPEC] * 5,
        out_specs=[VMEM_SPEC] * 8,
        scratch_shapes=[pltpu.VMEM((features, padded), jnp.bfloat16)] * 3,
        compiler_params=pltpu.CompilerParams(vmem_limit_bytes=32 << 20),
        cost_estimate=lasting(12),
        name="feed",
    )(weights, *rows, *top)
    return outs[0:2], outs[2:4], outs[4:6], outs[6:8]


ROW_TILE = 64


def join_kernel(*refs, terms):
    stream_ref, gain_ref = refs[terms : terms + 2]
    joined_ref, normed_ref = refs[terms + 2 :]

    def one_tile(index, _):
        tile = pl.ds(pl.multiple_of(index * ROW_TILE, ROW_TILE), ROW_TILE)
        rows = stream_ref[tile, :].astype(jnp.float32)
        for ref in refs[:terms]:
            rows = rows + ref[tile, :].astype(jnp.float32)
        joined_ref[tile, :] = rows
        normed_ref[tile, :] = low(rows * norm_scale(rows) * gain_ref[...])
        return 0

    lax.fori_loop(0, stream_ref.shape[0] // ROW_TILE, one_tile, 0)


def join(terms, stream, gain):
    return pl.pallas_call(
        functools.partial(join_kernel, terms=len(terms)),
        out_shape=[jax.ShapeDtypeStruct(stream.shape, kind) for kind in (jnp.float32, jnp.bfloat16)],
        in_specs=[VMEM_SPEC] * (len(terms) + 2),
        out_specs=[VMEM_SPEC] * 2,
        compiler_params=pltpu.CompilerParams(vmem_limit_bytes=12 << 20),
        cost_estimate=lasting(4),
        name="join",
    )(*terms, stream, gain[None])


def join_back_kernel(*refs, terms):
    stream_ref, upper_ref, gain_ref = refs[terms : terms + 3]
    total_ref, rounded_ref, gain_grad_ref = refs[terms + 3 :]
    gain_grad_ref[...] = jnp.zeros_like(gain_grad_ref)

    def one_tile(index, _):
        tile = pl.ds(pl.multiple_of(index * ROW_TILE, ROW_TILE), ROW_TILE)
        grads = refs[0][tile, :].astype(jnp.float32)
        for ref in refs[1:terms]:
            grads = grads + ref[tile, :].astype(jnp.float32)
        rows = stream_ref[tile, :].astype(jnp.float32)
        scale = norm_scale(rows)
        scaled = grads * gain_ref[...]
        row_grad = scale * scaled - rows * (scale * scale * scale) * jnp.mean(scaled * rows, axis=-1, keepdims=True)
        total = upper_ref[tile, :].astype(jnp.float32) + row_grad
        total_ref[tile, :] = total
        rounded_ref[tile, :] = low(total)
        gain_grad_ref[...] += jnp.sum(grads * rows * scale, axis=0, keepdims=True)
        return 0

    lax.fori_loop(0, stream_ref.shape[0] // ROW_TILE, one_tile, 0)


def join_back(terms, stream, upper, gain):
    total, rounded, gain_grad = pl.pallas_call(
        functools.partial(join_back_kernel, terms=len(terms)),
        out_shape=[
            jax.ShapeDtypeStruct(stream.shape, jnp.float32),
            jax.ShapeDtypeStruct(stream.shape, jnp.bfloat16),
            jax.ShapeDtypeStruct((1, stream.shape[1]), jnp.float32),
        ],
        in_specs=[VMEM_SPEC] * (len(terms) + 3),
        out_specs=[VMEM_SPEC] * 3,
        compiler_params=pltpu.CompilerParams(vmem_limit_bytes=16 << 20),
        cost_estimate=lasting(5),
        name="join_back",
    )(*terms, stream, upper, gain[None])
    return total, rounded, gain_grad[0]


def exchange(rows, axis, size, bits):
    return lax.ppermute(rows, axis, [(i, i ^ bits) for i in range(size)])


def to_core(rows):
    return exchange(rows, "mp", PEERS, 1)


def across(rows):
    return exchange(rows, "mp", PEERS, 2)


def after(value, *others):
    return lax.optimization_barrier((value, *others))[0]


def gather_four(rows):
    far = across(rows)
    return rows, to_core(rows), far, to_core(far)


def prepare(own, other):
    return low(own + to_core(low(other)).astype(jnp.float32))


def sum_core(own, other):
    return own + to_core(low(other)).astype(jnp.float32)


def split_kernel(me_ref, own_ref, far_ref, rest_ref, kept_ref, sent_ref, *, size):
    rows = own_ref.shape[0] // size
    wide = own_ref.shape[1]
    for order in range(size):
        at = pl.ds(pl.multiple_of((me_ref[0] ^ order) * rows, rows), rows)
        out_ref = sent_ref if order & 1 else kept_ref
        to = pl.ds((order >> 1) * rows, rows)
        out_ref[to, pl.ds(0, wide)] = low(own_ref[at, :].astype(jnp.float32) + far_ref[at, :].astype(jnp.float32))
        out_ref[to, pl.ds(wide, wide)] = rest_ref[at, :]


def split(own, far, rest, size, dp_index):
    half = jax.ShapeDtypeStruct((own.shape[0] // 2, 2 * own.shape[1]), jnp.bfloat16)
    return pl.pallas_call(
        functools.partial(split_kernel, size=size),
        out_shape=[half, half],
        in_specs=[SMEM_SPEC] + [VMEM_SPEC] * 3,
        out_specs=[VMEM_SPEC] * 2,
        compiler_params=pltpu.CompilerParams(vmem_limit_bytes=8 << 20),
        cost_estimate=lasting(2),
        name="split",
    )(dp_index[None], own, far, rest)


def reduce_in_steps(kept, sent, size):
    arrived = exchange(sent, "dp", size, 1)
    kept = low(kept.astype(jnp.float32) + arrived.astype(jnp.float32)).reshape(size // 2, -1, kept.shape[1])
    return [kept[0]] + [exchange(kept[order], "dp", size, 2 * order) for order in range(1, size // 2)]


def sum_everywhere(value, sizes):
    for axis in ("dp", "mp"):
        step = sizes[axis] // 2
        while step:
            value = value + exchange(value, axis, sizes[axis], step)
            step //= 2
    return value


def columns_of(array, widths):
    pieces = []
    at = 0
    for width in widths:
        pieces.append(array[:, at : at + width])
        at += width
    return pieces


def key_ranges(ids, key_ids, documents):
    numbers = jnp.arange(documents, dtype=jnp.int32)
    below = jnp.sum((key_ids[None, :] < numbers[:, None]).astype(jnp.int32), axis=1)
    upto = jnp.sum((key_ids[None, :] <= numbers[:, None]).astype(jnp.int32), axis=1)
    mine = (ids[None, :] == numbers[:, None]).astype(jnp.int32)
    return (jnp.sum(mine * below[:, None], axis=0), jnp.sum(mine * upto[:, None], axis=0))


def block_ranges(first, last, block, tall):
    return (first[::block] // tall, (last[block - 1 :: block] + tall - 1) // tall)


DOCUMENTS = 8
LONGEST = 768


def per_device(
    tokens,
    encoder_out,
    segments,
    encoder_segments,
    buckets,
    rel_table,
    gain_attend,
    gain_cross,
    gain_feed,
    self_query,
    self_key,
    self_value,
    self_output,
    cross_query,
    cross_key,
    cross_value,
    cross_output,
    w_gate,
    w_up,
    w_down,
    out_grad,
    *,
    sizes,
):
    parts = sizes["dp"]
    wide = self_query.shape[1]
    hidden_wide = w_gate.shape[1]
    heads = wide // DK
    block = 256
    own_rows = tokens.shape[0]
    me = lax.axis_index("mp")
    dp_index = lax.axis_index("dp")

    attend_shard = pack(
        [self_query, self_key, self_value, self_output, cross_query, cross_output, cross_key, cross_value],
        [False, False, False, True, False, True, False, False],
    )
    attend_all = lax.all_gather(attend_shard, "dp", axis=0, tiled=True)
    feed_shard = pack([w_gate.T, w_up.T, w_down], [True, True, True])
    feed_all = lax.all_gather(feed_shard, "dp", axis=0, tiled=True)
    to_cross = 4 * wide

    buckets_count = rel_table.shape[0]
    stream_zero = tokens.astype(jnp.float32)
    scale_zero = norm_scale(stream_zero)
    normed_zero = low(stream_zero * scale_zero * gain_attend)
    features = tokens.shape[1]
    encoder_rows = encoder_out.shape[0]
    ids = jnp.concatenate([segments, encoder_segments], axis=1)
    ids = jnp.pad(ids, ((0, 15), (0, features - ids.shape[1]))).astype(jnp.bfloat16)
    row_pieces = gather_four(jnp.concatenate([encoder_out, ids], axis=0))
    normed_one = list(gather_four(normed_zero))
    encoder_all = place(row_pieces, me, 0, encoder_rows)
    top = list(gather_four(after(out_grad, normed_one[2], row_pieces[2])))

    id_rows = jnp.concatenate([piece[encoder_rows:][:1] for piece in row_pieces], axis=0).astype(jnp.int32)
    near_ids = id_rows[:2, :own_rows].reshape(-1)
    ids = jnp.concatenate([lax.dynamic_slice_in_dim(id_rows, me ^ peer, 1, 0) for peer in range(PEERS)], axis=0)
    decoder_ids = ids[:, :own_rows].reshape(-1)
    encoder_ids = ids[:, own_rows : own_rows + encoder_rows].reshape(-1)
    length = decoder_ids.shape[0]
    self_first, unused = key_ranges(decoder_ids, decoder_ids, DOCUMENTS)
    self_last = jnp.arange(length, dtype=jnp.int32) + 1
    self_low, self_high = block_ranges(self_first, self_last, block, block)
    self_ranges = (self_low, self_high, self_first[None], self_last[None])
    cross_first, cross_last = key_ranges(near_ids, encoder_ids, DOCUMENTS)
    cross_low, cross_high = block_ranges(cross_first, cross_last, own_rows, block)
    cross_ranges = (cross_low, cross_high, cross_first[None], cross_last[None])

    offsets = min((LONGEST + block - 2) // block + 1, length // block)
    reach = offsets * block
    table_local = lax.dynamic_slice_in_dim(rel_table, me * heads, heads, 1)
    onehot = (buckets[None, :reach] == jnp.arange(buckets_count, dtype=jnp.int32)[:, None]).astype(jnp.float32)
    series = lax.dot_general(table_local, onehot, (((0,), (0,)), ((), ())), precision=lax.Precision.HIGHEST)
    bias = bias_tiles(jnp.pad(series, ((0, 0), (block, 0))), offsets, block)

    wider = [jnp.float32, jnp.bfloat16]
    qkv = multiply(normed_one, after(attend_all, top[2], top[3], feed_shard), 0, 3 * wide)
    *context_one, context_one_t, totals_one = attend_forward(self_ranges, me, qkv, None, bias, heads, block, block)
    cross_other = across(attend_all[:, to_cross : to_cross + 2 * wide])
    context_one[2] = after(context_one[2], cross_other)
    terms = multiply(context_one[2:], attend_all, 3 * wide, features, wider, True)
    far_ready = prepare(*terms)
    far_sum = across(far_ready)
    keys_values = multiply([encoder_all], attend_all, to_cross + 2 * wide, 2 * wide)[0]
    keys_values_two = [keys_values, across(keys_values)]
    terms = multiply([after(context_one[0], far_ready), context_one[1]], attend_all, 3 * wide, features, wider, True)
    far_sum = after(far_sum, terms[0], keys_values_two[1])
    stream_one, normed_own = join([terms[0], to_core(terms[1]), far_sum], tokens, gain_cross)

    cross_weights = [(attend_all, to_cross), (cross_other, 0)]
    normed_two = [normed_own, to_core(normed_own)]
    still = jnp.zeros_like(me)
    queries_two, contexts_two, backs_two = [], [], []
    for (weights, at), keys_values in zip(cross_weights, keys_values_two):
        queries_two.append(multiply(normed_two, weights, at, wide))
        *context, context_t, totals = attend_forward(
            cross_ranges, still, queries_two[-1], keys_values, None, heads, own_rows, block
        )
        contexts_two.append(context)
        backs_two.append((context_t, totals))
    terms = [
        multiply(context, weights, at + wide, features, wider, True)
        for context, (weights, at) in zip(contexts_two, cross_weights)
    ]
    stream_two, normed_own = join(
        [terms[0][0], terms[1][0], to_core(terms[0][1] + terms[1][1])], stream_one, gain_feed
    )

    normed_three = [normed_own, to_core(normed_own)]
    hidden_near, gate_grad_near, up_grad_near, back_near = feed(normed_three, top[:2], feed_all, hidden_wide)
    far_own = after(across(normed_own), *hidden_near, *gate_grad_near, *up_grad_near, *back_near)
    normed_three += [far_own, to_core(far_own)]
    hidden_far, gate_grad_far, up_grad_far, back_far = feed(normed_three[2:], top[2:], feed_all, hidden_wide)
    far_ready = prepare(*back_far)
    far_sum = across(far_ready)
    top[3] = after(top[3], far_ready)
    hidden = hidden_near + hidden_far
    feed_grads = weight_grads(
        [
            list(zip(normed_three, gate_grad_near + gate_grad_far)),
            list(zip(normed_three, up_grad_near + up_grad_far)),
            list(zip(top, hidden)),
        ],
        hidden_wide,
    )
    far_sum = after(far_sum, feed_grads)
    feed_sums = lax.psum_scatter(feed_grads, "dp", scatter_dimension=0, tiled=True)
    stream_grad, grad_own, feed_gain_grad = join_back(
        [back_near[0], to_core(back_near[1]), far_sum], stream_two, out_grad, gain_feed
    )

    grad_two = [grad_own, to_core(grad_own)]
    query_grads, key_value_grads, backs = [], [], []
    for (weights, at), queries, keys_values, back in zip(cross_weights, queries_two, keys_values_two, backs_two):
        context_grad = multiply(grad_two, weights, at + wide, wide)
        *query_grad, key_value_grad = attend_backward(
            cross_ranges, still, queries, keys_values, context_grad, *back, None, heads, own_rows, block
        )
        query_grads.append(query_grad)
        key_value_grads.append(key_value_grad)
        backs.append(multiply(query_grad, weights, at, features, wider, True))
    stream_grad, grad_own, cross_gain_grad = join_back(
        [backs[0][0], backs[1][0], to_core(backs[0][1] + backs[1][1])], stream_one, stream_grad, gain_cross
    )

    grad_peer = to_core(grad_own)
    context_grad = multiply([grad_own, grad_peer], attend_all, 3 * wide, wide)
    cross_grads = [
        weight_grads([list(zip(normed_two, query_grad)), list(zip([grad_two[0], after(grad_two[1], grad_own)], context))])
        for query_grad, context in zip(query_grads, contexts_two)
    ]
    cross_far = across(jnp.concatenate([cross_grads[1], key_value_grads[1]], axis=0))
    layer_terms = multiply(hidden_far, feed_all, 2 * hidden_wide, features, wider, True, hidden_wide)
    layer_ready = prepare(*layer_terms)
    grad_far = after(across(grad_own), *context_grad, *cross_grads, layer_ready)
    grad_one = [grad_own, grad_peer, grad_far, to_core(grad_far)]
    context_grad = context_grad + multiply(grad_one[2:], attend_all, 3 * wide, wide)
    *qkv_grad, diagonals = attend_backward(
        self_ranges, me, qkv, None, context_grad, context_one_t, totals_one, bias, heads, block, block
    )
    self_grads = weight_grads([list(zip(normed_one, qkv_grad)), list(zip(grad_one, context_one))])
    self_parts = lax.psum_scatter(self_grads, "dp", scatter_dimension=0, tiled=True)
    qkv_grad[2] = after(qkv_grad[2], self_grads, feed_sums)
    terms = multiply(qkv_grad[2:], attend_all, 0, features, wider, True)
    far_ready = prepare(*terms)
    far_sum = across(far_ready)
    cross_far = after(cross_far, self_grads, feed_sums)
    key_value_grad = low(key_value_grads[0].astype(jnp.float32) + cross_far[features:].astype(jnp.float32))
    key_value_weights = weight_grads([[(encoder_all, key_value_grad)]])
    cross_parts = reduce_in_steps(
        *split(cross_grads[0], cross_far, key_value_weights, parts, dp_index), parts
    )
    qkv_grad[0] = after(qkv_grad[0], far_ready)
    terms = multiply(qkv_grad[:2], attend_all, 0, features, wider, True)
    tokens_grad, unused, attend_gain_grad = join_back(
        [terms[0], to_core(terms[1]), far_sum], tokens, stream_grad, gain_attend
    )

    diagonals = diagonal_sums(after(diagonals, far_ready))
    ahead = jnp.moveaxis(diagonals[:, :, :block], 0, 1).reshape(heads, reach)
    behind = jnp.moveaxis(diagonals[1:, :, block:], 0, 1).reshape(heads, reach - block)
    series_grad = ahead + jnp.pad(behind, ((0, 0), (0, block)))
    table_grad = lax.dot_general(onehot, series_grad, (((1,), (1,)), ((), ())), precision=lax.Precision.HIGHEST)
    table_full = lax.dynamic_update_slice(jnp.zeros(rel_table.shape, jnp.float32), table_grad, (0, me * heads))
    small = jnp.concatenate([attend_gain_grad, cross_gain_grad, feed_gain_grad, table_full.reshape(-1)])
    small = sum_everywhere(small.reshape(-1, 128), sizes).reshape(-1)
    encoder_terms = multiply(
        [after(swap_order(key_value_grad, me), far_ready)], attend_all, to_cross + 2 * wide, features, jnp.float32, True
    )[0]
    encoder_terms = [encoder_terms[at : at + encoder_rows] for at in range(0, PEERS * encoder_rows, encoder_rows)]
    encoder_ready = prepare(encoder_terms[2], encoder_terms[3])
    layer_far, encoder_far = across(after(layer_ready, far_sum)), across(after(encoder_ready, far_sum))
    small, layer_far, encoder_far = lax.optimization_barrier((small, layer_far, encoder_far))
    layer_terms = multiply([after(hidden_near[0], far_ready), hidden_near[1]], feed_all, 2 * hidden_wide, features, wider, True, hidden_wide)
    layer_out = low(stream_two + sum_core(*layer_terms) + layer_far.astype(jnp.float32))
    encoder_grad = sum_core(encoder_terms[0], encoder_terms[1]) + encoder_far.astype(jnp.float32)

    attend_gain_sum, cross_gain_sum, feed_gain_sum = (
        small[:features],
        small[features : 2 * features],
        small[2 * features : 3 * features],
    )
    table_sum = small[3 * features :].reshape(rel_table.shape)
    cross_sums = sum(part.astype(jnp.float32) for part in cross_parts)
    self_parts = after(self_parts, small, layer_out, encoder_grad, cross_sums)
    query_one_sum, key_one_sum, value_one_sum, output_one_sum = unpack(
        self_parts, [wide] * 4, [False, False, False, True]
    )
    query_two_sum, output_two_sum, key_two_sum, value_two_sum = columns_of(cross_sums, [wide] * 4)
    gate_sum, up_sum, down_sum = unpack(feed_sums, [hidden_wide] * 3, [True, True, True])
    return (
        layer_out,
        tokens_grad,
        encoder_grad,
        table_sum,
        attend_gain_sum,
        cross_gain_sum,
        feed_gain_sum,
        query_one_sum,
        key_one_sum,
        value_one_sum,
        output_one_sum,
        query_two_sum,
        key_two_sum,
        value_two_sum,
        output_two_sum.T,
        gate_sum.T,
        up_sum.T,
        down_sum,
    )


def solution(mesh):
    in_specs = (
        P(("dp", "mp"), None),
        P(("dp", "mp"), None),
        P("dp", "mp"),
        P("dp", "mp"),
        P(),
        P(),
        P(),
        P(),
        P(),
        P("dp", "mp"),
        P("dp", "mp"),
        P("dp", "mp"),
        P("mp", "dp"),
        P("dp", "mp"),
        P("dp", "mp"),
        P("dp", "mp"),
        P("mp", "dp"),
        P("dp", "mp"),
        P("dp", "mp"),
        P("mp", "dp"),
        P(("dp", "mp"), None),
    )
    out_specs = (
        P(("dp", "mp"), None),
        P(("dp", "mp"), None),
        P(("dp", "mp"), None),
        P(),
        P(),
        P(),
        P(),
        P("dp", "mp"),
        P("dp", "mp"),
        P("dp", "mp"),
        P("mp", "dp"),
        P("dp", "mp"),
        P("dp", "mp"),
        P("dp", "mp"),
        P("mp", "dp"),
        P("dp", "mp"),
        P("dp", "mp"),
        P("mp", "dp"),
    )
    return jax.shard_map(
        functools.partial(per_device, sizes=dict(mesh.shape)), mesh=mesh, in_specs=in_specs, out_specs=out_specs, check_vma=False
    )
```
